32 devices in a mesh: dp: 8 (over z, x), space: 4 (over y, core).
Axes of the slice: x: 2, y: 2, z: 4, core: 2. Of those that a mesh axis runs over, the one named last changes fastest.
Arguments:
- images: bfloat16 [256, 24, 24, 384], P('dp', 'space'), may hold values from -6 to 6
- cotangent: bfloat16 [256, 24, 24, 384], P('dp', 'space'), may hold values from -6 to 6
- image_sides: int32 [256], P('dp'), may hold values from 14 to 24, as said below
- keep_flags: int32 [256], P('dp'), may hold values 0 or 1
- depth_kernel: float32 [49, 384], P(None, ('dp', 'space')), may hold values from -0.875 to 0.875
- kernel_moment: float32 [49, 384], P(None, ('dp', 'space')), may hold values from -0.00061035156 to 0.00061035156
- kernel_square: float32 [49, 384], P(None, ('dp', 'space')), may hold values from 4.1600107e-10 to 6.656017e-09
- block_vectors: float32 [5, 384], P(None, ('dp', 'space')), may hold values from -1.5 to 1.5
- vector_moment: float32 [5, 384], P(None, ('dp', 'space')), may hold values from -0.00061035156 to 0.00061035156
- vector_square: float32 [5, 384], P(None, ('dp', 'space')), may hold values from 4.1600107e-10 to 6.656017e-09
- up_weight: float32 [384, 1536], P(None, ('dp', 'space')), may hold values from -0.3125 to 0.3125
- up_moment: float32 [384, 1536], P(None, ('dp', 'space')), may hold values from -0.00061035156 to 0.00061035156
- up_square: float32 [384, 1536], P(None, ('dp', 'space')), may hold values from 4.1600107e-10 to 6.656017e-09
- up_bias: float32 [1536], P(('dp', 'space')), may hold values from -3 to 3
- bias_moment: float32 [1536], P(('dp', 'space')), may hold values from -0.00061035156 to 0.00061035156
- bias_square: float32 [1536], P(('dp', 'space')), may hold values from 4.1600107e-10 to 6.656017e-09
- down_weight: float32 [1536, 384], P(('dp', 'space')), may hold values from -0.15625 to 0.15625
- down_moment: float32 [1536, 384], P(('dp', 'space')), may hold values from -0.00061035156 to 0.00061035156
- down_square: float32 [1536, 384], P(('dp', 'space')), may hold values from 4.1600107e-10 to 6.656017e-09
Outputs:
- out_images: bfloat16 [256, 24, 24, 384], P('dp', 'space')
- grad_images: bfloat16 [256, 24, 24, 384], P('dp', 'space')
- new_kernel: float32 [49, 384], P(None, ('dp', 'space'))
- new_kernel_moment: float32 [49, 384], P(None, ('dp', 'space'))
- new_kernel_square: float32 [49, 384], P(None, ('dp', 'space'))
- new_vectors: float32 [5, 384], P(None, ('dp', 'space'))
- new_vector_moment: float32 [5, 384], P(None, ('dp', 'space'))
- new_vector_square: float32 [5, 384], P(None, ('dp', 'space'))
- new_up: float32 [384, 1536], P(None, ('dp', 'space'))
- new_up_moment: float32 [384, 1536], P(None, ('dp', 'space'))
- new_up_square: float32 [384, 1536], P(None, ('dp', 'space'))
- new_bias: float32 [1536], P(('dp', 'space'))
- new_bias_moment: float32 [1536], P(('dp', 'space'))
- new_bias_square: float32 [1536], P(('dp', 'space'))
- new_down: float32 [1536, 384], P(('dp', 'space'))
- new_down_moment: float32 [1536, 384], P(('dp', 'space'))
- new_down_square: float32 [1536, 384], P(('dp', 'space'))
- grad_norm: float32 [], replicated
The draws below stay inside these ranges and needn't reach their ends.
Inputs may be any that keep to these rules, and one draw needn't show every extreme that they name: `image_sides`: each image's valid square has one of the sides 24, 18, 14.
All inputs are finite; a program needn't handle non-finite values. No bound on the sum of `keep_flags` on one device may be relied on, other than what follows from the above.
Results may differ from the reference program's by a relative error of at most 0.0055.
Values may be sent and summed in bfloat16 or wider, within the bound.
No kernel may reach another device: no remote copies, remote signals or barrier semaphores. Data moves between devices by JAX's collectives and lax.ppermute only.
A program may use at most 192 MiB of HBM per device.

```python
import math
import jax
import jax.numpy as jnp
from jax import lax

C = 384
HID = 1536
S = 24
STEP = 5
IMAGES = 256
PARAMS = 1201920


def draw_image_sides(key, part):
    picks = jax.random.randint(key, (IMAGES,), 0, 3)
    values = jnp.where(picks == 0, S, jnp.where(picks == 1, S * 3 // 4, S * 7 // 12)).astype(jnp.int32)
    values = values.at[0].set(S).at[1].set(S * 7 // 12)
    return values


def draw_block_vectors(key, part):
    key_gain = jax.random.fold_in(key, 11)
    key_shift = jax.random.fold_in(key, 23)
    gain_part = jax.random.uniform(key_gain, (5, C), jnp.float32, 0.5, 1.5)
    shift_part = jnp.clip(0.5 * jax.random.normal(key_shift, (5, C), jnp.float32), -1.5, 1.5)
    row_ids = jnp.arange(5)[:, None]
    is_gain = (row_ids == 1) | (row_ids == 4)
    return jnp.where(is_gain, gain_part, shift_part)


def plant(result, stream_key, low, largest):
    shape = result.shape
    spot = [jax.random.randint(jax.random.fold_in(stream_key, axis), (), 0, shape[axis]) for axis in range(len(shape))]
    result = result.at[tuple(spot)].set(low)
    longest = shape.index(max(shape))
    spot[longest] = (spot[longest] + 1) % shape[longest]
    return result.at[tuple(spot)].set(largest)


def block_levels(own_key, dims, shards, least, high):
    level = 1.0
    for position, shards_of in shards:
        steps = jax.random.uniform(jax.random.fold_in(jax.random.fold_in(own_key, 6), position), (shards_of,), jnp.float32, least / len(shards), high / len(shards))
        level = level * jnp.repeat(jnp.exp(steps), dims[position] // shards_of).reshape((-1,) + (1,) * (len(dims) - 1 - position))
    return level


def normal_values(rng, dims, scale, most, cuts=(), kind=jnp.bfloat16):
    drawn = jax.random.normal(rng, dims, jnp.float32) * scale
    if len(cuts) > 0:
        drawn = block_levels(rng, dims, cuts, -0.22, 0.18) * drawn
    return jnp.clip(drawn, min=-most, max=most).astype(kind)


def setup_inputs(seed: int = 0) -> dict:
    streams_of = jax.random.split(jax.random.key(seed), 20)
    return {
        "images": normal_values(streams_of[0], (IMAGES, S, S, C), 1.0, 6.0, ((0, 8), (1, 4))),
        "cotangent": normal_values(streams_of[1], (IMAGES, S, S, C), 1.0, 6.0, ((0, 8), (1, 4))),
        "image_sides": draw_image_sides(jax.random.fold_in(streams_of[19], 71), 0),
        "keep_flags": plant((jax.random.randint(streams_of[3], (IMAGES,), 0, 4) < 3).astype(jnp.int32), jax.random.fold_in(streams_of[3], 1), 0, 1),
        "depth_kernel": normal_values(streams_of[4], (49, C), 49 ** -0.5, 0.875, ((1, 32),), jnp.float32),
        "kernel_moment": normal_values(streams_of[5], (49, C), (0.111 * PARAMS ** -0.5), 0.00061035156, ((1, 32),), jnp.float32),
        "kernel_square": jnp.clip(jnp.exp(math.log(6.656017070838516e-09) - 2.7725887 * jax.random.uniform(streams_of[6], (49, C), jnp.float32) ** block_levels(streams_of[6], (49, C), ((1, 32),), -0.2, 0.2)), 4.1600106692740724e-10, 6.656017070838516e-09),
        "block_vectors": draw_block_vectors(jax.random.fold_in(streams_of[19], 71), 0),
        "vector_moment": normal_values(streams_of[8], (5, C), (0.111 * PARAMS ** -0.5), 0.00061035156, ((1, 32),), jnp.float32),
        "vector_square": jnp.clip(jnp.exp(math.log(6.656017070838516e-09) - 2.7725887 * jax.random.uniform(streams_of[9], (5, C), jnp.float32) ** block_levels(streams_of[9], (5, C), ((1, 32),), -0.2, 0.2)), 4.1600106692740724e-10, 6.656017070838516e-09),
        "up_weight": normal_values(streams_of[10], (C, HID), C ** -0.5, 0.3125, ((1, 32),), jnp.float32),
        "up_moment": normal_values(streams_of[11], (C, HID), (0.111 * PARAMS ** -0.5), 0.00061035156, ((1, 32),), jnp.float32),
        "up_square": jnp.clip(jnp.exp(math.log(6.656017070838516e-09) - 2.7725887 * jax.random.uniform(streams_of[12], (C, HID), jnp.float32) ** block_levels(streams_of[12], (C, HID), ((1, 32),), -0.2, 0.2)), 4.1600106692740724e-10, 6.656017070838516e-09),
        "up_bias": normal_values(streams_of[13], (HID,), 0.5, 3.0, ((0, 32),), jnp.float32),
        "bias_moment": normal_values(streams_of[14], (HID,), (0.111 * PARAMS ** -0.5), 0.00061035156, ((0, 32),), jnp.float32),
        "bias_square": jnp.clip(jnp.exp(math.log(6.656017070838516e-09) - 2.7725887 * jax.random.uniform(streams_of[15], (HID,), jnp.float32) ** block_levels(streams_of[15], (HID,), ((0, 32),), -0.2, 0.2)), 4.1600106692740724e-10, 6.656017070838516e-09),
        "down_weight": normal_values(streams_of[16], (HID, C), HID ** -0.5, 0.15625, ((0, 32),), jnp.float32),
        "down_moment": normal_values(streams_of[17], (HID, C), (0.111 * PARAMS ** -0.5), 0.00061035156, ((0, 32),), jnp.float32),
        "down_square": jnp.clip(jnp.exp(math.log(6.656017070838516e-09) - 2.7725887 * jax.random.uniform(streams_of[18], (HID, C), jnp.float32) ** block_levels(streams_of[18], (HID, C), ((0, 32),), -0.2, 0.2)), 4.1600106692740724e-10, 6.656017070838516e-09),
    }


@jax.custom_vjp
def low(v):
    return lax.optimization_barrier(v.astype(jnp.bfloat16)).astype(jnp.float32)

@jax.custom_vjp
def low_back(v):
    return v

def low_keep(v):
    return (low(v), None)

def low_pass(kept, grad):
    return (grad,)

def back_keep(v):
    return (v, None)

def back_low(kept, grad):
    return (low(grad),)
low.defvjp(low_keep, low_pass)
low_back.defvjp(back_keep, back_low)
keep_scale = 4.0 / 3.0
norm_eps = 1e-06
clip_limit = 1.0
beta_one = 0.9
beta_two = 0.999
adam_eps = 1e-08
decay_rate = 0.05
step_rates = (0.15, 0.5, 0.05, 0.2, 0.025)
highest = lax.Precision.HIGHEST

def depthwise(padded, kernel, out_rows, out_cols):
    running = jnp.zeros((padded.shape[0], out_rows, out_cols, padded.shape[3]), jnp.float32)
    for row_off in range(7):
        for col_off in range(7):
            running = running + kernel[row_off * 7 + col_off] * padded[:, row_off:row_off + out_rows, col_off:col_off + out_cols, :]
    return running

def block_forward(image_block, depth_kernel, block_vectors, up_weight, up_bias, down_weight, mask_block, scale_block):
    masked = image_block * mask_block[..., None]
    padded = jnp.pad(masked, ((0, 0), (3, 3), (3, 3), (0, 0)))
    conv = depthwise(padded, depth_kernel, S, S) + block_vectors[0]
    chan_mean = lax.optimization_barrier(jnp.mean(conv, axis=-1, keepdims=True))
    centred = conv - chan_mean
    chan_var = lax.optimization_barrier(jnp.mean(centred * centred, axis=-1, keepdims=True))
    normed = low(centred * lax.rsqrt(chan_var + norm_eps) * block_vectors[1] + block_vectors[2])
    hidden = low_back(jnp.einsum('nijc,ch->nijh', normed, low(up_weight), precision=highest) + up_bias)
    active = low(jax.nn.gelu(hidden, approximate=False))
    branch = low_back(jnp.einsum('nijh,hc->nijc', active, low(down_weight), precision=highest) + block_vectors[3])
    return image_block + scale_block[..., None] * block_vectors[4] * branch

def reference(images, cotangent, image_sides, keep_flags, depth_kernel, kernel_moment, kernel_square, block_vectors, vector_moment, vector_square, up_weight, up_moment, up_square, up_bias, bias_moment, bias_square, down_weight, down_moment, down_square):
    row_ids = jnp.arange(S, dtype=jnp.int32)
    inside = row_ids[None, :] < image_sides[:, None]
    pixel_mask = (inside[:, :, None] & inside[:, None, :]).astype(jnp.float32)
    branch_scale = pixel_mask * (keep_flags.astype(jnp.float32) * keep_scale)[:, None, None]
    blocks = images.shape[0] // 4
    params = (depth_kernel, block_vectors, up_weight, up_bias, down_weight)

    def regroup(value):
        return value.reshape((blocks, 4) + value.shape[1:])

    def scan_step(totals, item):
        image_block, cot_block, mask_block, scale_block = item

        def forward_fn(x_value, *weights):
            return block_forward(x_value, *weights, mask_block, scale_block)
        out_block, pullback = jax.vjp(forward_fn, image_block.astype(jnp.float32), *params)
        grads = pullback(cot_block.astype(jnp.float32))
        new_totals = tuple((total_part + grad_part for total_part, grad_part in zip(totals, grads[1:])))
        return (new_totals, (out_block.astype(jnp.bfloat16), grads[0].astype(jnp.bfloat16)))
    zero_grads = tuple((jnp.zeros(p.shape, jnp.float32) for p in params))
    totals, (out_blocks, grad_blocks) = lax.scan(scan_step, zero_grads, (regroup(images), regroup(cotangent), regroup(pixel_mask), regroup(branch_scale)))
    grad_norm = jnp.sqrt(sum((jnp.sum(g * g) for g in totals)))
    factor = clip_limit / jnp.maximum(grad_norm, clip_limit)
    states = ((depth_kernel, kernel_moment, kernel_square), (block_vectors, vector_moment, vector_square), (up_weight, up_moment, up_square), (up_bias, bias_moment, bias_square), (down_weight, down_moment, down_square))
    results = []
    for (weight, moment, square), grad_part, step_rate in zip(states, totals, step_rates):
        scaled = grad_part * factor
        new_moment = beta_one * moment + (1.0 - beta_one) * scaled
        new_square = beta_two * square + (1.0 - beta_two) * scaled * scaled
        corrected = new_moment / (1.0 - beta_one ** STEP)
        spread = jnp.sqrt(new_square / (1.0 - beta_two ** STEP))
        new_weight = weight - step_rate * (corrected / (spread + adam_eps) + decay_rate * weight)
        results.extend([new_weight, new_moment, new_square])
    return (out_blocks.reshape(images.shape), grad_blocks.reshape(images.shape), results[0], results[1], results[2], results[3], results[4], results[5], results[6], results[7], results[8], results[9], results[10], results[11], results[12], results[13], results[14], grad_norm)
```

```python
import functools

import jax
import jax.numpy as jnp
from jax import lax
from jax.experimental import pallas as pl
from jax.experimental.pallas import tpu as pltpu
from jax.sharding import PartitionSpec as P

STEP = 5

keep_scale = 4.0 / 3.0
norm_eps = 1e-06
clip_limit = 1.0
beta_one = 0.9
beta_two = 0.999
adam_eps = 1e-08
decay_rate = 0.05
step_rates = (0.15, 0.5, 0.05, 0.2, 0.025)
inv_root_two = 0.7071067811865476
inv_root_tau = 0.3989422804014327
f32 = jnp.float32
bf16 = jnp.bfloat16
AXES = ("dp", "space")
LANES = 128
REACH = 3
TAPS = 7
EDGE = 8
MLP_ROWS = 512
MLP_COLS = 256
MIB = 1 << 20


def clear_edges(pad_ref, cols):
    tiles, rows, width, lanes = pad_ref.shape
    for tile in range(tiles):
        for row in range(rows):
            pad_ref[tile, row, 0:EDGE, :] = jnp.zeros((EDGE, lanes), f32)
            pad_ref[tile, row, EDGE + cols : width, :] = jnp.zeros((width - EDGE - cols, lanes), f32)


def fill_rows(pad_ref, first, block, limit=None, row_start=None):
    rows, cols, channels = block.shape
    for row in range(rows):
        line = block[row].astype(f32)
        if limit is not None:
            reach = jnp.where(row_start + row < limit, limit, 0)
            inside = lax.broadcasted_iota(jnp.int32, (cols, channels), 0) < reach
            line = jnp.where(inside, line, 0.0)
        for tile in range(channels // LANES):
            pad_ref[tile, first + row, EDGE : EDGE + cols, :] = line[:, tile * LANES : (tile + 1) * LANES]


def conv_tile(pad_ref, tile, taps_ref, out_rows, cols, flip):
    lanes = slice(tile * LANES, (tile + 1) * LANES)
    sums = [None] * out_rows
    for col_off in range(TAPS):
        weights = []
        for row_off in range(TAPS):
            index = row_off * TAPS + col_off
            if flip:
                index = TAPS * TAPS - 1 - index
            weights.append(taps_ref[index : index + 1, lanes])
        for row in range(out_rows + 2 * REACH):
            start = EDGE - REACH + col_off
            line = pad_ref[tile, row, start : start + cols, :]
            for row_off in range(TAPS):
                out = row - row_off
                if 0 <= out < out_rows:
                    term = weights[row_off] * line
                    sums[out] = term if sums[out] is None else sums[out] + term
    return sums


def conv_norm_kernel(
    keep_ref, slot_ref, side_ref, row_ref, above_ref, own_ref, below_ref, cot_ref, taps_ref, vec_ref,
    unit_ref, inv_ref, cotm_ref, pad_ref, conv_ref,
):
    image = pl.program_id(0)
    rows, cols, channels = own_ref.shape[1:]

    @pl.when(image == 0)
    def _():
        clear_edges(pad_ref, cols)

    @pl.when(keep_ref[image] > 0)
    def _():
        side = side_ref[image]
        start = row_ref[0]
        fill_rows(pad_ref, 0, above_ref[0], side, start - REACH)
        fill_rows(pad_ref, REACH, own_ref[0], side, start)
        fill_rows(pad_ref, REACH + rows, below_ref[0], side, start + rows)
        for tile in range(channels // LANES):
            lanes = slice(tile * LANES, (tile + 1) * LANES)
            sums = conv_tile(pad_ref, tile, taps_ref, rows, cols, False)
            for row in range(rows):
                conv_ref[row * cols : (row + 1) * cols, lanes] = sums[row] + vec_ref[0:1, lanes]
        conv = conv_ref[...]
        mean = jnp.mean(conv, axis=-1, keepdims=True)
        centred = conv - mean
        var = jnp.mean(centred * centred, axis=-1, keepdims=True)
        inv_std = lax.rsqrt(var + norm_eps)
        unit_ref[...] = centred * inv_std
        inv_ref[...] = jnp.broadcast_to(inv_std, inv_ref.shape)
        for row in range(rows):
            line = cot_ref[0, row].astype(f32)
            reach = jnp.where(start + row < side, side, 0)
            inside = lax.broadcasted_iota(jnp.int32, (cols, channels), 0) < reach
            conv_ref[row * cols : (row + 1) * cols, :] = jnp.where(inside, line, 0.0)
        cotm_ref[...] = conv_ref[...].astype(bf16)


def dot_nn(a, b):
    return lax.dot_general(a, b, (((1,), (0,)), ((), ())), preferred_element_type=f32)


def dot_nt(a, b):
    return lax.dot_general(a, b, (((1,), (1,)), ((), ())), preferred_element_type=f32)


def fold(value):
    rows, channels = value.shape
    return jnp.sum(value.reshape(rows // 8, 8, channels), axis=0)


def mlp_kernel(
    count_ref, unit_ref, inv_ref, cotm_ref, near_ref, far_ref, bias_ref, vec_ref,
    branch_ref, gc_ref, grad_ref, bsum_ref, vsum_ref, up_acc, down_acc, scaled_ref, bias_acc, vec_acc,
):
    step = pl.program_id(0)
    rows, channels = unit_ref.shape
    half = near_ref.shape[0]
    hidden_size = 2 * half
    used = count_ref[0]
    gamma = vec_ref[4:5, :] * keep_scale

    def weights(start):
        ref = near_ref if start < half else far_ref
        base = start % half
        return ref, slice(base, base + MLP_COLS)

    @pl.when(step == 0)
    def _():
        up_acc[...] = jnp.zeros_like(up_acc)
        down_acc[...] = jnp.zeros_like(down_acc)
        bias_acc[...] = jnp.zeros_like(bias_acc)
        vec_acc[...] = jnp.zeros_like(vec_acc)
        for start in range(0, hidden_size, MLP_COLS):
            ref, part = weights(start)
            down = ref[part, channels : 2 * channels].astype(f32)
            scaled_ref[start : start + MLP_COLS, :] = (down * gamma).astype(bf16)

    @pl.when(step * rows < used)
    def _():
        inside = lax.broadcasted_iota(jnp.int32, (rows, channels), 0) < used - step * rows
        unit = jnp.where(inside, unit_ref[...], 0.0)
        cotm32 = jnp.where(inside, cotm_ref[...].astype(f32), 0.0)
        cotm = cotm32.astype(bf16)
        normed = (unit * vec_ref[1:2, :] + vec_ref[2:3, :]).astype(bf16)
        normed_t = normed.T
        cotm_t = cotm.T
        branch = None
        grad_normed = None
        for start in range(0, hidden_size, MLP_COLS):
            ref, part = weights(start)
            cols = slice(start, start + MLP_COLS)
            up = ref[part, 0:channels]
            down = ref[part, channels : 2 * channels]
            hidden = dot_nt(normed, up) + bias_ref[0:1, cols]
            cdf = 0.5 + 0.5 * lax.erf(hidden * inv_root_two)
            active = (hidden * cdf).astype(bf16)
            slope = cdf + hidden * (inv_root_tau * jnp.exp(-0.5 * hidden * hidden))
            part_branch = dot_nn(active, down)
            branch = part_branch if branch is None else branch + part_branch
            grad_hidden32 = dot_nt(cotm, scaled_ref[cols, :]) * slope
            bias_acc[:, cols] += fold(grad_hidden32)
            grad_hidden = grad_hidden32.astype(bf16)
            part_grad = dot_nn(grad_hidden, up)
            grad_normed = part_grad if grad_normed is None else grad_normed + part_grad
            up_acc[:, cols] += dot_nn(normed_t, grad_hidden)
            down_acc[:, cols] += dot_nn(cotm_t, active)
        branch = branch + vec_ref[3:4, :]
        branch_ref[...] = branch.astype(bf16)
        inv_std = inv_ref[:, 0:1]
        scaled = grad_normed * vec_ref[1:2, :]
        mean_a = jnp.mean(scaled, axis=-1, keepdims=True)
        mean_b = jnp.mean(scaled * unit, axis=-1, keepdims=True)
        grad_conv = inv_std * (scaled - mean_a - unit * mean_b)
        grad_conv = jnp.where(inside, grad_conv, 0.0)
        gc_ref[...] = grad_conv.astype(bf16)
        vec_acc[0:8, :] += fold(grad_conv)
        vec_acc[8:16, :] += fold(grad_normed * unit)
        vec_acc[16:24, :] += fold(grad_normed)
        vec_acc[24:32, :] += fold(cotm32)
        vec_acc[32:40, :] += fold(cotm32 * branch)

    @pl.when(step == pl.num_programs(0) - 1)
    def _():
        for start in range(0, hidden_size, MLP_COLS):
            cols = slice(start, start + MLP_COLS)
            grad_ref[cols, 0:channels] = up_acc[:, cols].T.astype(bf16)
            grad_ref[cols, channels : 2 * channels] = (down_acc[:, cols].T * gamma).astype(bf16)
        bsum_ref[...] = jnp.sum(bias_acc[...], axis=0, keepdims=True)
        vsum_ref[...] = jnp.zeros_like(vsum_ref)
        for row in range(5):
            total = jnp.sum(vec_acc[8 * row : 8 * row + 8, :], axis=0, keepdims=True)
            if row == 3:
                total = total * gamma
            if row == 4:
                total = total * keep_scale
            vsum_ref[row : row + 1, :] = total


def taps_grad_kernel(
    keep_ref, slot_ref, side_ref, row_ref, above_ref, own_ref, below_ref, gc_ref,
    out_ref, pad_ref, acc_ref, grad_ref,
):
    image = pl.program_id(0)
    rows, cols, channels = own_ref.shape[1:]

    @pl.when(image == 0)
    def _():
        clear_edges(pad_ref, cols)
        acc_ref[...] = jnp.zeros_like(acc_ref)

    @pl.when(keep_ref[image] > 0)
    def _():
        side = side_ref[image]
        start = row_ref[0]
        fill_rows(pad_ref, 0, above_ref[0], side, start - REACH)
        fill_rows(pad_ref, REACH, own_ref[0], side, start)
        fill_rows(pad_ref, REACH + rows, below_ref[0], side, start + rows)
        grad_ref[...] = gc_ref[...].astype(f32)
        for tile in range(channels // LANES):
            lanes = slice(tile * LANES, (tile + 1) * LANES)
            lines = [grad_ref[row * cols : (row + 1) * cols, lanes] for row in range(rows)]
            for col_off in range(TAPS):
                sums = [None] * TAPS
                for row in range(rows + 2 * REACH):
                    at = EDGE - REACH + col_off
                    line = pad_ref[tile, row, at : at + cols, :]
                    for row_off in range(TAPS):
                        out = row - row_off
                        if 0 <= out < rows:
                            term = line * lines[out]
                            sums[row_off] = term if sums[row_off] is None else sums[row_off] + term
                for row_off in range(TAPS):
                    index = row_off * TAPS + col_off
                    acc_ref[index, :, lanes] += fold(sums[row_off])

    @pl.when(image == pl.num_programs(0) - 1)
    def _():
        out_ref[...] = jnp.sum(acc_ref[...], axis=1)


def finish_kernel(
    keep_ref, slot_ref, side_ref, row_ref, above_ref, own_ref, below_ref, branch_ref, image_ref, cot_ref, taps_ref, vec_ref,
    out_ref, gim_ref, pad_ref,
):
    image = pl.program_id(0)
    rows, cols, channels = image_ref.shape[1:]

    @pl.when(image == 0)
    def _():
        clear_edges(pad_ref, cols)

    @pl.when(keep_ref[image] > 0)
    def _():
        side = side_ref[image]
        start = row_ref[0]
        fill_rows(pad_ref, 0, above_ref[0])
        fill_rows(pad_ref, REACH, own_ref[...].astype(f32).reshape(rows, cols, channels))
        fill_rows(pad_ref, REACH + rows, below_ref[0])
        branch = branch_ref[...].astype(f32).reshape(rows, cols, channels)
        scale = vec_ref[4:5, :] * keep_scale
        for tile in range(channels // LANES):
            lanes = slice(tile * LANES, (tile + 1) * LANES)
            sums = conv_tile(pad_ref, tile, taps_ref, rows, cols, True)
            for row in range(rows):
                reach = jnp.where(start + row < side, side, 0)
                inside = lax.broadcasted_iota(jnp.int32, (cols, LANES), 0) < reach
                grad = cot_ref[0, row, :, lanes].astype(f32) + jnp.where(inside, sums[row], 0.0)
                gim_ref[0, row, :, lanes] = grad.astype(bf16)
                extra = jnp.where(inside, branch[row, :, lanes] * scale[:, lanes], 0.0)
                out = image_ref[0, row, :, lanes].astype(f32) + extra
                out_ref[0, row, :, lanes] = out.astype(bf16)

    @pl.when(keep_ref[image] == 0)
    def _():
        out_ref[...] = image_ref[...]
        gim_ref[...] = cot_ref[...]


def params(mib):
    return pltpu.CompilerParams(dimension_semantics=("arbitrary",), vmem_limit_bytes=mib * MIB)


def conv_norm(scalars, above, own, below, cot, taps, vecs):
    count, rows, cols, channels = own.shape
    pixels = rows * cols
    image_map = lambda i, k, s, d, r: (i, 0, 0, 0)
    whole = lambda i, k, s, d, r: (0, 0)
    slot_map = lambda i, k, s, d, r: (s[i], 0)
    return pl.pallas_call(
        conv_norm_kernel,
        grid_spec=pltpu.PrefetchScalarGridSpec(
            num_scalar_prefetch=4,
            grid=(count,),
            in_specs=[
                pl.BlockSpec((1, REACH, cols, channels), image_map),
                pl.BlockSpec((1, rows, cols, channels), image_map),
                pl.BlockSpec((1, REACH, cols, channels), image_map),
                pl.BlockSpec((1, rows, cols, channels), image_map),
                pl.BlockSpec(taps.shape, whole),
                pl.BlockSpec(vecs.shape, whole),
            ],
            out_specs=[
                pl.BlockSpec((pixels, channels), slot_map),
                pl.BlockSpec((pixels, LANES), slot_map),
                pl.BlockSpec((pixels, channels), slot_map),
            ],
            scratch_shapes=[
                pltpu.VMEM((channels // LANES, rows + 2 * REACH, cols + 2 * EDGE, LANES), f32),
                pltpu.VMEM((pixels, channels), f32),
            ],
        ),
        out_shape=[
            jax.ShapeDtypeStruct((count * pixels, channels), f32),
            jax.ShapeDtypeStruct((count * pixels, LANES), f32),
            jax.ShapeDtypeStruct((count * pixels, channels), bf16),
        ],
        compiler_params=params(40),
        name="conv_norm",
    )(*scalars, above, own, below, cot, taps, vecs)


def mlp(used, unit, inv_std, cotm, near, far, bias, vecs):
    total, channels = unit.shape
    hidden_size = bias.shape[1]
    steps = total // MLP_ROWS

    def tile_map(i, n):
        return (jnp.minimum(i, jnp.maximum((n[0] + MLP_ROWS - 1) // MLP_ROWS - 1, 0)), 0)

    whole = lambda i, n: (0, 0)
    return pl.pallas_call(
        mlp_kernel,
        grid_spec=pltpu.PrefetchScalarGridSpec(
            num_scalar_prefetch=1,
            grid=(steps,),
            in_specs=[
                pl.BlockSpec((MLP_ROWS, channels), tile_map),
                pl.BlockSpec((MLP_ROWS, LANES), tile_map),
                pl.BlockSpec((MLP_ROWS, channels), tile_map),
                pl.BlockSpec(near.shape, whole),
                pl.BlockSpec(far.shape, whole),
                pl.BlockSpec(bias.shape, whole),
                pl.BlockSpec(vecs.shape, whole),
            ],
            out_specs=[
                pl.BlockSpec((MLP_ROWS, channels), tile_map),
                pl.BlockSpec((MLP_ROWS, channels), tile_map),
                pl.BlockSpec((hidden_size, 2 * channels), whole),
                pl.BlockSpec((1, hidden_size), whole),
                pl.BlockSpec((8, channels), whole),
            ],
            scratch_shapes=[
                pltpu.VMEM((channels, hidden_size), f32),
                pltpu.VMEM((channels, hidden_size), f32),
                pltpu.VMEM((hidden_size, channels), bf16),
                pltpu.VMEM((8, hidden_size), f32),
                pltpu.VMEM((40, channels), f32),
            ],
        ),
        out_shape=[
            jax.ShapeDtypeStruct((total, channels), bf16),
            jax.ShapeDtypeStruct((total, channels), bf16),
            jax.ShapeDtypeStruct((hidden_size, 2 * channels), bf16),
            jax.ShapeDtypeStruct((1, hidden_size), f32),
            jax.ShapeDtypeStruct((8, channels), f32),
        ],
        compiler_params=params(56),
        name="mlp",
    )(used, unit, inv_std, cotm, near, far, bias, vecs)


def taps_grad(scalars, above, own, below, gc):
    count, rows, cols, channels = own.shape
    pixels = rows * cols
    image_map = lambda i, k, s, d, r: (i, 0, 0, 0)
    return pl.pallas_call(
        taps_grad_kernel,
        grid_spec=pltpu.PrefetchScalarGridSpec(
            num_scalar_prefetch=4,
            grid=(count,),
            in_specs=[
                pl.BlockSpec((1, REACH, cols, channels), image_map),
                pl.BlockSpec((1, rows, cols, channels), image_map),
                pl.BlockSpec((1, REACH, cols, channels), image_map),
                pl.BlockSpec((pixels, channels), lambda i, k, s, d, r: (s[i], 0)),
            ],
            out_specs=pl.BlockSpec((TAPS * TAPS, channels), lambda i, k, s, d, r: (0, 0)),
            scratch_shapes=[
                pltpu.VMEM((channels // LANES, rows + 2 * REACH, cols + 2 * EDGE, LANES), f32),
                pltpu.VMEM((TAPS * TAPS, 8, channels), f32),
                pltpu.VMEM((pixels, channels), f32),
            ],
        ),
        out_shape=jax.ShapeDtypeStruct((TAPS * TAPS, channels), f32),
        compiler_params=params(40),
        name="taps_grad",
    )(*scalars, above, own, below, gc)


def finish(scalars, above, gc, below, branch, images, cot, taps, vecs):
    count, rows, cols, channels = images.shape
    pixels = rows * cols
    image_map = lambda i, k, s, d, r: (i, 0, 0, 0)
    slot_map = lambda i, k, s, d, r: (s[i], 0)
    slot_halo = lambda i, k, s, d, r: (s[i], 0, 0, 0)
    whole = lambda i, k, s, d, r: (0, 0)
    return pl.pallas_call(
        finish_kernel,
        grid_spec=pltpu.PrefetchScalarGridSpec(
            num_scalar_prefetch=4,
            grid=(count,),
            in_specs=[
                pl.BlockSpec((1, REACH, cols, channels), slot_halo),
                pl.BlockSpec((pixels, channels), slot_map),
                pl.BlockSpec((1, REACH, cols, channels), slot_halo),
                pl.BlockSpec((pixels, channels), slot_map),
                pl.BlockSpec((1, rows, cols, channels), image_map),
                pl.BlockSpec((1, rows, cols, channels), image_map),
                pl.BlockSpec(taps.shape, whole),
                pl.BlockSpec(vecs.shape, whole),
            ],
            out_specs=[
                pl.BlockSpec((1, rows, cols, channels), image_map),
                pl.BlockSpec((1, rows, cols, channels), image_map),
            ],
            scratch_shapes=[
                pltpu.VMEM((channels // LANES, rows + 2 * REACH, cols + 2 * EDGE, LANES), f32),
            ],
        ),
        out_shape=[
            jax.ShapeDtypeStruct(images.shape, bf16),
            jax.ShapeDtypeStruct(images.shape, bf16),
        ],
        compiler_params=params(40),
        name="finish",
    )(*scalars, above, gc, below, branch, images, cot, taps, vecs)


def neighbour_rows(value, places):
    above = lax.ppermute(value[:, -REACH:], "space", [(i, i + 1) for i in range(places - 1)])
    below = lax.ppermute(value[:, :REACH], "space", [(i + 1, i) for i in range(places - 1)])
    return above, below


def spread(value, devices):
    sent = jnp.broadcast_to(value[None], (devices,) + value.shape)
    return lax.all_to_all(sent, AXES, 0, 0, tiled=True)


def flip_perm(size, bit):
    return [(i, i ^ bit) for i in range(size)]


def swap(value, bits):
    axis, bit, size = ("dp", bits[0], 8) if bits[0] else ("space", bits[1], 4)
    return lax.ppermute(value, axis, flip_perm(size, bit))


X, Y, CORE = (1, 0), (0, 2), (0, 1)
Z1, Z2, Z3 = (2, 0), (4, 0), (6, 0)


def cube_order():
    first = [0, 2 * 4]
    last = [4 * 4, 6 * 4]
    first = first + [v ^ 4 for v in first]
    last = last + [v ^ 2 for v in last]
    first = first + [v ^ 2 for v in first]
    last = last + [v ^ 4 for v in last]
    near = first + last
    return near + [v ^ 1 for v in near]


def join(*parts):
    return jnp.concatenate(parts, axis=0)


def gather_cube(piece):
    first = join(piece, swap(piece, Z1))
    last = join(swap(piece, Z2), swap(piece, Z3))
    first = join(first, swap(first, X))
    last = join(last, swap(last, Y))
    near = join(first, swap(first, Y), last, swap(last, X))
    return near, swap(near, CORE)


def scatter_cube(value):
    half = value.shape[0] // 2
    near = value[:half].astype(f32) + swap(value[half:], CORE).astype(f32)
    first, last = near[: half // 2], near[half // 2 :]
    rows = half // 4
    got_first = swap(first[rows:].astype(bf16), Y)
    got_last = swap(last[rows:].astype(bf16), X)
    first = first[:rows] + got_first.astype(f32)
    last = last[:rows] + got_last.astype(f32)
    rows = rows // 2
    got_first = swap(first[rows:].astype(bf16), X)
    got_last = swap(last[rows:].astype(bf16), Y)
    first = first[:rows] + got_first.astype(f32)
    last = last[:rows] + got_last.astype(f32)
    rows = rows // 2
    one = swap(first[rows:].astype(bf16), Z1)
    two = swap(last[:rows].astype(bf16), Z2)
    three = swap(last[rows:].astype(bf16), Z3)
    return first[:rows] + one.astype(f32) + two.astype(f32) + three.astype(f32)


def by_owner(value, devices):
    rows, width = value.shape
    return value.reshape(rows, devices, width // devices).transpose(1, 0, 2).reshape(devices, -1)


def from_owner(value, rows):
    devices = value.shape[0]
    return value.reshape(devices, rows, -1).transpose(1, 0, 2).reshape(rows, -1)


def pack_lanes(value):
    devices, size = value.shape
    padded = -(-size // (8 * LANES)) * 8 * LANES
    return jnp.pad(value, ((0, 0), (0, padded - size))).reshape(devices, padded // LANES, LANES)


def adam_update(weight, moment, square, grad_part, factor, step_rate):
    scaled = grad_part * factor
    new_moment = beta_one * moment + (1.0 - beta_one) * scaled
    new_square = beta_two * square + (1.0 - beta_two) * scaled * scaled
    corrected = new_moment / (1.0 - beta_one**STEP)
    spread_ = jnp.sqrt(new_square / (1.0 - beta_two**STEP))
    new_weight = weight - step_rate * (corrected / (spread_ + adam_eps) + decay_rate * weight)
    return (new_weight, new_moment, new_square)


def body(
    dp_size, space_size,
    images, cotangent, image_sides, keep_flags,
    depth_kernel, kernel_moment, kernel_square,
    block_vectors, vector_moment, vector_square,
    up_weight, up_moment, up_square,
    up_bias, bias_moment, bias_square,
    down_weight, down_moment, down_square,
):
    devices = dp_size * space_size
    count, rows, cols, channels = images.shape
    pixels = rows * cols
    part = up_weight.shape[1]
    width = depth_kernel.shape[1]
    taps_n, vecs_n = depth_kernel.shape[0], block_vectors.shape[0]
    place = lax.axis_index("space")
    me = lax.axis_index(AXES)
    cube = dp_size == 8 and space_size == 4

    above, below = neighbour_rows(images, space_size)
    small = jnp.concatenate([depth_kernel.reshape(-1), block_vectors.reshape(-1), up_bias])
    small_all = spread(pack_lanes(small[None])[0], devices).reshape(devices, -1)
    piece = jnp.concatenate([up_weight.astype(bf16).T, down_weight.astype(bf16)], axis=1)
    if cube:
        near, far = gather_cube(piece)
        order = me ^ jnp.array(cube_order(), jnp.int32)
    else:
        whole = lax.all_gather(piece, AXES, axis=0, tiled=True)
        near, far = whole[: whole.shape[0] // 2], whole[whole.shape[0] // 2 :]
        order = jnp.arange(devices, dtype=jnp.int32)
    cut_a, cut_b = taps_n * width, (taps_n + vecs_n) * width
    taps = from_owner(small_all[:, :cut_a], taps_n)
    vecs = jnp.pad(from_owner(small_all[:, cut_a:cut_b], vecs_n), ((0, 3), (0, 0)))
    bias_own = small_all[:, cut_b : cut_b + part]
    hits = (order[:, None] == jnp.arange(devices, dtype=jnp.int32)[None, :])
    bias = jnp.sum(jnp.where(hits[:, :, None], bias_own[None], 0.0), axis=1).reshape(1, -1)

    keep = (keep_flags > 0).astype(jnp.int32)
    ids = jnp.arange(count, dtype=jnp.int32)
    before = jnp.sum(jnp.where(ids[None, :] <= ids[:, None], keep[None, :], 0), axis=1)
    slot = jnp.maximum(before - 1, 0)
    used = (jnp.sum(keep) * pixels).reshape(1)
    first_row = (place * rows).astype(jnp.int32).reshape(1)
    scalars = (keep, slot, image_sides, first_row)

    unit, inv_std, cotm = conv_norm(scalars, above, images, below, cotangent, taps, vecs)
    branch, gc, grads, bias_sum, vec_sum = mlp(used, unit, inv_std, cotm, near, far, bias, vecs)
    gc_above, gc_below = neighbour_rows(gc.reshape(count, rows, cols, channels), space_size)
    taps_sum = taps_grad(scalars, above, images, below, gc)
    if cube:
        own = scatter_cube(grads)
    else:
        own = lax.psum_scatter(grads.astype(f32), AXES, scatter_dimension=0, tiled=True)
    bias_rows = bias_sum.reshape(devices, part)
    bias_true = jnp.sum(jnp.where(hits[:, :, None], bias_rows[:, None], 0.0), axis=0)
    mine = jnp.concatenate([by_owner(taps_sum, devices), by_owner(vec_sum[:vecs_n], devices), bias_true], axis=1)
    got = jnp.sum(lax.all_to_all(pack_lanes(mine), AXES, 0, 0, tiled=True), axis=0).reshape(-1)
    grad_kernel = got[:cut_a].reshape(taps_n, width)
    grad_vectors = got[cut_a:cut_b].reshape(vecs_n, width)
    grad_bias = got[cut_b : cut_b + part]
    grad_up = own[:, :channels].T
    grad_down = own[:, channels:]
    local = jnp.sum(own * own) + jnp.sum(got * got)
    total = jnp.sum(spread(jnp.broadcast_to(local, (8, LANES)), devices)[:, 0, 0] if False else spread(jnp.broadcast_to(local, (8, LANES)), devices).reshape(devices, 8, LANES)[:, 0, 0])
    out_images, grad_images = finish(scalars, gc_above, gc, gc_below, branch, images, cotangent, taps, vecs)
    grad_norm = jnp.sqrt(total)
    factor = clip_limit / jnp.maximum(grad_norm, clip_limit)
    states = (
        (depth_kernel, kernel_moment, kernel_square),
        (block_vectors, vector_moment, vector_square),
        (up_weight, up_moment, up_square),
        (up_bias, bias_moment, bias_square),
        (down_weight, down_moment, down_square),
    )
    shards = (grad_kernel, grad_vectors, grad_up, grad_bias, grad_down)
    results = []
    for (weight, moment, square), grad_part, step_rate in zip(states, shards, step_rates):
        results.extend(adam_update(weight, moment, square, grad_part, factor, step_rate))
    return (out_images, grad_images, *results, grad_norm)


def solution(mesh):
    lanes = P(None, AXES)
    flat = P(AXES)
    tall = P(AXES, None)
    maps = P("dp", "space", None, None)
    in_specs = (maps, maps, P("dp"), P("dp")) + (lanes,) * 9 + (flat,) * 3 + (tall,) * 3
    out_specs = (maps, maps) + (lanes,) * 9 + (flat,) * 3 + (tall,) * 3 + (P(),)
    run = functools.partial(body, mesh.shape["dp"], mesh.shape["space"])
    return jax.shard_map(run, mesh=mesh, in_specs=in_specs, out_specs=out_specs, check_vma=False)
```

```python
import functools

import jax
import jax.numpy as jnp
from jax import lax
from jax.experimental import pallas as pl
from jax.experimental.pallas import tpu as pltpu
from jax.sharding import PartitionSpec as P

STEP = 5

keep_scale = 4.0 / 3.0
norm_eps = 1e-06
clip_limit = 1.0
beta_one = 0.9
beta_two = 0.999
adam_eps = 1e-08
decay_rate = 0.05
step_rates = (0.15, 0.5, 0.05, 0.2, 0.025)
inv_root_two = 0.7071067811865476
inv_root_tau = 0.3989422804014327
f32 = jnp.float32
bf16 = jnp.bfloat16
AXES = ("dp", "space")
LANES = 128
REACH = 3
TAPS = 7
VEC = TAPS * TAPS
ROWS = 64
EDGE = 8
MLP_SLOTS = 4
VMEM_MIB = 60
DEPTH = 5
AHEAD = DEPTH - 2
MLP_COLS = 768
MIB = 1 << 20


def dot_nn(a, b):
    return lax.dot_general(a, b, (((1,), (0,)), ((), ())), preferred_element_type=f32)


def dot_nt(a, b):
    return lax.dot_general(a, b, (((1,), (1,)), ((), ())), preferred_element_type=f32)


def fold(value):
    rows, channels = value.shape
    return jnp.sum(value.reshape(rows // 8, 8, channels), axis=0)


def mlp_kernel(
    count_ref, unit_ref, stat_ref, cot_ref, bias_ref, par_ref, *refs
):
    step = pl.program_id(0)
    rows, channels = unit_ref.shape
    pieces = refs[:-14]
    (branch_ref, gc_ref, top_ref, low_ref, grad_near_ref, grad_far_ref, bsum_ref, vsum_ref,
     up_acc, down_acc, scaled_ref, both_ref, bias_acc, vec_acc) = refs[-14:]
    hidden_size = both_ref.shape[0]
    half = hidden_size // 2
    pixels = rows // MLP_SLOTS
    used = count_ref[0] * pixels
    gamma = par_ref[VEC + 4 : VEC + 5, :] * keep_scale

    @pl.when(step == 0)
    def _():
        up_acc[...] = jnp.zeros_like(up_acc)
        down_acc[...] = jnp.zeros_like(down_acc)
        bias_acc[...] = jnp.zeros_like(bias_acc)
        vec_acc[...] = jnp.zeros_like(vec_acc)
        at = 0
        for ref in pieces:
            size = ref.shape[0]
            both_ref[at : at + size, :] = ref[...]
            down = ref[:, channels : 2 * channels].astype(f32)
            scaled_ref[at : at + size, :] = (down * gamma).astype(bf16)
            at += size

    @pl.when(step * rows < used)
    def _():
        inside = lax.broadcasted_iota(jnp.int32, (rows, channels), 0) < used - step * rows
        unit = jnp.where(inside, unit_ref[...], 0.0)
        valid = stat_ref[:, LANES // 2 : LANES // 2 + 1]
        cotm32 = jnp.where(inside, cot_ref[...].astype(f32) * valid, 0.0)
        cotm = cotm32.astype(bf16)
        normed = (unit * par_ref[VEC + 1 : VEC + 2, :] + par_ref[VEC + 2 : VEC + 3, :]).astype(bf16)
        normed_t = normed.T
        cotm_t = cotm.T
        branch = None
        grad_normed = None
        for start in range(0, hidden_size, MLP_COLS):
            cols = slice(start, start + MLP_COLS)
            up = both_ref[cols, 0:channels]
            down = both_ref[cols, channels : 2 * channels]
            hidden = dot_nt(normed, up) + bias_ref[0:1, cols]
            cdf = 0.5 + 0.5 * lax.erf(hidden * inv_root_two)
            active = (hidden * cdf).astype(bf16)
            slope = cdf + hidden * (inv_root_tau * jnp.exp(-0.5 * hidden * hidden))
            part_branch = dot_nn(active, down)
            branch = part_branch if branch is None else branch + part_branch
            grad_hidden32 = dot_nt(cotm, scaled_ref[cols, :]) * slope
            bias_acc[:, cols] += fold(grad_hidden32)
            grad_hidden = grad_hidden32.astype(bf16)
            part_grad = dot_nn(grad_hidden, up)
            grad_normed = part_grad if grad_normed is None else grad_normed + part_grad
            up_acc[:, cols] += dot_nn(normed_t, grad_hidden)
            down_acc[:, cols] += dot_nn(cotm_t, active)
        branch = branch + par_ref[VEC + 3 : VEC + 4, :]
        branch_ref[...] = branch.astype(bf16).reshape(branch_ref.shape)
        inv_std = stat_ref[:, 0:1]
        scaled = grad_normed * par_ref[VEC + 1 : VEC + 2, :]
        mean_a = jnp.mean(scaled, axis=-1, keepdims=True)
        mean_b = jnp.mean(scaled * unit, axis=-1, keepdims=True)
        grad_conv = inv_std * (scaled - mean_a - unit * mean_b)
        grad_conv = jnp.where(inside, grad_conv, 0.0)
        maps = grad_conv.reshape(gc_ref.shape).astype(bf16)
        gc_ref[...] = maps
        top_ref[...] = maps[:, :REACH]
        low_ref[...] = maps[:, -REACH:]
        vec_acc[0:8, :] += fold(grad_conv)
        vec_acc[8:16, :] += fold(grad_normed * unit)
        vec_acc[16:24, :] += fold(grad_normed)
        vec_acc[24:32, :] += fold(cotm32)
        vec_acc[32:40, :] += fold(cotm32 * branch)

    @pl.when(step == pl.num_programs(0) - 1)
    def _():
        for start in range(0, hidden_size, MLP_COLS):
            cols = slice(start, start + MLP_COLS)
            ref = grad_near_ref if start < half else grad_far_ref
            part = slice(start % half, start % half + MLP_COLS)
            ref[part, 0:channels] = up_acc[:, cols].T.astype(bf16)
            ref[part, channels : 2 * channels] = (down_acc[:, cols].T * gamma).astype(bf16)
        bsum_ref[...] = jnp.sum(bias_acc[...], axis=0, keepdims=True)
        vsum_ref[...] = jnp.zeros_like(vsum_ref)
        for row in range(5):
            total = jnp.sum(vec_acc[8 * row : 8 * row + 8, :], axis=0, keepdims=True)
            if row == 3:
                total = total * gamma
            if row == 4:
                total = total * keep_scale
            vsum_ref[row : row + 1, :] = total


def walk(low, high, fetch, compute, store, load, prepare):
    def begin(i, carry):
        for copy in fetch(i, lax.rem(i - low, DEPTH)):
            copy.start()
        return carry

    def end(i, carry):
        for copy in store(i, lax.rem(i - low, DEPTH)):
            copy.wait()
        return carry

    if load is not None:
        load.start()
    lax.fori_loop(low, jnp.minimum(high, low + AHEAD), begin, 0)
    prepare()
    if load is not None:
        load.wait()

    def step(i, carry):
        buf = lax.rem(i - low, DEPTH)
        for copy in fetch(i, buf):
            copy.wait()

        @pl.when(i - low >= 2)
        def _():
            end(i - 2, 0)

        @pl.when(i + AHEAD < high)
        def _():
            begin(i + AHEAD, 0)

        compute(i, buf)
        for copy in store(i, buf):
            copy.start()
        return carry

    lax.fori_loop(low, high, step, 0)
    lax.fori_loop(jnp.maximum(low, high - 2), high, end, 0)


def copies(pairs, sems, buf):
    return [pltpu.make_async_copy(src, dst, sems.at[buf, at]) for at, (src, dst) in enumerate(pairs)]


def clear_edges(pad_ref, cols):
    tiles, rows, width, lanes = pad_ref.shape
    for tile in range(tiles):
        for row in range(rows):
            pad_ref[tile, row, 0:EDGE, :] = jnp.zeros((EDGE, lanes), f32)
            pad_ref[tile, row, EDGE + cols : width, :] = jnp.zeros((width - EDGE - cols, lanes), f32)


def inside_cols(cols, row, side):
    reach = jnp.where(row < side, side, 0)
    return lax.broadcasted_iota(jnp.int32, (cols, LANES), 0) < reach


def fill_rows(pad_ref, win_ref, side=None, first_row=None):
    rows, cols, channels = win_ref.shape
    for row in range(rows):
        inside = None if side is None else inside_cols(cols, first_row + row, side)
        for tile in range(channels // LANES):
            line = win_ref[row, :, tile * LANES : (tile + 1) * LANES].astype(f32)
            if side is not None:
                line = jnp.where(inside, line, 0.0)
            pad_ref[tile, row, EDGE : EDGE + cols, :] = line


def conv_tile(pad_ref, tile, par_ref, out_rows, cols, flip):
    lanes = slice(tile * LANES, (tile + 1) * LANES)
    sums = [None] * out_rows
    for col_off in range(TAPS):
        weights = []
        for row_off in range(TAPS):
            index = row_off * TAPS + col_off
            if flip:
                index = TAPS * TAPS - 1 - index
            weights.append(par_ref[index : index + 1, lanes])
        for row in range(out_rows + 2 * REACH):
            start = EDGE - REACH + col_off
            line = pad_ref[tile, row, start : start + cols, :]
            for row_off in range(TAPS):
                out = row - row_off
                if 0 <= out < out_rows:
                    term = weights[row_off] * line
                    sums[out] = term if sums[out] is None else sums[out] + term
    return sums


def conv_norm_kernel(
    which, first, order_ref, range_ref, side_ref, above_ref, own_ref, below_ref, cot_ref, pars_ref, *rest
):
    (unit_ref, stat_ref, cots_ref, win_ref, unit_buf, stat_buf, cot_buf, pad_ref, conv_ref, par_ref,
     in_sems, out_sems, par_sem) = rest[-13:]
    rows, cols, channels = own_ref.shape[1:]
    low, high, start = range_ref[which, 0], range_ref[which, 1], range_ref[which, 2]

    def fetch(i, buf):
        image = order_ref[i]
        win = win_ref.at[buf]
        return copies(
            [
                (above_ref.at[image - first], win.at[0:REACH]),
                (own_ref.at[image], win.at[REACH : REACH + rows]),
                (below_ref.at[image - first], win.at[REACH + rows : 2 * REACH + rows]),
                (cot_ref.at[image], cot_buf.at[buf]),
            ],
            in_sems,
            buf,
        )

    def store(i, buf):
        pairs = [(unit_buf, unit_ref), (stat_buf, stat_ref), (cot_buf, cots_ref)]
        return copies([(mine.at[buf], ref.at[i]) for mine, ref in pairs], out_sems, buf)

    def compute(i, buf):
        side = side_ref[order_ref[i]]
        fill_rows(pad_ref, win_ref.at[buf], side, start - REACH)
        for tile in range(channels // LANES):
            lanes = slice(tile * LANES, (tile + 1) * LANES)
            sums = conv_tile(pad_ref, tile, par_ref, rows, cols, False)
            for row in range(rows):
                conv_ref[row * cols : (row + 1) * cols, lanes] = sums[row] + par_ref[VEC : VEC + 1, lanes]

        @pl.when(i < high)
        def _():
            conv = conv_ref[...]
            mean = jnp.mean(conv, axis=-1, keepdims=True)
            centred = conv - mean
            var = jnp.mean(centred * centred, axis=-1, keepdims=True)
            inv_std = lax.rsqrt(var + norm_eps)
            unit_buf[buf] = centred * inv_std
            left = lax.broadcasted_iota(jnp.int32, (cols, LANES), 1) < LANES // 2
            for row in range(rows):
                inside = inside_cols(cols, start + row, side)
                spread_inv = jnp.broadcast_to(inv_std[row * cols : (row + 1) * cols], (cols, LANES))
                lines = slice(row * cols, (row + 1) * cols)
                stat_buf[buf, lines, :] = jnp.where(left, spread_inv, jnp.where(inside, 1.0, 0.0))

    load = pltpu.make_async_copy(pars_ref, par_ref, par_sem)
    walk(low, high, fetch, compute, store, load, lambda: clear_edges(pad_ref, cols))


def fill_pairs(pair_ref, win_ref, side=None, first_row=None):
    tiles, pairs = pair_ref.shape[:2]
    rows, cols, channels = win_ref.shape
    apart = rows - pairs
    for row in range(rows):
        if side is not None:
            mask = jnp.where(inside_cols(cols, first_row + row, side), 1.0, 0.0).astype(bf16)
        for tile in range(tiles):
            line = win_ref[row, :, tile * LANES : (tile + 1) * LANES]
            if side is not None:
                line = line * mask
            if row < pairs:
                pair_ref[tile, row, 0:cols, :] = line
            if row >= apart:
                pair_ref[tile, row - apart, cols : 2 * cols, :] = line


def taps_grad_kernel(
    which, split, order_ref, range_ref, side_ref, above_ref, own_ref, below_ref, far_above_ref, far_below_ref, gc_ref,
    out_ref, win_ref, gc_buf, pair_ref, acc_ref, grad_ref, in_sems,
):
    rows, cols, channels = own_ref.shape[1:]
    half = rows // 2
    low, high, start = range_ref[which, 0], range_ref[which, 1], range_ref[which, 2]

    def halo_copies(above, below, image, buf):
        win = win_ref.at[buf]
        return [
            pltpu.make_async_copy(above.at[image], win.at[0:REACH], in_sems.at[buf, 2]),
            pltpu.make_async_copy(below.at[image], win.at[REACH + rows : 2 * REACH + rows], in_sems.at[buf, 3]),
        ]

    class Halo:
        def __init__(self, image, buf):
            self.image, self.buf = image, buf

        def start(self):
            @pl.when(self.image < split)
            def _():
                for copy in halo_copies(above_ref, below_ref, self.image, self.buf):
                    copy.start()

            @pl.when(self.image >= split)
            def _():
                for copy in halo_copies(far_above_ref, far_below_ref, self.image - split, self.buf):
                    copy.start()

        def wait(self):
            for copy in halo_copies(above_ref, below_ref, 0, self.buf):
                copy.wait()

    def fetch(i, buf):
        image = order_ref[i]
        win = win_ref.at[buf]
        near = copies([(own_ref.at[image], win.at[REACH : REACH + rows]), (gc_ref.at[i], gc_buf.at[buf])], in_sems, buf)
        return near + [Halo(image, buf)]

    def compute(i, buf):
        fill_pairs(pair_ref, win_ref.at[buf], side_ref[order_ref[i]], start - REACH)
        for row in range(rows):
            for tile in range(channels // LANES):
                line = gc_buf[buf, row, :, tile * LANES : (tile + 1) * LANES]
                grad_ref[tile, row, EDGE : EDGE + cols, :] = line.astype(f32)
        for tile in range(channels // LANES):
            lanes = slice(tile * LANES, (tile + 1) * LANES)
            for col_off in range(TAPS):
                at = EDGE + REACH - col_off
                grads = []
                for row in range(half):
                    two = [grad_ref[tile, row, at : at + cols, :], grad_ref[tile, row + half, at : at + cols, :]]
                    grads.append(jnp.concatenate(two, axis=0).astype(bf16))
                for row_off in range(TAPS):
                    total = grads[0] * pair_ref[tile, row_off]
                    for row in range(1, half):
                        total = total + grads[row] * pair_ref[tile, row_off + row]
                    total = total[0:16] + total[16:32] + total[32:48]
                    acc_ref[row_off * TAPS + col_off, :, lanes] += fold(total.astype(f32))

    def prepare():
        acc_ref[...] = jnp.zeros_like(acc_ref)
        clear_edges(grad_ref, cols)

    walk(low, high, fetch, compute, lambda i, buf: [], None, prepare)
    out_ref[...] = jnp.sum(acc_ref[...], axis=1)


def finish_kernel(
    which, order_ref, range_ref, side_ref, above_ref, gc_ref, below_ref, branch_ref, image_ref, cot_ref, pars_ref, *rest
):
    (out_ref, gim_ref, win_ref, branch_buf, image_buf, cot_buf, out_buf, gim_buf, pair_ref, part_ref, sum_ref, par_ref,
     in_sems, out_sems, par_sem) = rest[-15:]
    rows, cols, channels = image_ref.shape[1:]
    half = rows // 2
    low, high, start = range_ref[which, 0], range_ref[which, 1], range_ref[which, 2]
    plain_low, plain_high = range_ref[which, 3], range_ref[which, 4]

    def fetch(i, buf):
        image = order_ref[i]
        win = win_ref.at[buf]
        return copies(
            [
                (above_ref.at[i], win.at[0:REACH]),
                (gc_ref.at[i], win.at[REACH : REACH + rows]),
                (below_ref.at[i], win.at[REACH + rows : 2 * REACH + rows]),
                (branch_ref.at[i], branch_buf.at[buf]),
                (image_ref.at[image], image_buf.at[buf]),
                (cot_ref.at[image], cot_buf.at[buf]),
            ],
            in_sems,
            buf,
        )

    def store(i, buf):
        image = order_ref[i]
        return copies([(out_buf.at[buf], out_ref.at[image]), (gim_buf.at[buf], gim_ref.at[image])], out_sems, buf)

    def pass_in(i, buf):
        image = order_ref[i]
        return copies([(image_ref.at[image], image_buf.at[buf]), (cot_ref.at[image], cot_buf.at[buf])], in_sems, buf)

    def pass_out(i, buf):
        image = order_ref[i]
        return copies([(image_buf.at[buf], out_ref.at[image]), (cot_buf.at[buf], gim_ref.at[image])], out_sems, buf)

    def compute(i, buf):
        side = side_ref[order_ref[i]]
        fill_pairs(pair_ref, win_ref.at[buf])
        for tile in range(channels // LANES):
            lanes = slice(tile * LANES, (tile + 1) * LANES)
            for col_off in range(TAPS):
                at = EDGE
                weights = []
                for row_off in range(TAPS):
                    index = TAPS * TAPS - 1 - row_off * TAPS - col_off
                    weights.append(par_ref[index : index + 1, lanes].astype(bf16))
                for row in range(half):
                    total = weights[0] * pair_ref[tile, row]
                    for row_off in range(1, TAPS):
                        total = total + weights[row_off] * pair_ref[tile, row + row_off]
                    total = total.astype(f32)
                    part_ref[col_off, row, at : at + cols, :] = total[0:cols]
                    part_ref[col_off, row + half, at : at + cols, :] = total[cols : 2 * cols]
            for row in range(rows):
                total = part_ref[REACH, row, EDGE : EDGE + cols, :]
                for col_off in range(TAPS):
                    if col_off != REACH:
                        at = EDGE - REACH + col_off
                        total = total + part_ref[col_off, row, at : at + cols, :]
                sum_ref[row, :, lanes] = total

        @pl.when(i < high)
        def _():
            scale = par_ref[VEC + 4 : VEC + 5, :] * keep_scale
            for row in range(rows):
                inside = inside_cols(cols, start + row, side)
                for tile in range(channels // LANES):
                    lanes = slice(tile * LANES, (tile + 1) * LANES)
                    grad = cot_buf[buf, row, :, lanes].astype(f32) + jnp.where(inside, sum_ref[row, :, lanes], 0.0)
                    gim_buf[buf, row, :, lanes] = grad.astype(bf16)
                    extra = branch_buf[buf, row, :, lanes].astype(f32) * scale[:, lanes]
                    out = image_buf[buf, row, :, lanes].astype(f32) + jnp.where(inside, extra, 0.0)
                    out_buf[buf, row, :, lanes] = out.astype(bf16)

    load = pltpu.make_async_copy(pars_ref, par_ref, par_sem)
    walk(low, high, fetch, compute, store, load, lambda: clear_edges(part_ref, cols))
    walk(plain_low, plain_high, pass_in, lambda i, buf: None, pass_out, None, lambda: None)


def lane_mask(low, high):
    lanes = lax.broadcasted_iota(jnp.int32, (8, LANES), 1)
    return (lanes >= low) & (lanes < high)


def pack_kernel(
    spans, codes, space_size, rows, keep_ref, kernel_ref, vectors_ref, bias_ref, up_ref, down_ref,
    small_ref, piece_ref, order_ref, range_ref, owner_ref, used_ref, rows_ref, seen_ref,
):
    part, channels = up_ref.shape
    width = kernel_ref.shape[0]
    count = keep_ref.shape[0]
    rows_ref[...] = jnp.zeros_like(rows_ref)
    rows_ref[0:width, 0:VEC] = kernel_ref[...]
    rows_ref[...] = rows_ref[...].T
    rows_ref[VEC : VEC + 5, 0:width] = vectors_ref[...]
    for at in range(part // width):
        rows_ref[VEC + 5 + at : VEC + 6 + at, 0:width] = bias_ref[0:1, at * width : (at + 1) * width]
    small = rows_ref[0:8, :]
    for group in range(1, ROWS // 8):
        small = small + pltpu.roll(rows_ref[8 * group : 8 * group + 8, :], group * width, 1)
    for device in range(small_ref.shape[0]):
        small_ref[device] = small
    piece_ref[:, 0:channels] = up_ref[...].astype(bf16)
    piece_ref[:, channels : 2 * channels] = down_ref[...].astype(bf16)

    def place(i, at):
        keep = keep_ref[i] > 0
        upper, lower = at
        seen_ref[i] = upper
        order_ref[jnp.where(keep, upper, lower)] = i
        return jnp.where(keep, upper + 1, upper), jnp.where(keep, lower, lower + 1)

    kept = lax.fori_loop(0, count, lambda i, at: at + jnp.where(keep_ref[i] > 0, 1, 0), 0)
    lax.fori_loop(0, count, place, (0, kept))
    seen_ref[count] = kept
    me_space = lax.axis_index("space")
    me = lax.axis_index("dp") * space_size + me_space
    for which, (low, high, plain) in enumerate(spans):
        range_ref[which, 0] = seen_ref[low]
        range_ref[which, 1] = seen_ref[high]
        range_ref[which, 2] = me_space * rows
        range_ref[which, 3] = jnp.maximum(kept, plain)
        range_ref[which, 4] = jnp.maximum(kept, count)
    for at, code in enumerate(codes):
        owner_ref[at] = code if space_size != 4 or len(codes) != 32 else me ^ code
    used_ref[0] = kept


def join_kernel(*refs):
    outs, pieces = refs[-2:], refs[:-2]
    each = len(pieces) // 2
    for out, group in zip(outs, (pieces[:each], pieces[each:])):
        size = group[0].shape[0]
        for at, ref in enumerate(group):
            out[at * size : (at + 1) * size, :] = ref[...]


def unpack_kernel(order_ref, small_ref, par_ref, bias_ref):
    devices = small_ref.shape[0]
    channels = par_ref.shape[1]
    width = channels // devices
    part = bias_ref.shape[1] // devices
    for group in range(ROWS // 8):
        tiles = [jnp.zeros((8, LANES), f32) for _ in range(channels // LANES)]
        for device in range(devices):
            start = device * width
            tile, low = start // LANES, start % LANES
            moved = pltpu.roll(small_ref[device], (start - group * width) % LANES, 1)
            tiles[tile] = jnp.where(lane_mask(low, low + width), moved, tiles[tile])
            if low + width > LANES:
                tiles[tile + 1] = jnp.where(lane_mask(0, low + width - LANES), moved, tiles[tile + 1])
        for tile, value in enumerate(tiles):
            par_ref[8 * group : 8 * group + 8, tile * LANES : (tile + 1) * LANES] = value
    bias_ref[...] = jnp.zeros_like(bias_ref)
    for place in range(devices):
        for at in range(part // width):
            row = VEC + 5 + at
            group, line = row // 8, row % 8
            start = place * part + at * width
            tile, low = start // LANES, start % LANES
            source = small_ref[order_ref[place], line : line + 1, :]
            moved = pltpu.roll(jnp.broadcast_to(source, (8, LANES)), (start - group * width) % LANES, 1)
            for where_, lower, upper in ((tile, low, low + width), (tile + 1, 0, low + width - LANES)):
                if upper > lower:
                    lanes = slice(where_ * LANES, (where_ + 1) * LANES)
                    kept = jnp.broadcast_to(bias_ref[0:1, lanes], (8, LANES))
                    bias_ref[0:1, lanes] = jnp.where(lane_mask(lower, upper), moved, kept)[0:1]


def pack_grads_kernel(order_ref, taps_ref, vec_ref, bias_ref, out_ref, rows_ref):
    devices = out_ref.shape[0]
    channels = taps_ref.shape[1]
    width = channels // devices
    part = bias_ref.shape[1] // devices
    rows_ref[...] = jnp.zeros_like(rows_ref)
    rows_ref[0:VEC, :] = taps_ref[...]
    rows_ref[VEC : VEC + 5, :] = vec_ref[0:5, :]

    def cut(row_slice, source, start, group):
        tile, low = start // LANES, start % LANES
        shift = (group * width - low) % LANES
        moved = pltpu.roll(source(row_slice, tile), shift, 1)
        if low + width > LANES:
            split = group * width + LANES - low
            moved = jnp.where(lane_mask(0, split), moved, pltpu.roll(source(row_slice, tile + 1), shift, 1))
        return moved

    def of_rows(rows, tile):
        return rows_ref[rows, tile * LANES : (tile + 1) * LANES]

    def of_bias(rows, tile):
        return jnp.broadcast_to(bias_ref[0:1, tile * LANES : (tile + 1) * LANES], (8, LANES))

    for device in range(devices):
        total = jnp.zeros((8, LANES), f32)
        for group in range(ROWS // 8):
            moved = cut(slice(8 * group, 8 * group + 8), of_rows, device * width, group)
            total = jnp.where(lane_mask(group * width, (group + 1) * width), moved, total)
        out_ref[device] = total
    for place in range(devices):
        device = order_ref[place]
        for at in range(part // width):
            row = VEC + 5 + at
            group, line = row // 8, row % 8
            moved = cut(None, of_bias, place * part + at * width, group)
            kept = jnp.broadcast_to(out_ref[device, line : line + 1, :], (8, LANES))
            mask = lane_mask(group * width, (group + 1) * width)
            out_ref[device, line : line + 1, :] = jnp.where(mask, moved, kept)[0:1]


def total_kernel(small_ref, *refs):
    count = (len(refs) - 5) // 2
    parts, (own_ref, sums_ref, norm_ref), bufs, (sems, small_buf) = refs[:count], refs[count : count + 3], refs[count + 3 : -2], refs[-2:]
    size = own_ref.shape[0]
    loads = [pltpu.make_async_copy(small_ref, small_buf, sems.at[count])]
    for at, (ref, buf) in enumerate(zip(parts, bufs)):
        loads.append(pltpu.make_async_copy(ref.at[0:size], buf, sems.at[at]))
    for load in loads:
        load.start()
    for load in loads:
        load.wait()
    own = bufs[0][...].astype(f32)
    for buf in bufs[1:]:
        own = own + buf[...].astype(f32)
    own_ref[...] = own
    sums = jnp.sum(small_buf[...], axis=0)
    sums_ref[...] = sums
    local = jnp.sum(own * own) + jnp.sum(sums * sums)
    norm_ref[...] = jnp.full_like(norm_ref, local)


def adam(weight, moment, square, grad, factor, rate):
    scaled = grad * factor
    new_moment = beta_one * moment + (1.0 - beta_one) * scaled
    new_square = beta_two * square + (1.0 - beta_two) * scaled * scaled
    corrected = new_moment / (1.0 - beta_one**STEP)
    spread = jnp.sqrt(new_square / (1.0 - beta_two**STEP))
    return weight - rate * (corrected / (spread + adam_eps) + decay_rate * weight), new_moment, new_square


def adam_kernel(own_ref, sums_ref, norms_ref, *refs):
    states, outs, norm_ref, rows_ref, flip_ref = refs[:15], refs[15:30], refs[30], refs[31], refs[32]
    part, channels = states[6].shape
    width = states[0].shape[0]
    total = jnp.sum(norms_ref[:, 0, 0:1])
    norm = jnp.sqrt(jnp.full((8, LANES), total, f32))
    norm_ref[...] = norm[0:1, 0:1]
    factor = (clip_limit / jnp.maximum(norm, clip_limit))[0:1, 0:1]
    sums = sums_ref[...]
    rows_ref[...] = jnp.zeros_like(rows_ref)
    for group in range(ROWS // 8):
        rows_ref[8 * group : 8 * group + 8, :] = pltpu.roll(sums, (-group * width) % LANES, 1)
    flip_ref[...] = rows_ref[...].T
    grads = [
        flip_ref[0:width, 0:VEC],
        rows_ref[VEC : VEC + 5, 0:width],
        own_ref[:, 0:channels],
        None,
        own_ref[:, channels : 2 * channels],
    ]
    for index, (grad, rate) in enumerate(zip(grads, step_rates)):
        if grad is None:
            continue
        results = adam(*(ref[...] for ref in states[3 * index : 3 * index + 3]), grad, factor, rate)
        for ref, value in zip(outs[3 * index : 3 * index + 3], results):
            ref[...] = value
    for at in range(part // width):
        lanes = slice(at * width, (at + 1) * width)
        row = VEC + 5 + at
        grad = rows_ref[row : row + 1, 0:width]
        results = adam(*(ref[0:1, lanes] for ref in states[9:12]), grad, factor, step_rates[3])
        for ref, value in zip(outs[9:12], results):
            ref[0:1, lanes] = value


def mlp(kept, unit, stat, cots, pieces, bias, pars, dims):
    count, rows, cols, channels = dims
    pixels = rows * cols
    total = count * pixels
    hidden_size = bias.shape[1]
    tall = MLP_SLOTS * pixels

    def last(i, n):
        return jnp.minimum(i, jnp.maximum((n[0] + MLP_SLOTS - 1) // MLP_SLOTS - 1, 0))

    tile_map = lambda i, n: (last(i, n), 0)
    slot_map = lambda i, n: (last(i, n), 0, 0, 0)
    whole = lambda i, n: (0, 0)
    grad = (hidden_size // 2, 2 * channels)
    halo = (count, REACH, cols, channels)
    once = pl.Buffered(1)
    return pl.pallas_call(
        mlp_kernel,
        grid_spec=pltpu.PrefetchScalarGridSpec(
            num_scalar_prefetch=1,
            grid=(-(-count // MLP_SLOTS),),
            in_specs=[
                pl.BlockSpec((tall, channels), tile_map),
                pl.BlockSpec((tall, LANES), tile_map),
                pl.BlockSpec((tall, channels), tile_map),
                pl.BlockSpec(bias.shape, whole),
                pl.BlockSpec(pars.shape, whole),
            ]
            + [pl.BlockSpec(value.shape, whole, pipeline_mode=once) for value in pieces],
            out_specs=[
                pl.BlockSpec((MLP_SLOTS, rows, cols, channels), slot_map),
                pl.BlockSpec((MLP_SLOTS, rows, cols, channels), slot_map),
                pl.BlockSpec((MLP_SLOTS, REACH, cols, channels), slot_map),
                pl.BlockSpec((MLP_SLOTS, REACH, cols, channels), slot_map),
                pl.BlockSpec(grad, whole),
                pl.BlockSpec(grad, whole),
                pl.BlockSpec((1, hidden_size), whole),
                pl.BlockSpec((8, channels), whole),
            ],
            scratch_shapes=[
                pltpu.VMEM((channels, hidden_size), f32),
                pltpu.VMEM((channels, hidden_size), f32),
                pltpu.VMEM((hidden_size, channels), bf16),
                pltpu.VMEM((hidden_size, 2 * channels), bf16),
                pltpu.VMEM((8, hidden_size), f32),
                pltpu.VMEM((40, channels), f32),
            ],
        ),
        out_shape=[
            shape(dims, bf16),
            shape(dims, bf16),
            shape(halo, bf16),
            shape(halo, bf16),
            shape(grad, bf16),
            shape(grad, bf16),
            shape((1, hidden_size), f32),
            shape((8, channels), f32),
        ],
        compiler_params=pltpu.CompilerParams(dimension_semantics=("arbitrary",), vmem_limit_bytes=VMEM_MIB * MIB),
        name="mlp",
    )(kept, unit.reshape(total, channels), stat.reshape(total, LANES), cots.reshape(total, channels), bias, pars, *pieces)


IN_PLACE = pl.BlockSpec(memory_space=pltpu.HBM)
SCALARS = pl.BlockSpec(memory_space=pltpu.SMEM)
LOADED = pl.BlockSpec(memory_space=pltpu.VMEM)


def call(kernel, in_specs, out_specs, out_shape, scratch, name, aliases=None):
    return pl.pallas_call(
        kernel,
        in_specs=in_specs,
        out_specs=out_specs,
        out_shape=out_shape,
        scratch_shapes=scratch,
        input_output_aliases=aliases or {},
        compiler_params=pltpu.CompilerParams(vmem_limit_bytes=VMEM_MIB * MIB),
        name=name,
    )


def shape(dims, kind):
    return jax.ShapeDtypeStruct(dims, kind)


def window(rows, cols, channels):
    return pltpu.VMEM((DEPTH, rows + 2 * REACH, cols, channels), bf16)


def padded(rows, cols, channels):
    return pltpu.VMEM((channels // LANES, rows + 2 * REACH, cols + 2 * EDGE, LANES), f32)


def paired(rows, cols, channels):
    return pltpu.VMEM((channels // LANES, rows // 2 + 2 * REACH, 2 * cols, LANES), bf16)


def conv_norm(which, first, order, ranges, sides, above, own, below, cot, pars, earlier):
    count, rows, cols, channels = own.shape
    pixels = rows * cols
    outs = [
        shape((count, pixels, channels), f32),
        shape((count, pixels, LANES), f32),
        shape((count, rows, cols, channels), bf16),
    ]
    run = call(
        functools.partial(conv_norm_kernel, which, first),
        [SCALARS] * 3 + [IN_PLACE] * (5 + len(earlier)),
        [IN_PLACE] * 3,
        outs,
        [
            window(rows, cols, channels),
            pltpu.VMEM((DEPTH, pixels, channels), f32),
            pltpu.VMEM((DEPTH, pixels, LANES), f32),
            pltpu.VMEM((DEPTH, rows, cols, channels), bf16),
            padded(rows, cols, channels),
            pltpu.VMEM((pixels, channels), f32),
            pltpu.VMEM(pars.shape, f32),
            pltpu.SemaphoreType.DMA((DEPTH, 4)),
            pltpu.SemaphoreType.DMA((DEPTH, 3)),
            pltpu.SemaphoreType.DMA,
        ],
        "conv_norm",
        {8 + at: at for at in range(len(earlier))},
    )
    return run(order, ranges, sides, above, own, below, cot, pars, *earlier)


def taps_grad(which, order, ranges, sides, halos, own, gc):
    count, rows, cols, channels = own.shape
    pixels = rows * cols
    run = call(
        functools.partial(taps_grad_kernel, which, halos[0].shape[0]),
        [SCALARS] * 3 + [IN_PLACE] * 6,
        LOADED,
        shape((TAPS * TAPS, channels), f32),
        [
            window(rows, cols, channels),
            pltpu.VMEM((DEPTH, rows, cols, channels), bf16),
            paired(rows, cols, channels),
            pltpu.VMEM((TAPS * TAPS, 8, channels), f32),
            pltpu.VMEM((channels // LANES, rows, cols + 2 * EDGE, LANES), f32),
            pltpu.SemaphoreType.DMA((DEPTH, 4)),
        ],
        "taps_grad",
    )
    return run(order, ranges, sides, halos[0], own, halos[1], halos[2], halos[3], gc.reshape(own.shape))


def finish(which, order, ranges, sides, above, gc, below, branch, images, cot, pars, earlier):
    count, rows, cols, channels = images.shape
    block = (DEPTH, rows, cols, channels)
    run = call(
        functools.partial(finish_kernel, which),
        [SCALARS] * 3 + [IN_PLACE] * (7 + len(earlier)),
        [IN_PLACE] * 2,
        [shape(images.shape, bf16)] * 2,
        [
            window(rows, cols, channels),
            pltpu.VMEM(block, bf16),
            pltpu.VMEM(block, bf16),
            pltpu.VMEM(block, bf16),
            pltpu.VMEM(block, bf16),
            pltpu.VMEM(block, bf16),
            paired(rows, cols, channels),
            pltpu.VMEM((TAPS, rows, cols + 2 * EDGE, LANES), f32),
            pltpu.VMEM((rows, cols, channels), f32),
            pltpu.VMEM(pars.shape, f32),
            pltpu.SemaphoreType.DMA((DEPTH, 6)),
            pltpu.SemaphoreType.DMA((DEPTH, 2)),
            pltpu.SemaphoreType.DMA,
        ],
        "finish",
        {10 + at: at for at in range(len(earlier))},
    )
    maps = (value.reshape(images.shape) for value in (gc, branch))
    gc, branch = maps
    return run(order, ranges, sides, above, gc, below, branch, images, cot, pars, *earlier)


def pack(spans, codes, space_size, rows, keep, kernel, vectors, bias, up, down):
    channels, part = up.shape
    return call(
        functools.partial(pack_kernel, spans, codes, space_size, rows),
        [SCALARS] + [LOADED] * 5,
        [LOADED] * 2 + [SCALARS] * 4,
        [
            shape((len(codes), 8, LANES), f32),
            shape((part, 2 * channels), bf16),
            shape(keep.shape, jnp.int32),
            shape((len(spans), 5), jnp.int32),
            shape((len(codes),), jnp.int32),
            shape((1,), jnp.int32),
        ],
        [pltpu.VMEM((LANES, LANES), f32), pltpu.SMEM((keep.shape[0] + 1,), jnp.int32)],
        "pack",
    )(keep, kernel.T, vectors, bias.reshape(1, -1), up.T, down)


def join_two(*pieces):
    size, width = pieces[0].shape
    each = len(pieces) // 2
    out = shape((each * size, width), pieces[0].dtype)
    return call(join_kernel, [LOADED] * len(pieces), [LOADED] * 2, [out, out], [], "join")(*pieces)


def unpack(order, small, channels, hidden_size):
    return call(
        unpack_kernel,
        [SCALARS, LOADED],
        [LOADED] * 2,
        [shape((ROWS, channels), f32), shape((1, hidden_size), f32)],
        [],
        "unpack",
    )(order, small)


def pack_grads(order, taps, vec, bias):
    return call(
        pack_grads_kernel,
        [SCALARS] + [LOADED] * 3,
        LOADED,
        shape((order.shape[0], 8, LANES), f32),
        [pltpu.VMEM((ROWS, taps.shape[1]), f32)],
        "pack_grads",
    )(order, taps, vec, bias)


def add_up(small, parts, size):
    devices = small.shape[0]
    width = parts[0].shape[1]
    return call(
        total_kernel,
        [IN_PLACE] * (1 + len(parts)),
        [LOADED] * 3,
        [shape((size, width), f32), shape((8, LANES), f32), shape((devices, 8, LANES), f32)],
        [pltpu.VMEM((size, width), value.dtype) for value in parts]
        + [pltpu.SemaphoreType.DMA((len(parts) + 1,)), pltpu.VMEM(small.shape, f32)],
        "add_up",
    )(small, *parts)


def update(own, sums, norms, states):
    def view(at, value):
        if at // 3 in (0, 2):
            return value.T
        return value.reshape(1, -1) if at // 3 == 3 else value

    def unview(at, value):
        return value.reshape(-1) if at // 3 == 3 else view(at, value)

    views = [view(at, value) for at, value in enumerate(states)]
    results = call(
        adam_kernel,
        [LOADED] * 18,
        [LOADED] * 16,
        [shape(value.shape, f32) for value in views] + [shape((1, 1), f32)],
        [pltpu.VMEM((LANES, LANES), f32), pltpu.VMEM((LANES, LANES), f32)],
        "update",
    )(own, sums, norms, *views)
    return [unview(at, value) for at, value in enumerate(results[:15])], results[15].reshape(())


def pass_rows(top, low, places):
    above = lax.ppermute(low, "space", [(i, i + 1) for i in range(places - 1)])
    below = lax.ppermute(top, "space", [(i + 1, i) for i in range(places - 1)])
    return above, below


def flip_perm(size, bit):
    return [(i, i ^ bit) for i in range(size)]


def swap(value, bits):
    axis, bit, size = ("dp", bits[0], 8) if bits[0] else ("space", bits[1], 4)
    return lax.ppermute(value, axis, flip_perm(size, bit))


X, Y, CORE = (1, 0), (0, 2), (0, 1)
Z1, Z2, Z3 = (2, 0), (4, 0), (6, 0)


def cube_order():
    first = [0, 2 * 4]
    last = [4 * 4, 6 * 4]
    first = first + [v ^ 4 for v in first]
    last = last + [v ^ 2 for v in last]
    first = first + [v ^ 2 for v in first]
    last = last + [v ^ 4 for v in last]
    near = first + last
    return near + [v ^ 1 for v in near]


def after(value, *others):
    return lax.optimization_barrier((value,) + others)[0]


def behind(values, token):
    return lax.optimization_barrier((*values, token))[:-1]


def total_of(*pieces):
    total = pieces[0].astype(f32)
    for piece in pieces[1:]:
        total = total + piece.astype(f32)
    return total.astype(bf16)


def exchange(value):
    return lax.all_to_all(value, AXES, 0, 0, tiled=True)


def body(dp_size, space_size, images, cotangent, image_sides, keep_flags, *states):
    devices = dp_size * space_size
    count, rows, cols, channels = images.shape
    depth_kernel, block_vectors, up_weight, up_bias, down_weight = states[0::3]
    part = up_weight.shape[1]
    hidden_size = part * devices
    cube = dp_size == 8 and space_size == 4

    cut, mid = 3 * count // 8, 11 * count // 16
    spans = ((0, cut, count), (cut, mid, count), (mid, count, count), (mid, count, 0), (0, count, count), (0, count, 0))
    codes = tuple(cube_order()) if cube else tuple(range(devices))
    small, piece, order, ranges, owners, kept = pack(
        spans, codes, space_size, rows, keep_flags, depth_kernel, block_vectors, up_bias, up_weight, down_weight
    )
    small_all = exchange(small)
    piece, maps = after((piece, images), small) if cube else (piece, images)
    halos = pass_rows(maps[:cut, :REACH], maps[:cut, -REACH:], space_size)
    pars, bias = unpack(owners, small_all, channels, hidden_size)

    def conv_part(which, earlier, *waits):
        above, below = halos[:2] if which == 0 else halos[2:]
        first = 0 if which == 0 else cut
        return conv_norm(
            which, first, after(order, *waits), ranges, image_sides, above, images, below, cotangent, pars, earlier
        )

    later = images
    if cube:
        first, last = join_two(*behind((piece, *(swap(piece, step) for step in (Z1, Z2, Z3))), small_all))
        later = after(images, first, last, *halos)
        got = (swap(first, X), swap(last, Y))
    halos += pass_rows(later[cut:, :REACH], later[cut:, -REACH:], space_size)
    if cube:
        made = conv_part(0, (), first, last)
        got = behind(got, made[1])
        first, last = join_two(first, got[0], last, got[1])
        got = (swap(first, Y), swap(last, X))
        made = conv_part(1, made, first, last)
        got = behind(got, made[1])
        pieces = [first, got[0], last, got[1]]
        far = [swap(value, CORE) for value in pieces]
        unit, stat, cots = conv_part(2, made, *pieces)
        pieces = pieces + list(behind(far, stat))
    else:
        pieces = [lax.all_gather(piece, AXES, axis=0, tiled=True)]
        made = conv_part(0, ())
        made = conv_part(1, made)
        unit, stat, cots = conv_part(2, made)
    branch, gc, top, low, grad_near, grad_far, bias_sum, vec_sum = mlp(
        kept, unit, stat, cots, pieces, bias, pars, images.shape
    )

    def taps_part(which, *waits):
        return taps_grad(which, after(order, *waits), ranges, image_sides, halos, images, gc)

    def finish_part(which, earlier, *waits):
        return finish(
            which, after(order, *waits), ranges, image_sides,
            gc_above, gc, gc_below, branch, images, cotangent, pars, earlier,
        )

    if cube:
        core = swap(grad_far, CORE)
        half = grad_near.shape[0] // 2
        quarter, eighth = half // 2, half // 4

        def kept_sum(which, low, high, *got):
            lines = slice(which * half + low, which * half + high)
            return total_of(grad_near[lines], core[lines], *(value[low:high] for value in got))

        gc_above, gc_below = pass_rows(top, low, space_size)
        send = [kept_sum(0, quarter, half), kept_sum(1, quarter, half)]
        two_a, two_b = swap(send[0], Y), swap(send[1], X)
        taps = taps_part(4, *send)
        two_a, two_b = behind((two_a, two_b), taps)
        got = exchange(pack_grads(owners, taps, vec_sum, bias_sum))
        send = [kept_sum(0, eighth, quarter, two_a), kept_sum(1, eighth, quarter, two_b)]
        three_a, three_b = swap(send[0], X), swap(send[1], Y)
        made = finish_part(0, (), *send)
        three_a, three_b, got = behind((three_a, three_b, got), made[0])
        send = [
            kept_sum(0, part, 2 * part, two_a, three_a),
            kept_sum(1, 0, part, two_b, three_b),
            kept_sum(1, part, 2 * part, two_b, three_b),
        ]
        z_got = [swap(value, step) for value, step in zip(send, (Z1, Z2, Z3))]
        made = finish_part(1, made, *send)
        z_got = behind(z_got, made[0])
        own, sums, norm = add_up(got, [grad_near, core, two_a, three_a, *z_got], part)
        norms = exchange(norm)
        out_images, grad_images = finish_part(3, made, norm)
        norms, grad_images = lax.optimization_barrier((norms, grad_images))
    else:
        gc_above, gc_below = pass_rows(top, low, space_size)
        grads = jnp.concatenate([grad_near, grad_far]).astype(f32)
        parts = [lax.psum_scatter(grads, AXES, scatter_dimension=0, tiled=True)]
        got = exchange(pack_grads(owners, taps_part(4), vec_sum, bias_sum))
        own, sums, norm = add_up(got, parts, part)
        norms = exchange(norm)
        out_images, grad_images = finish_part(5, ())
    results, grad_norm = update(own, sums, norms, states)
    return (out_images, grad_images, *results, grad_norm)


def solution(mesh):
    lanes = P(None, AXES)
    flat = P(AXES)
    tall = P(AXES, None)
    maps = P("dp", "space", None, None)
    in_specs = (maps, maps, P("dp"), P("dp")) + (lanes,) * 9 + (flat,) * 3 + (tall,) * 3
    out_specs = (maps, maps) + (lanes,) * 9 + (flat,) * 3 + (tall,) * 3 + (P(),)
    run = functools.partial(body, mesh.shape["dp"], mesh.shape["space"])
    return jax.shard_map(run, mesh=mesh, in_specs=in_specs, out_specs=out_specs, check_vma=False)
```

```python
import functools

import jax
import jax.numpy as jnp
from jax import lax
from jax.experimental import pallas as pl
from jax.experimental.pallas import tpu as pltpu
from jax.sharding import PartitionSpec as P

STEP = 5

keep_scale = 4.0 / 3.0
norm_eps = 1e-06
clip_limit = 1.0
beta_one = 0.9
beta_two = 0.999
adam_eps = 1e-08
decay_rate = 0.05
step_rates = (0.15, 0.5, 0.05, 0.2, 0.025)
inv_root_two = 0.7071067811865476
inv_root_tau = 0.3989422804014327
f32 = jnp.float32
bf16 = jnp.bfloat16
AXES = ("dp", "space")
LANES = 128
REACH = 3
TAPS = 7
VEC = TAPS * TAPS
ROWS = 64
NARROW = 16
EDGE = 8
MLP_SLOTS = 4
VMEM_MIB = 64
DEPTH = 5
AHEAD = DEPTH - 2
MLP_COLS = 768
MIB = 1 << 20


def dot_nn(a, b):
    return lax.dot_general(a, b, (((1,), (0,)), ((), ())), preferred_element_type=f32)


def dot_nt(a, b):
    return lax.dot_general(a, b, (((1,), (1,)), ((), ())), preferred_element_type=f32)


def fold(value):
    rows, channels = value.shape
    return jnp.sum(value.reshape(rows // 8, 8, channels), axis=0)


def mlp_kernel(
    at, table_ref, unit_ref, stat_ref, cot_ref, bias_ref, par_ref, *refs
):
    step = pl.program_id(0)
    rows, channels = unit_ref.shape
    pieces = refs[:-14]
    (branch_ref, gc_ref, top_ref, low_ref, grad_near_ref, grad_far_ref, bsum_ref, vsum_ref,
     up_acc, down_acc, scaled_ref, both_ref, bias_acc, vec_acc) = refs[-14:]
    hidden_size = both_ref.shape[0]
    half = hidden_size // 2
    pixels = rows // MLP_SLOTS
    used = table_ref[at] * pixels
    gamma = par_ref[VEC + 4 : VEC + 5, :] * keep_scale

    @pl.when(step == 0)
    def _():
        up_acc[...] = jnp.zeros_like(up_acc)
        down_acc[...] = jnp.zeros_like(down_acc)
        bias_acc[...] = jnp.zeros_like(bias_acc)
        vec_acc[...] = jnp.zeros_like(vec_acc)
        at = 0
        for ref in pieces:
            size = ref.shape[0]
            both_ref[at : at + size, :] = ref[...]
            down = ref[:, channels : 2 * channels].astype(f32)
            scaled_ref[at : at + size, :] = (down * gamma).astype(bf16)
            at += size

    @pl.when(step * rows < used)
    def _():
        inside = lax.broadcasted_iota(jnp.int32, (rows, channels), 0) < used - step * rows
        unit = jnp.where(inside, unit_ref[...], 0.0)
        valid = stat_ref[:, LANES // 2 : LANES // 2 + 1]
        cotm32 = jnp.where(inside, cot_ref[...].astype(f32) * valid, 0.0)
        cotm = cotm32.astype(bf16)
        normed = (unit * par_ref[VEC + 1 : VEC + 2, :] + par_ref[VEC + 2 : VEC + 3, :]).astype(bf16)
        normed_t = normed.T
        cotm_t = cotm.T
        branch = None
        grad_normed = None
        for start in range(0, hidden_size, MLP_COLS):
            cols = slice(start, start + MLP_COLS)
            up = both_ref[cols, 0:channels]
            down = both_ref[cols, channels : 2 * channels]
            hidden = dot_nt(normed, up) + bias_ref[0:1, cols]
            cdf = 0.5 + 0.5 * lax.erf(hidden * inv_root_two)
            active = (hidden * cdf).astype(bf16)
            slope = cdf + hidden * (inv_root_tau * jnp.exp(-0.5 * hidden * hidden))
            part_branch = dot_nn(active, down)
            branch = part_branch if branch is None else branch + part_branch
            grad_hidden32 = dot_nt(cotm, scaled_ref[cols, :]) * slope
            bias_acc[:, cols] += fold(grad_hidden32)
            grad_hidden = grad_hidden32.astype(bf16)
            part_grad = dot_nn(grad_hidden, up)
            grad_normed = part_grad if grad_normed is None else grad_normed + part_grad
            up_acc[:, cols] += dot_nn(normed_t, grad_hidden)
            down_acc[:, cols] += dot_nn(cotm_t, active)
        branch = branch + par_ref[VEC + 3 : VEC + 4, :]
        branch_ref[...] = branch.astype(bf16).reshape(branch_ref.shape)
        inv_std = stat_ref[:, 0:1]
        scaled = grad_normed * par_ref[VEC + 1 : VEC + 2, :]
        mean_a = jnp.mean(scaled, axis=-1, keepdims=True)
        mean_b = jnp.mean(scaled * unit, axis=-1, keepdims=True)
        grad_conv = inv_std * (scaled - mean_a - unit * mean_b)
        grad_conv = jnp.where(inside, grad_conv, 0.0)
        maps = grad_conv.reshape(gc_ref.shape).astype(bf16)
        gc_ref[...] = maps
        top_ref[...] = maps[:, :REACH]
        low_ref[...] = maps[:, -REACH:]
        vec_acc[0:8, :] += fold(grad_conv)
        vec_acc[8:16, :] += fold(grad_normed * unit)
        vec_acc[16:24, :] += fold(grad_normed)
        vec_acc[24:32, :] += fold(cotm32)
        vec_acc[32:40, :] += fold(cotm32 * branch)

    @pl.when(step == pl.num_programs(0) - 1)
    def _():
        for start in range(0, hidden_size, MLP_COLS):
            cols = slice(start, start + MLP_COLS)
            ref = grad_near_ref if start < half else grad_far_ref
            part = slice(start % half, start % half + MLP_COLS)
            ref[part, 0:channels] = up_acc[:, cols].T.astype(bf16)
            ref[part, channels : 2 * channels] = (down_acc[:, cols].T * gamma).astype(bf16)
        bsum_ref[...] = jnp.sum(bias_acc[...], axis=0, keepdims=True)
        vsum_ref[...] = jnp.zeros_like(vsum_ref)
        for row in range(5):
            total = jnp.sum(vec_acc[8 * row : 8 * row + 8, :], axis=0, keepdims=True)
            if row == 3:
                total = total * gamma
            if row == 4:
                total = total * keep_scale
            vsum_ref[row : row + 1, :] = total


def walk(low, high, fetch, compute, store, load, prepare):
    def begin(i, carry):
        for copy in fetch(i, lax.rem(i - low, DEPTH)):
            copy.start()
        return carry

    def end(i, carry):
        for copy in store(i, lax.rem(i - low, DEPTH)):
            copy.wait()
        return carry

    if load is not None:
        load.start()
    lax.fori_loop(low, jnp.minimum(high, low + AHEAD), begin, 0)
    prepare()
    if load is not None:
        load.wait()

    def step(i, carry):
        buf = lax.rem(i - low, DEPTH)
        for copy in fetch(i, buf):
            copy.wait()

        @pl.when(i - low >= 2)
        def _():
            end(i - 2, 0)

        @pl.when(i + AHEAD < high)
        def _():
            begin(i + AHEAD, 0)

        compute(i, buf)
        for copy in store(i, buf):
            copy.start()
        return carry

    lax.fori_loop(low, high, step, 0)
    lax.fori_loop(jnp.maximum(low, high - 2), high, end, 0)


def copies(pairs, sems, buf):
    return [pltpu.make_async_copy(src, dst, sems.at[buf, at]) for at, (src, dst) in enumerate(pairs)]


def clear_edges(pad_ref, cols):
    tiles, rows, width, lanes = pad_ref.shape
    for tile in range(tiles):
        for row in range(rows):
            pad_ref[tile, row, 0:EDGE, :] = jnp.zeros((EDGE, lanes), f32)
            pad_ref[tile, row, EDGE + cols : width, :] = jnp.zeros((width - EDGE - cols, lanes), f32)


def inside_cols(cols, row, side):
    reach = jnp.where(row < side, side, 0)
    return lax.broadcasted_iota(jnp.int32, (cols, LANES), 0) < reach


def fill_rows(pad_ref, win_ref, width, side, first_row):
    rows, cols, channels = win_ref.shape
    for row in range(rows):
        inside = inside_cols(width, first_row + row, side)
        for tile in range(channels // LANES):
            line = win_ref[row, 0:width, tile * LANES : (tile + 1) * LANES].astype(f32)
            pad_ref[tile, row, EDGE : EDGE + width, :] = jnp.where(inside, line, 0.0)
            if width < cols:
                pad_ref[tile, row, EDGE + width : EDGE + cols, :] = jnp.zeros((cols - width, LANES), f32)


def by_width(cols, side, work):
    if NARROW < cols:
        pl.when(side <= NARROW)(lambda: work(NARROW))
        pl.when(side > NARROW)(lambda: work(cols))
    else:
        work(cols)


def conv_tile(pad_ref, tile, par_ref, out_rows, cols):
    lanes = slice(tile * LANES, (tile + 1) * LANES)
    sums = [None] * out_rows
    for col_off in range(TAPS):
        weights = []
        for row_off in range(TAPS):
            index = row_off * TAPS + col_off
            weights.append(par_ref[index : index + 1, lanes])
        for row in range(out_rows + 2 * REACH):
            start = EDGE - REACH + col_off
            line = pad_ref[tile, row, start : start + cols, :]
            for row_off in range(TAPS):
                out = row - row_off
                if 0 <= out < out_rows:
                    term = weights[row_off] * line
                    sums[out] = term if sums[out] is None else sums[out] + term
    return sums


def conv_norm_kernel(
    which, first, table_ref, above_ref, own_ref, below_ref, cot_ref, pars_ref, *rest
):
    (unit_ref, stat_ref, cots_ref, win_ref, unit_buf, stat_buf, cot_buf, pad_ref, conv_ref, par_ref,
     in_sems, out_sems, par_sem) = rest[-13:]
    count, rows, cols, channels = own_ref.shape
    at = 2 * count + 5 * which
    low, high, start = table_ref[at], table_ref[at + 1], table_ref[at + 2]

    def fetch(i, buf):
        image = table_ref[i]
        win = win_ref.at[buf]
        return copies(
            [
                (above_ref.at[image - first], win.at[0:REACH]),
                (own_ref.at[image], win.at[REACH : REACH + rows]),
                (below_ref.at[image - first], win.at[REACH + rows : 2 * REACH + rows]),
                (cot_ref.at[image], cot_buf.at[buf]),
            ],
            in_sems,
            buf,
        )

    def store(i, buf):
        pairs = [(unit_buf, unit_ref), (stat_buf, stat_ref), (cot_buf, cots_ref)]
        return copies([(mine.at[buf], ref.at[i]) for mine, ref in pairs], out_sems, buf)

    def compute(i, buf):
        side = table_ref[count + i]

        def convolve(width):
            fill_rows(pad_ref, win_ref.at[buf], width, side, start - REACH)
            for tile in range(channels // LANES):
                lanes = slice(tile * LANES, (tile + 1) * LANES)
                sums = conv_tile(pad_ref, tile, par_ref, rows, width)
                for row in range(rows):
                    begin, end = row * cols, (row + 1) * cols
                    conv_ref[begin : begin + width, lanes] = sums[row] + par_ref[VEC : VEC + 1, lanes]
                    if width < cols:
                        conv_ref[begin + width : end, lanes] = jnp.zeros((cols - width, LANES), f32)

        by_width(cols, side, convolve)

        @pl.when(i < high)
        def _():
            conv = conv_ref[...]
            mean = jnp.mean(conv, axis=-1, keepdims=True)
            centred = conv - mean
            var = jnp.mean(centred * centred, axis=-1, keepdims=True)
            inv_std = lax.rsqrt(var + norm_eps)
            unit_buf[buf] = centred * inv_std
            left = lax.broadcasted_iota(jnp.int32, (cols, LANES), 1) < LANES // 2
            for row in range(rows):
                inside = inside_cols(cols, start + row, side)
                spread_inv = jnp.broadcast_to(inv_std[row * cols : (row + 1) * cols], (cols, LANES))
                lines = slice(row * cols, (row + 1) * cols)
                stat_buf[buf, lines, :] = jnp.where(left, spread_inv, jnp.where(inside, 1.0, 0.0))

    load = pltpu.make_async_copy(pars_ref, par_ref, par_sem)
    walk(low, high, fetch, compute, store, load, lambda: clear_edges(pad_ref, cols))


def fill_pairs(pair_ref, win_ref, width, side=None, first_row=None):
    tiles, pairs = pair_ref.shape[:2]
    rows = win_ref.shape[0]
    apart = rows - pairs
    for row in range(rows):
        if side is not None:
            mask = jnp.where(inside_cols(width, first_row + row, side), 1.0, 0.0).astype(bf16)
        for tile in range(tiles):
            line = win_ref[row, 0:width, tile * LANES : (tile + 1) * LANES]
            if side is not None:
                line = line * mask
            if row < pairs:
                pair_ref[tile, row, 0:width, :] = line
            if row >= apart:
                pair_ref[tile, row - apart, width : 2 * width, :] = line


def taps_grad_kernel(
    which, split, table_ref, above_ref, own_ref, below_ref, far_above_ref, far_below_ref, gc_ref,
    owner_ref, vec_ref, bias_ref, out_ref, win_ref, gc_buf, pair_ref, acc_ref, grad_ref, rows_ref, in_sems,
):
    count, rows, cols, channels = own_ref.shape
    half = rows // 2
    at = 2 * count + 5 * which
    low, high, start = table_ref[at], table_ref[at + 1], table_ref[at + 2]

    def halo_copies(above, below, image, buf):
        win = win_ref.at[buf]
        return [
            pltpu.make_async_copy(above.at[image], win.at[0:REACH], in_sems.at[buf, 2]),
            pltpu.make_async_copy(below.at[image], win.at[REACH + rows : 2 * REACH + rows], in_sems.at[buf, 3]),
        ]

    class Halo:
        def __init__(self, image, buf):
            self.image, self.buf = image, buf

        def start(self):
            @pl.when(self.image < split)
            def _():
                for copy in halo_copies(above_ref, below_ref, self.image, self.buf):
                    copy.start()

            @pl.when(self.image >= split)
            def _():
                for copy in halo_copies(far_above_ref, far_below_ref, self.image - split, self.buf):
                    copy.start()

        def wait(self):
            for copy in halo_copies(above_ref, below_ref, 0, self.buf):
                copy.wait()

    def fetch(i, buf):
        image = table_ref[i]
        win = win_ref.at[buf]
        near = copies([(own_ref.at[image], win.at[REACH : REACH + rows]), (gc_ref.at[i], gc_buf.at[buf])], in_sems, buf)
        return near + [Halo(image, buf)]

    def compute(i, buf):
        side = table_ref[count + i]

        def multiply(width):
            fill_pairs(pair_ref, win_ref.at[buf], width, side, start - REACH)
            for row in range(rows):
                for tile in range(channels // LANES):
                    line = gc_buf[buf, row, :, tile * LANES : (tile + 1) * LANES]
                    grad_ref[tile, row, EDGE : EDGE + cols, :] = line.astype(f32)
            for tile in range(channels // LANES):
                lanes = slice(tile * LANES, (tile + 1) * LANES)
                for col_off in range(TAPS):
                    at = EDGE + REACH - col_off
                    grads = []
                    for row in range(half):
                        two = [grad_ref[tile, r, at : at + width, :] for r in (row, row + half)]
                        grads.append(jnp.concatenate(two, axis=0).astype(bf16))
                    for row_off in range(TAPS):
                        total = grads[0] * pair_ref[tile, row_off, 0 : 2 * width]
                        for row in range(1, half):
                            total = total + grads[row] * pair_ref[tile, row_off + row, 0 : 2 * width]
                        short = total[0:16]
                        for begin in range(16, 2 * width, 16):
                            short = short + total[begin : begin + 16]
                        acc_ref[row_off * TAPS + col_off, :, lanes] += fold(short.astype(f32))

        by_width(cols, side, multiply)

    def prepare():
        acc_ref[...] = jnp.zeros_like(acc_ref)
        clear_edges(grad_ref, cols)

    walk(low, high, fetch, compute, lambda i, buf: [], None, prepare)
    pack_grads(owner_ref, jnp.sum(acc_ref[...], axis=1), vec_ref, bias_ref, out_ref, rows_ref)


def finish_kernel(
    which, table_ref, above_ref, gc_ref, below_ref, branch_ref, image_ref, cot_ref, pars_ref, *rest
):
    (out_ref, gim_ref, win_ref, branch_buf, image_buf, cot_buf, out_buf, gim_buf, pair_ref, part_ref, sum_ref, par_ref,
     in_sems, out_sems, par_sem) = rest[-15:]
    count, rows, cols, channels = image_ref.shape
    half = rows // 2
    at = 2 * count + 5 * which
    low, high, start = table_ref[at], table_ref[at + 1], table_ref[at + 2]
    plain_low, plain_high = table_ref[at + 3], table_ref[at + 4]

    def fetch(i, buf):
        image = table_ref[i]
        win = win_ref.at[buf]
        return copies(
            [
                (above_ref.at[i], win.at[0:REACH]),
                (gc_ref.at[i], win.at[REACH : REACH + rows]),
                (below_ref.at[i], win.at[REACH + rows : 2 * REACH + rows]),
                (branch_ref.at[i], branch_buf.at[buf]),
                (image_ref.at[image], image_buf.at[buf]),
                (cot_ref.at[image], cot_buf.at[buf]),
            ],
            in_sems,
            buf,
        )

    def store(i, buf):
        image = table_ref[i]
        return copies([(out_buf.at[buf], out_ref.at[image]), (gim_buf.at[buf], gim_ref.at[image])], out_sems, buf)

    def pass_in(i, buf):
        image = table_ref[i]
        return copies([(image_ref.at[image], image_buf.at[buf]), (cot_ref.at[image], cot_buf.at[buf])], in_sems, buf)

    def pass_out(i, buf):
        image = table_ref[i]
        return copies([(image_buf.at[buf], out_ref.at[image]), (cot_buf.at[buf], gim_ref.at[image])], out_sems, buf)

    def compute(i, buf):
        side = table_ref[count + i]

        def convolve(width):
            fill_pairs(pair_ref, win_ref.at[buf], width)
            for tile in range(channels // LANES):
                lanes = slice(tile * LANES, (tile + 1) * LANES)
                for col_off in range(TAPS):
                    at = EDGE
                    weights = []
                    for row_off in range(TAPS):
                        index = TAPS * TAPS - 1 - row_off * TAPS - col_off
                        weights.append(par_ref[index : index + 1, lanes].astype(bf16))
                    for row in range(half):
                        total = weights[0] * pair_ref[tile, row, 0 : 2 * width]
                        for row_off in range(1, TAPS):
                            total = total + weights[row_off] * pair_ref[tile, row + row_off, 0 : 2 * width]
                        total = total.astype(f32)
                        for line, begin in ((row, 0), (row + half, width)):
                            part_ref[col_off, line, at : at + width, :] = total[begin : begin + width]
                            if width < cols:
                                part_ref[col_off, line, at + width : at + cols, :] = jnp.zeros((cols - width, LANES), f32)
                for row in range(rows):
                    total = part_ref[REACH, row, EDGE : EDGE + width, :]
                    for col_off in range(TAPS):
                        if col_off != REACH:
                            at = EDGE - REACH + col_off
                            total = total + part_ref[col_off, row, at : at + width, :]
                    sum_ref[row, 0:width, lanes] = total

        by_width(cols, side, convolve)

        @pl.when(i < high)
        def _():
            scale = par_ref[VEC + 4 : VEC + 5, :] * keep_scale
            for row in range(rows):
                inside = inside_cols(cols, start + row, side)
                for tile in range(channels // LANES):
                    lanes = slice(tile * LANES, (tile + 1) * LANES)
                    grad = cot_buf[buf, row, :, lanes].astype(f32) + jnp.where(inside, sum_ref[row, :, lanes], 0.0)
                    gim_buf[buf, row, :, lanes] = grad.astype(bf16)
                    extra = branch_buf[buf, row, :, lanes].astype(f32) * scale[:, lanes]
                    out = image_buf[buf, row, :, lanes].astype(f32) + jnp.where(inside, extra, 0.0)
                    out_buf[buf, row, :, lanes] = out.astype(bf16)

    load = pltpu.make_async_copy(pars_ref, par_ref, par_sem)
    walk(low, high, fetch, compute, store, load, lambda: clear_edges(part_ref, cols))
    walk(plain_low, plain_high, pass_in, lambda i, buf: None, pass_out, None, lambda: None)


def lane_mask(low, high):
    lanes = lax.broadcasted_iota(jnp.int32, (8, LANES), 1)
    return (lanes >= low) & (lanes < high)


def pack_kernel(
    spans, codes, space_size, rows, keep_ref, side_ref, kernel_ref, vectors_ref, bias_ref, up_ref, down_ref,
    small_ref, piece_ref, table_ref, owner_ref, rows_ref, seen_ref,
):
    part, channels = up_ref.shape
    width = kernel_ref.shape[0]
    count = keep_ref.shape[0]
    rows_ref[...] = jnp.zeros_like(rows_ref)
    rows_ref[0:width, 0:VEC] = kernel_ref[...]
    rows_ref[...] = rows_ref[...].T
    rows_ref[VEC : VEC + 5, 0:width] = vectors_ref[...]
    for at in range(part // width):
        rows_ref[VEC + 5 + at : VEC + 6 + at, 0:width] = bias_ref[0:1, at * width : (at + 1) * width]
    small = rows_ref[0:8, :]
    for group in range(1, ROWS // 8):
        small = small + pltpu.roll(rows_ref[8 * group : 8 * group + 8, :], group * width, 1)
    for device in range(small_ref.shape[0]):
        small_ref[device] = small
    piece_ref[:, 0:channels] = up_ref[...].astype(bf16)
    piece_ref[:, channels : 2 * channels] = down_ref[...].astype(bf16)

    def place(i, at):
        keep = keep_ref[i] > 0
        upper, lower = at
        seen_ref[i] = upper
        spot = jnp.where(keep, upper, lower)
        table_ref[spot] = i
        table_ref[count + spot] = side_ref[i]
        return jnp.where(keep, upper + 1, upper), jnp.where(keep, lower, lower + 1)

    kept = lax.fori_loop(0, count, lambda i, at: at + jnp.where(keep_ref[i] > 0, 1, 0), 0)
    lax.fori_loop(0, count, place, (0, kept))
    seen_ref[count] = kept
    me_space = lax.axis_index("space")
    me = lax.axis_index("dp") * space_size + me_space
    for which, (low, high, plain) in enumerate(spans):
        at = 2 * count + 5 * which
        table_ref[at] = seen_ref[low]
        table_ref[at + 1] = seen_ref[high]
        table_ref[at + 2] = me_space * rows
        table_ref[at + 3] = jnp.maximum(kept, plain)
        table_ref[at + 4] = jnp.maximum(kept, count)
    for at, code in enumerate(codes):
        owner_ref[at] = code if space_size != 4 or len(codes) != 32 else me ^ code


def join_kernel(*refs):
    outs, pieces = refs[-2:], refs[:-2]
    each = len(pieces) // 2
    for out, group in zip(outs, (pieces[:each], pieces[each:])):
        size = group[0].shape[0]
        for at, ref in enumerate(group):
            out[at * size : (at + 1) * size, :] = ref[...]


def unpack_kernel(order_ref, small_ref, par_ref, bias_ref):
    devices = small_ref.shape[0]
    channels = par_ref.shape[1]
    width = channels // devices
    part = bias_ref.shape[1] // devices
    for group in range(ROWS // 8):
        tiles = [jnp.zeros((8, LANES), f32) for _ in range(channels // LANES)]
        for device in range(devices):
            start = device * width
            tile, low = start // LANES, start % LANES
            moved = pltpu.roll(small_ref[device], (start - group * width) % LANES, 1)
            tiles[tile] = jnp.where(lane_mask(low, low + width), moved, tiles[tile])
            if low + width > LANES:
                tiles[tile + 1] = jnp.where(lane_mask(0, low + width - LANES), moved, tiles[tile + 1])
        for tile, value in enumerate(tiles):
            par_ref[8 * group : 8 * group + 8, tile * LANES : (tile + 1) * LANES] = value
    bias_ref[...] = jnp.zeros_like(bias_ref)
    for place in range(devices):
        for at in range(part // width):
            row = VEC + 5 + at
            group, line = row // 8, row % 8
            start = place * part + at * width
            tile, low = start // LANES, start % LANES
            source = small_ref[order_ref[place], line : line + 1, :]
            moved = pltpu.roll(jnp.broadcast_to(source, (8, LANES)), (start - group * width) % LANES, 1)
            for where_, lower, upper in ((tile, low, low + width), (tile + 1, 0, low + width - LANES)):
                if upper > lower:
                    lanes = slice(where_ * LANES, (where_ + 1) * LANES)
                    kept = jnp.broadcast_to(bias_ref[0:1, lanes], (8, LANES))
                    bias_ref[0:1, lanes] = jnp.where(lane_mask(lower, upper), moved, kept)[0:1]


def pack_grads(owner_ref, taps, vec_ref, bias_ref, out_ref, rows_ref):
    devices = out_ref.shape[0]
    channels = taps.shape[1]
    width = channels // devices
    part = bias_ref.shape[1] // devices
    rows_ref[...] = jnp.zeros_like(rows_ref)
    rows_ref[0:VEC, :] = taps
    rows_ref[VEC : VEC + 5, :] = vec_ref[0:5, :]

    def cut(row_slice, source, start, group):
        tile, low = start // LANES, start % LANES
        shift = (group * width - low) % LANES
        moved = pltpu.roll(source(row_slice, tile), shift, 1)
        if low + width > LANES:
            split = group * width + LANES - low
            moved = jnp.where(lane_mask(0, split), moved, pltpu.roll(source(row_slice, tile + 1), shift, 1))
        return moved

    def of_rows(rows, tile):
        return rows_ref[rows, tile * LANES : (tile + 1) * LANES]

    def of_bias(rows, tile):
        return jnp.broadcast_to(bias_ref[0:1, tile * LANES : (tile + 1) * LANES], (8, LANES))

    for device in range(devices):
        total = jnp.zeros((8, LANES), f32)
        for group in range(ROWS // 8):
            moved = cut(slice(8 * group, 8 * group + 8), of_rows, device * width, group)
            total = jnp.where(lane_mask(group * width, (group + 1) * width), moved, total)
        out_ref[device] = total
    for place in range(devices):
        device = owner_ref[place]
        for at in range(part // width):
            row = VEC + 5 + at
            group, line = row // 8, row % 8
            moved = cut(None, of_bias, place * part + at * width, group)
            kept = jnp.broadcast_to(out_ref[device, line : line + 1, :], (8, LANES))
            mask = lane_mask(group * width, (group + 1) * width)
            out_ref[device, line : line + 1, :] = jnp.where(mask, moved, kept)[0:1]


def total_kernel(small_ref, *refs):
    count = (len(refs) - 5) // 2
    parts, (own_ref, sums_ref, norm_ref), bufs, (sems, small_buf) = refs[:count], refs[count : count + 3], refs[count + 3 : -2], refs[-2:]
    size = own_ref.shape[0]
    loads = [pltpu.make_async_copy(small_ref, small_buf, sems.at[count])]
    for at, (ref, buf) in enumerate(zip(parts, bufs)):
        loads.append(pltpu.make_async_copy(ref.at[0:size], buf, sems.at[at]))
    for load in loads:
        load.start()
    for load in loads:
        load.wait()
    own = bufs[0][...].astype(f32)
    for buf in bufs[1:]:
        own = own + buf[...].astype(f32)
    own_ref[...] = own
    sums = jnp.sum(small_buf[...], axis=0)
    sums_ref[...] = sums
    local = jnp.sum(own * own) + jnp.sum(sums * sums)
    norm_ref[...] = jnp.full_like(norm_ref, local)


def adam(weight, moment, square, grad, factor, rate):
    scaled = grad * factor
    new_moment = beta_one * moment + (1.0 - beta_one) * scaled
    new_square = beta_two * square + (1.0 - beta_two) * scaled * scaled
    corrected = new_moment / (1.0 - beta_one**STEP)
    spread = jnp.sqrt(new_square / (1.0 - beta_two**STEP))
    return weight - rate * (corrected / (spread + adam_eps) + decay_rate * weight), new_moment, new_square


def adam_kernel(own_ref, sums_ref, norms_ref, *refs):
    states, outs, norm_ref, rows_ref, flip_ref = refs[:15], refs[15:30], refs[30], refs[31], refs[32]
    part, channels = states[6].shape
    width = states[0].shape[0]
    total = jnp.sum(norms_ref[:, 0, 0:1])
    norm = jnp.sqrt(jnp.full((8, LANES), total, f32))
    norm_ref[...] = norm[0:1, 0:1]
    factor = (clip_limit / jnp.maximum(norm, clip_limit))[0:1, 0:1]
    sums = sums_ref[...]
    rows_ref[...] = jnp.zeros_like(rows_ref)
    for group in range(ROWS // 8):
        rows_ref[8 * group : 8 * group + 8, :] = pltpu.roll(sums, (-group * width) % LANES, 1)
    flip_ref[...] = rows_ref[...].T
    grads = [
        flip_ref[0:width, 0:VEC],
        rows_ref[VEC : VEC + 5, 0:width],
        own_ref[:, 0:channels],
        None,
        own_ref[:, channels : 2 * channels],
    ]
    for index, (grad, rate) in enumerate(zip(grads, step_rates)):
        if grad is None:
            continue
        results = adam(*(ref[...] for ref in states[3 * index : 3 * index + 3]), grad, factor, rate)
        for ref, value in zip(outs[3 * index : 3 * index + 3], results):
            ref[...] = value
    for at in range(part // width):
        lanes = slice(at * width, (at + 1) * width)
        row = VEC + 5 + at
        grad = rows_ref[row : row + 1, 0:width]
        results = adam(*(ref[0:1, lanes] for ref in states[9:12]), grad, factor, step_rates[3])
        for ref, value in zip(outs[9:12], results):
            ref[0:1, lanes] = value


def mlp(which, table, unit, stat, cots, pieces, bias, pars, dims):
    count, rows, cols, channels = dims
    pixels = rows * cols
    total = count * pixels
    hidden_size = bias.shape[1]
    tall = MLP_SLOTS * pixels
    at = 2 * count + 5 * which + 1

    def last(i, n):
        return jnp.minimum(i, jnp.maximum((n[at] + MLP_SLOTS - 1) // MLP_SLOTS - 1, 0))

    tile_map = lambda i, n: (last(i, n), 0)
    slot_map = lambda i, n: (last(i, n), 0, 0, 0)
    whole = lambda i, n: (0, 0)
    grad = (hidden_size // 2, 2 * channels)
    halo = (count, REACH, cols, channels)
    once = pl.Buffered(1)
    return pl.pallas_call(
        functools.partial(mlp_kernel, at),
        grid_spec=pltpu.PrefetchScalarGridSpec(
            num_scalar_prefetch=1,
            grid=(-(-count // MLP_SLOTS),),
            in_specs=[
                pl.BlockSpec((tall, channels), tile_map),
                pl.BlockSpec((tall, LANES), tile_map),
                pl.BlockSpec((tall, channels), tile_map),
                pl.BlockSpec(bias.shape, whole),
                pl.BlockSpec(pars.shape, whole),
            ]
            + [pl.BlockSpec(value.shape, whole, pipeline_mode=once) for value in pieces],
            out_specs=[
                pl.BlockSpec((MLP_SLOTS, rows, cols, channels), slot_map),
                pl.BlockSpec((MLP_SLOTS, rows, cols, channels), slot_map),
                pl.BlockSpec((MLP_SLOTS, REACH, cols, channels), slot_map),
                pl.BlockSpec((MLP_SLOTS, REACH, cols, channels), slot_map),
                pl.BlockSpec(grad, whole),
                pl.BlockSpec(grad, whole),
                pl.BlockSpec((1, hidden_size), whole),
                pl.BlockSpec((8, channels), whole),
            ],
            scratch_shapes=[
                pltpu.VMEM((channels, hidden_size), f32),
                pltpu.VMEM((channels, hidden_size), f32),
                pltpu.VMEM((hidden_size, channels), bf16),
                pltpu.VMEM((hidden_size, 2 * channels), bf16),
                pltpu.VMEM((8, hidden_size), f32),
                pltpu.VMEM((40, channels), f32),
            ],
        ),
        out_shape=[
            shape(dims, bf16),
            shape(dims, bf16),
            shape(halo, bf16),
            shape(halo, bf16),
            shape(grad, bf16),
            shape(grad, bf16),
            shape((1, hidden_size), f32),
            shape((8, channels), f32),
        ],
        compiler_params=pltpu.CompilerParams(dimension_semantics=("arbitrary",), vmem_limit_bytes=VMEM_MIB * MIB),
        name="mlp",
    )(table, unit.reshape(total, channels), stat.reshape(total, LANES), cots.reshape(total, channels), bias, pars, *pieces)


IN_PLACE = pl.BlockSpec(memory_space=pltpu.HBM)
SCALARS = pl.BlockSpec(memory_space=pltpu.SMEM)
LOADED = pl.BlockSpec(memory_space=pltpu.VMEM)


def call(kernel, in_specs, out_specs, out_shape, scratch, name, aliases=None):
    return pl.pallas_call(
        kernel,
        in_specs=in_specs,
        out_specs=out_specs,
        out_shape=out_shape,
        scratch_shapes=scratch,
        input_output_aliases=aliases or {},
        compiler_params=pltpu.CompilerParams(vmem_limit_bytes=VMEM_MIB * MIB),
        name=name,
    )


def shape(dims, kind):
    return jax.ShapeDtypeStruct(dims, kind)


def window(rows, cols, channels):
    return pltpu.VMEM((DEPTH, rows + 2 * REACH, cols, channels), bf16)


def padded(rows, cols, channels):
    return pltpu.VMEM((channels // LANES, rows + 2 * REACH, cols + 2 * EDGE, LANES), f32)


def paired(rows, cols, channels):
    return pltpu.VMEM((channels // LANES, rows // 2 + 2 * REACH, 2 * cols, LANES), bf16)


def conv_norm(which, first, table, above, own, below, cot, pars, earlier):
    count, rows, cols, channels = own.shape
    pixels = rows * cols
    outs = [
        shape((count, pixels, channels), f32),
        shape((count, pixels, LANES), f32),
        shape((count, rows, cols, channels), bf16),
    ]
    run = call(
        functools.partial(conv_norm_kernel, which, first),
        [SCALARS] + [IN_PLACE] * (5 + len(earlier)),
        [IN_PLACE] * 3,
        outs,
        [
            window(rows, cols, channels),
            pltpu.VMEM((DEPTH, pixels, channels), f32),
            pltpu.VMEM((DEPTH, pixels, LANES), f32),
            pltpu.VMEM((DEPTH, rows, cols, channels), bf16),
            padded(rows, cols, channels),
            pltpu.VMEM((pixels, channels), f32),
            pltpu.VMEM(pars.shape, f32),
            pltpu.SemaphoreType.DMA((DEPTH, 4)),
            pltpu.SemaphoreType.DMA((DEPTH, 3)),
            pltpu.SemaphoreType.DMA,
        ],
        "conv_norm",
        {6 + at: at for at in range(len(earlier))},
    )
    return run(table, above, own, below, cot, pars, *earlier)


def taps_grad(which, table, halos, own, gc, owners, vec, bias):
    count, rows, cols, channels = own.shape
    run = call(
        functools.partial(taps_grad_kernel, which, halos[0].shape[0]),
        [SCALARS] + [IN_PLACE] * 6 + [SCALARS] + [LOADED] * 2,
        LOADED,
        shape((owners.shape[0], 8, LANES), f32),
        [
            window(rows, cols, channels),
            pltpu.VMEM((DEPTH, rows, cols, channels), bf16),
            paired(rows, cols, channels),
            pltpu.VMEM((TAPS * TAPS, 8, channels), f32),
            pltpu.VMEM((channels // LANES, rows, cols + 2 * EDGE, LANES), f32),
            pltpu.VMEM((ROWS, channels), f32),
            pltpu.SemaphoreType.DMA((DEPTH, 4)),
        ],
        "taps_grad",
    )
    return run(table, halos[0], own, halos[1], halos[2], halos[3], gc, owners, vec, bias)


def finish(which, table, above, gc, below, branch, images, cot, pars, earlier):
    count, rows, cols, channels = images.shape
    block = (DEPTH, rows, cols, channels)
    run = call(
        functools.partial(finish_kernel, which),
        [SCALARS] + [IN_PLACE] * (7 + len(earlier)),
        [IN_PLACE] * 2,
        [shape(images.shape, bf16)] * 2,
        [
            window(rows, cols, channels),
            pltpu.VMEM(block, bf16),
            pltpu.VMEM(block, bf16),
            pltpu.VMEM(block, bf16),
            pltpu.VMEM(block, bf16),
            pltpu.VMEM(block, bf16),
            paired(rows, cols, channels),
            pltpu.VMEM((TAPS, rows, cols + 2 * EDGE, LANES), f32),
            pltpu.VMEM((rows, cols, channels), f32),
            pltpu.VMEM(pars.shape, f32),
            pltpu.SemaphoreType.DMA((DEPTH, 6)),
            pltpu.SemaphoreType.DMA((DEPTH, 2)),
            pltpu.SemaphoreType.DMA,
        ],
        "finish",
        {8 + at: at for at in range(len(earlier))},
    )
    maps = (value.reshape(images.shape) for value in (gc, branch))
    gc, branch = maps
    return run(table, above, gc, below, branch, images, cot, pars, *earlier)


def pack(spans, codes, space_size, rows, keep, sides, kernel, vectors, bias, up, down):
    channels, part = up.shape
    return call(
        functools.partial(pack_kernel, spans, codes, space_size, rows),
        [SCALARS] * 2 + [LOADED] * 5,
        [LOADED] * 2 + [SCALARS] * 2,
        [
            shape((len(codes), 8, LANES), f32),
            shape((part, 2 * channels), bf16),
            shape((2 * keep.shape[0] + 5 * len(spans),), jnp.int32),
            shape((len(codes),), jnp.int32),
        ],
        [pltpu.VMEM((LANES, LANES), f32), pltpu.SMEM((keep.shape[0] + 1,), jnp.int32)],
        "pack",
    )(keep, sides, kernel.T, vectors, bias.reshape(1, -1), up.T, down)


def join_two(*pieces):
    size, width = pieces[0].shape
    each = len(pieces) // 2
    out = shape((each * size, width), pieces[0].dtype)
    return call(join_kernel, [LOADED] * len(pieces), [LOADED] * 2, [out, out], [], "join")(*pieces)


def unpack(order, small, channels, hidden_size):
    return call(
        unpack_kernel,
        [SCALARS, LOADED],
        [LOADED] * 2,
        [shape((ROWS, channels), f32), shape((1, hidden_size), f32)],
        [],
        "unpack",
    )(order, small)


def add_up(small, parts, size):
    devices = small.shape[0]
    width = parts[0].shape[1]
    return call(
        total_kernel,
        [IN_PLACE] * (1 + len(parts)),
        [LOADED] * 3,
        [shape((size, width), f32), shape((8, LANES), f32), shape((devices, 8, LANES), f32)],
        [pltpu.VMEM((size, width), value.dtype) for value in parts]
        + [pltpu.SemaphoreType.DMA((len(parts) + 1,)), pltpu.VMEM(small.shape, f32)],
        "add_up",
    )(small, *parts)


def update(own, sums, norms, states):
    def view(at, value):
        if at // 3 in (0, 2):
            return value.T
        return value.reshape(1, -1) if at // 3 == 3 else value

    def unview(at, value):
        return value.reshape(-1) if at // 3 == 3 else view(at, value)

    views = [view(at, value) for at, value in enumerate(states)]
    results = call(
        adam_kernel,
        [LOADED] * 18,
        [LOADED] * 16,
        [shape(value.shape, f32) for value in views] + [shape((1, 1), f32)],
        [pltpu.VMEM((LANES, LANES), f32), pltpu.VMEM((LANES, LANES), f32)],
        "update",
    )(own, sums, norms, *views)
    return [unview(at, value) for at, value in enumerate(results[:15])], results[15].reshape(())


def pass_rows(top, low, places):
    above = lax.ppermute(low, "space", [(i, i + 1) for i in range(places - 1)])
    below = lax.ppermute(top, "space", [(i + 1, i) for i in range(places - 1)])
    return above, below


def flip_perm(size, bit):
    return [(i, i ^ bit) for i in range(size)]


def swap(value, bits):
    axis, bit, size = ("dp", bits[0], 8) if bits[0] else ("space", bits[1], 4)
    return lax.ppermute(value, axis, flip_perm(size, bit))


X, Y, CORE = (1, 0), (0, 2), (0, 1)
Z1, Z2, Z3 = (2, 0), (4, 0), (6, 0)


def cube_order():
    first = [0, 2 * 4]
    last = [4 * 4, 6 * 4]
    first = first + [v ^ 4 for v in first]
    last = last + [v ^ 2 for v in last]
    first = first + [v ^ 2 for v in first]
    last = last + [v ^ 4 for v in last]
    near = first + last
    return near + [v ^ 1 for v in near]


def after(value, *others):
    return lax.optimization_barrier((value,) + others)[0]


def behind(values, token):
    return lax.optimization_barrier((*values, token))[:-1]


def total_of(*pieces):
    total = pieces[0].astype(f32)
    for piece in pieces[1:]:
        total = total + piece.astype(f32)
    return total.astype(bf16)


def exchange(value):
    return lax.all_to_all(value, AXES, 0, 0, tiled=True)


def body(dp_size, space_size, images, cotangent, image_sides, keep_flags, *states):
    devices = dp_size * space_size
    count, rows, cols, channels = images.shape
    depth_kernel, block_vectors, up_weight, up_bias, down_weight = states[0::3]
    part = up_weight.shape[1]
    hidden_size = part * devices
    cube = dp_size == 8 and space_size == 4

    cut, mid = 3 * count // 8, 11 * count // 16
    spans = ((0, cut, count), (cut, mid, count), (mid, count, count), (mid, count, 0), (0, count, count), (0, count, 0))
    codes = tuple(cube_order()) if cube else tuple(range(devices))
    small, piece, table, owners = pack(
        spans, codes, space_size, rows, keep_flags, image_sides, depth_kernel, block_vectors, up_bias, up_weight, down_weight
    )
    small_all = exchange(small)
    piece, maps = after((piece, images), small) if cube else (piece, images)
    halos = pass_rows(maps[:cut, :REACH], maps[:cut, -REACH:], space_size)
    pars, bias = unpack(owners, small_all, channels, hidden_size)

    def conv_part(which, earlier, *waits):
        above, below = halos[:2] if which == 0 else halos[2:]
        first = 0 if which == 0 else cut
        return conv_norm(
            which, first, after(table, *waits), above, images, below, cotangent, pars, earlier
        )

    later = images
    if cube:
        first, last = join_two(*behind((piece, *(swap(piece, step) for step in (Z1, Z2, Z3))), small_all))
        later = after(images, first, last, *halos)
        got = (swap(first, X), swap(last, Y))
    halos += pass_rows(later[cut:, :REACH], later[cut:, -REACH:], space_size)
    if cube:
        made = conv_part(0, (), first, last)
        got = behind(got, made[1])
        first, last = join_two(first, got[0], last, got[1])
        got = (swap(first, Y), swap(last, X))
        made = conv_part(1, made, first, last)
        got = behind(got, made[1])
        pieces = [first, got[0], last, got[1]]
        far = [swap(value, CORE) for value in pieces]
        unit, stat, cots = conv_part(2, made, *pieces)
        pieces = pieces + list(behind(far, stat))
    else:
        pieces = [lax.all_gather(piece, AXES, axis=0, tiled=True)]
        made = conv_part(0, ())
        made = conv_part(1, made)
        unit, stat, cots = conv_part(2, made)
    branch, gc, top, low, grad_near, grad_far, bias_sum, vec_sum = mlp(
        4, table, unit, stat, cots, pieces, bias, pars, images.shape
    )

    def taps_part(which, *waits):
        return taps_grad(which, after(table, *waits), halos, images, gc, owners, vec_sum, bias_sum)

    def finish_part(which, earlier, *waits):
        return finish(
            which, after(table, *waits),
            gc_above, gc, gc_below, branch, images, cotangent, pars, earlier,
        )

    if cube:
        core = swap(grad_far, CORE)
        half = grad_near.shape[0] // 2
        quarter, eighth = half // 2, half // 4

        def kept_sum(which, low, high, *got):
            lines = slice(which * half + low, which * half + high)
            return total_of(grad_near[lines], core[lines], *(value[low:high] for value in got))

        gc_above, gc_below = pass_rows(top, low, space_size)
        send = [kept_sum(0, quarter, half), kept_sum(1, quarter, half)]
        two_a, two_b = swap(send[0], Y), swap(send[1], X)
        taps = taps_part(4, *send)
        two_a, two_b = behind((two_a, two_b), taps)
        got = exchange(taps)
        send = [kept_sum(0, eighth, quarter, two_a), kept_sum(1, eighth, quarter, two_b)]
        three_a, three_b = swap(send[0], X), swap(send[1], Y)
        made = finish_part(0, (), *send)
        three_a, three_b, got = behind((three_a, three_b, got), made[0])
        send = [
            kept_sum(0, part, 2 * part, two_a, three_a),
            kept_sum(1, 0, part, two_b, three_b),
            kept_sum(1, part, 2 * part, two_b, three_b),
        ]
        z_got = [swap(value, step) for value, step in zip(send, (Z1, Z2, Z3))]
        made = finish_part(1, made, *send)
        z_got = behind(z_got, made[0])
        own, sums, norm = add_up(got, [grad_near, core, two_a, three_a, *z_got], part)
        norms = exchange(norm)
        out_images, grad_images = finish_part(3, made, norm)
        norms, grad_images = lax.optimization_barrier((norms, grad_images))
    else:
        gc_above, gc_below = pass_rows(top, low, space_size)
        grads = jnp.concatenate([grad_near, grad_far]).astype(f32)
        parts = [lax.psum_scatter(grads, AXES, scatter_dimension=0, tiled=True)]
        got = exchange(taps_part(4))
        own, sums, norm = add_up(got, parts, part)
        norms = exchange(norm)
        out_images, grad_images = finish_part(5, ())
    results, grad_norm = update(own, sums, norms, states)
    return (out_images, grad_images, *results, grad_norm)


def solution(mesh):
    lanes = P(None, AXES)
    flat = P(AXES)
    tall = P(AXES, None)
    maps = P("dp", "space", None, None)
    in_specs = (maps, maps, P("dp"), P("dp")) + (lanes,) * 9 + (flat,) * 3 + (tall,) * 3
    out_specs = (maps, maps) + (lanes,) * 9 + (flat,) * 3 + (tall,) * 3 + (P(),)
    run = functools.partial(body, mesh.shape["dp"], mesh.shape["space"])
    return jax.shard_map(run, mesh=mesh, in_specs=in_specs, out_specs=out_specs, check_vma=False)
```

```python
import functools

import jax
import jax.numpy as jnp
from jax import lax
from jax.experimental import pallas as pl
from jax.experimental.pallas import tpu as pltpu
from jax.sharding import PartitionSpec as P

STEP = 5

keep_scale = 4.0 / 3.0
norm_eps = 1e-06
clip_limit = 1.0
beta_one = 0.9
beta_two = 0.999
adam_eps = 1e-08
decay_rate = 0.05
step_rates = (0.15, 0.5, 0.05, 0.2, 0.025)
inv_root_two = 0.7071067811865476
inv_root_tau = 0.3989422804014327
f32 = jnp.float32
bf16 = jnp.bfloat16
AXES = ("dp", "space")
LANES = 128
REACH = 3
TAPS = 7
VEC = TAPS * TAPS
ROWS = 64
NARROW = 16
EDGE = 8
MLP_SLOTS = 4
DEEP = 256
VMEM_MIB = 64
DEPTH = 5
AHEAD = DEPTH - 2
MLP_COLS = 768
MIB = 1 << 20


def dot_nn(a, b):
    return lax.dot_general(a, b, (((1,), (0,)), ((), ())), preferred_element_type=f32)


def dot_nt(a, b):
    return lax.dot_general(a, b, (((1,), (1,)), ((), ())), preferred_element_type=f32)


def fold(value):
    rows, channels = value.shape
    return jnp.sum(value.reshape(rows // 8, 8, channels), axis=0)


def mlp_kernel(
    at, table_ref, unit_ref, stat_ref, cot_ref, bias_ref, par_ref, *refs
):
    step = pl.program_id(0)
    rows, channels = unit_ref.shape
    pieces = refs[:-18]
    (branch_ref, gc_ref, top_ref, low_ref, grad_near_ref, grad_far_ref, bsum_ref, vsum_ref,
     up_acc, down_acc, scaled_ref, both_ref, bias_acc, vec_acc,
     rest_n, rest_c, rest_g, rest_a) = refs[-18:]
    hidden_size = both_ref.shape[0]
    half = hidden_size // 2
    pixels = rows // MLP_SLOTS
    used = table_ref[at] * pixels
    gamma = par_ref[VEC + 4 : VEC + 5, :] * keep_scale
    full = rows // DEEP * DEEP

    @pl.when(step == 0)
    def _():
        up_acc[...] = jnp.zeros_like(up_acc)
        down_acc[...] = jnp.zeros_like(down_acc)
        bias_acc[...] = jnp.zeros_like(bias_acc)
        vec_acc[...] = jnp.zeros_like(vec_acc)
        for ref in (rest_n, rest_c, rest_g, rest_a):
            ref[...] = jnp.zeros_like(ref)
        at = 0
        for ref in pieces:
            size = ref.shape[0]
            both_ref[at : at + size, :] = ref[...]
            down = ref[:, channels : 2 * channels].astype(f32)
            scaled_ref[at : at + size, :] = (down * gamma).astype(bf16)
            at += size

    @pl.when(step * rows < used)
    def _():
        inside = lax.broadcasted_iota(jnp.int32, (rows, channels), 0) < used - step * rows
        unit = jnp.where(inside, unit_ref[...], 0.0)
        valid = stat_ref[:, LANES // 2 : LANES // 2 + 1]
        cotm32 = jnp.where(inside, cot_ref[...].astype(f32) * valid, 0.0)
        cotm = cotm32.astype(bf16)
        normed = (unit * par_ref[VEC + 1 : VEC + 2, :] + par_ref[VEC + 2 : VEC + 3, :]).astype(bf16)
        left = rows - full
        spot = pl.ds(pl.multiple_of(step * left, left), left)
        rest_n[spot, :] = normed[full:]
        rest_c[spot, :] = cotm[full:]
        normed_t = normed[:full].T
        cotm_t = cotm[:full].T
        branch = None
        grad_normed = None
        for start in range(0, hidden_size, MLP_COLS):
            cols = slice(start, start + MLP_COLS)
            up = both_ref[cols, 0:channels]
            down = both_ref[cols, channels : 2 * channels]
            hidden = dot_nt(normed, up) + bias_ref[0:1, cols]
            cdf = 0.5 + 0.5 * lax.erf(hidden * inv_root_two)
            active = (hidden * cdf).astype(bf16)
            slope = cdf + hidden * (inv_root_tau * jnp.exp(-0.5 * hidden * hidden))
            part_branch = dot_nn(active, down)
            branch = part_branch if branch is None else branch + part_branch
            grad_hidden32 = dot_nt(cotm, scaled_ref[cols, :]) * slope
            bias_acc[:, cols] += fold(grad_hidden32)
            grad_hidden = grad_hidden32.astype(bf16)
            part_grad = dot_nn(grad_hidden, up)
            grad_normed = part_grad if grad_normed is None else grad_normed + part_grad
            rest_g[spot, cols] = grad_hidden[full:]
            rest_a[spot, cols] = active[full:]
            up_acc[:, cols] += dot_nn(normed_t, grad_hidden[:full])
            down_acc[:, cols] += dot_nn(cotm_t, active[:full])
        branch = branch + par_ref[VEC + 3 : VEC + 4, :]
        branch_ref[...] = branch.astype(bf16).reshape(branch_ref.shape)
        inv_std = stat_ref[:, 0:1]
        scaled = grad_normed * par_ref[VEC + 1 : VEC + 2, :]
        mean_a = jnp.mean(scaled, axis=-1, keepdims=True)
        mean_b = jnp.mean(scaled * unit, axis=-1, keepdims=True)
        grad_conv = inv_std * (scaled - mean_a - unit * mean_b)
        grad_conv = jnp.where(inside, grad_conv, 0.0)
        maps = grad_conv.reshape(gc_ref.shape).astype(bf16)
        gc_ref[...] = maps
        top_ref[...] = maps[:, :REACH]
        low_ref[...] = maps[:, -REACH:]
        vec_acc[0:8, :] += fold(grad_conv)
        vec_acc[8:16, :] += fold(grad_normed * unit)
        vec_acc[16:24, :] += fold(grad_normed)
        vec_acc[24:32, :] += fold(cotm32)
        vec_acc[32:40, :] += fold(cotm32 * branch)

    @pl.when(step == pl.num_programs(0) - 1)
    def _():
        rest_nt = rest_n[...].T
        rest_ct = rest_c[...].T
        for start in range(0, hidden_size, MLP_COLS):
            cols = slice(start, start + MLP_COLS)
            up_acc[:, cols] += dot_nn(rest_nt, rest_g[:, cols])
            down_acc[:, cols] += dot_nn(rest_ct, rest_a[:, cols])
            ref = grad_near_ref if start < half else grad_far_ref
            part = slice(start % half, start % half + MLP_COLS)
            ref[part, 0:channels] = up_acc[:, cols].T.astype(bf16)
            ref[part, channels : 2 * channels] = (down_acc[:, cols].T * gamma).astype(bf16)
        bsum_ref[...] = jnp.sum(bias_acc[...], axis=0, keepdims=True)
        vsum_ref[...] = jnp.zeros_like(vsum_ref)
        for row in range(5):
            total = jnp.sum(vec_acc[8 * row : 8 * row + 8, :], axis=0, keepdims=True)
            if row == 3:
                total = total * gamma
            if row == 4:
                total = total * keep_scale
            vsum_ref[row : row + 1, :] = total


def walk(low, high, fetch, compute, store, load, prepare):
    def begin(i, carry):
        for copy in fetch(i, lax.rem(i - low, DEPTH)):
            copy.start()
        return carry

    def end(i, carry):
        for copy in store(i, lax.rem(i - low, DEPTH)):
            copy.wait()
        return carry

    if load is not None:
        load.start()
    lax.fori_loop(low, jnp.minimum(high, low + AHEAD), begin, 0)
    prepare()
    if load is not None:
        load.wait()

    def step(i, carry):
        buf = lax.rem(i - low, DEPTH)
        for copy in fetch(i, buf):
            copy.wait()

        @pl.when(i - low >= 2)
        def _():
            end(i - 2, 0)

        @pl.when(i + AHEAD < high)
        def _():
            begin(i + AHEAD, 0)

        compute(i, buf)
        for copy in store(i, buf):
            copy.start()
        return carry

    lax.fori_loop(low, high, step, 0)
    lax.fori_loop(jnp.maximum(low, high - 2), high, end, 0)


def copies(pairs, sems, buf):
    return [pltpu.make_async_copy(src, dst, sems.at[buf, at]) for at, (src, dst) in enumerate(pairs)]


def clear_edges(pad_ref, cols):
    tiles, rows, width, lanes = pad_ref.shape
    for tile in range(tiles):
        for row in range(rows):
            pad_ref[tile, row, 0:EDGE, :] = jnp.zeros((EDGE, lanes), f32)
            pad_ref[tile, row, EDGE + cols : width, :] = jnp.zeros((width - EDGE - cols, lanes), f32)


def inside_cols(cols, row, side):
    reach = jnp.where(row < side, side, 0)
    return lax.broadcasted_iota(jnp.int32, (cols, LANES), 0) < reach


def fill_pairs(pair_ref, win_ref, width, side=None, first_row=None):
    tiles, pairs = pair_ref.shape[:2]
    rows = win_ref.shape[0]
    apart = rows - pairs
    for row in range(rows):
        if side is not None:
            mask = jnp.where(inside_cols(width, first_row + row, side), 1.0, 0.0).astype(bf16)
        for tile in range(tiles):
            line = win_ref[row, 0:width, tile * LANES : (tile + 1) * LANES]
            if side is not None:
                line = line * mask
            if row < pairs:
                pair_ref[tile, row, 0:width, :] = line
            if row >= apart:
                pair_ref[tile, row - apart, width : 2 * width, :] = line


def by_width(cols, side, work):
    if NARROW < cols:
        pl.when(side <= NARROW)(lambda: work(NARROW))
        pl.when(side > NARROW)(lambda: work(cols))
    else:
        work(cols)


def tree_sum(terms):
    while len(terms) > 1:
        pairs = [a + b for a, b in zip(terms[0::2], terms[1::2])]
        terms = pairs + ([terms[-1]] if len(terms) % 2 else [])
    return terms[0]


def conv_tile(pair_ref, part_ref, par_ref, tile, width, cols, flip):
    lanes = slice(tile * LANES, (tile + 1) * LANES)
    rows = part_ref.shape[1]
    half = rows // 2
    for col_off in range(TAPS):
        weights = []
        for row_off in range(TAPS):
            index = row_off * TAPS + col_off
            if flip:
                index = TAPS * TAPS - 1 - index
            weights.append(par_ref[index : index + 1, lanes].astype(bf16))
        for row in range(half):
            terms = [weights[row_off] * pair_ref[tile, row + row_off, 0 : 2 * width] for row_off in range(TAPS)]
            total = tree_sum(terms).astype(f32)
            for line, begin in ((row, 0), (row + half, width)):
                part_ref[col_off, line, EDGE : EDGE + width, :] = total[begin : begin + width]
                if width < cols:
                    part_ref[col_off, line, EDGE + width : EDGE + cols, :] = jnp.zeros((cols - width, LANES), f32)
    sums = []
    for row in range(rows):
        total = part_ref[REACH, row, EDGE : EDGE + width, :]
        for col_off in range(TAPS):
            if col_off != REACH:
                at = EDGE - REACH + col_off
                total = total + part_ref[col_off, row, at : at + width, :]
        sums.append(total)
    return sums


def conv_norm_kernel(
    which, first, table_ref, above_ref, own_ref, below_ref, cot_ref, pars_ref, *rest
):
    (unit_ref, stat_ref, cots_ref, win_ref, unit_buf, stat_buf, cot_buf, pair_ref, part_ref, conv_ref, par_ref,
     in_sems, out_sems, par_sem) = rest[-14:]
    count, rows, cols, channels = own_ref.shape
    at = 2 * count + 5 * which
    low, high, start = table_ref[at], table_ref[at + 1], table_ref[at + 2]

    def fetch(i, buf):
        image = table_ref[i]
        win = win_ref.at[buf]
        return copies(
            [
                (above_ref.at[image - first], win.at[0:REACH]),
                (own_ref.at[image], win.at[REACH : REACH + rows]),
                (below_ref.at[image - first], win.at[REACH + rows : 2 * REACH + rows]),
                (cot_ref.at[image], cot_buf.at[buf]),
            ],
            in_sems,
            buf,
        )

    def store(i, buf):
        pairs = [(unit_buf, unit_ref), (stat_buf, stat_ref), (cot_buf, cots_ref)]
        return copies([(mine.at[buf], ref.at[i]) for mine, ref in pairs], out_sems, buf)

    def compute(i, buf):
        side = table_ref[count + i]

        def convolve(width):
            fill_pairs(pair_ref, win_ref.at[buf], width, side, start - REACH)
            for tile in range(channels // LANES):
                lanes = slice(tile * LANES, (tile + 1) * LANES)
                sums = conv_tile(pair_ref, part_ref, par_ref, tile, width, cols, False)
                for row in range(rows):
                    begin, end = row * cols, (row + 1) * cols
                    conv_ref[begin : begin + width, lanes] = sums[row] + par_ref[VEC : VEC + 1, lanes]
                    if width < cols:
                        conv_ref[begin + width : end, lanes] = jnp.zeros((cols - width, LANES), f32)

        by_width(cols, side, convolve)

        @pl.when(i < high)
        def _():
            conv = conv_ref[...]
            mean = jnp.mean(conv, axis=-1, keepdims=True)
            centred = conv - mean
            var = jnp.mean(centred * centred, axis=-1, keepdims=True)
            inv_std = lax.rsqrt(var + norm_eps)
            unit_buf[buf] = centred * inv_std
            left = lax.broadcasted_iota(jnp.int32, (cols, LANES), 1) < LANES // 2
            for row in range(rows):
                inside = inside_cols(cols, start + row, side)
                spread_inv = jnp.broadcast_to(inv_std[row * cols : (row + 1) * cols], (cols, LANES))
                lines = slice(row * cols, (row + 1) * cols)
                stat_buf[buf, lines, :] = jnp.where(left, spread_inv, jnp.where(inside, 1.0, 0.0))

    load = pltpu.make_async_copy(pars_ref, par_ref, par_sem)
    walk(low, high, fetch, compute, store, load, lambda: clear_edges(part_ref, cols))


def taps_grad_kernel(
    which, split, table_ref, above_ref, own_ref, below_ref, far_above_ref, far_below_ref, gc_ref,
    owner_ref, vec_ref, bias_ref, out_ref, win_ref, gc_buf, pair_ref, acc_ref, grad_ref, rows_ref, in_sems,
):
    count, rows, cols, channels = own_ref.shape
    half = rows // 2
    at = 2 * count + 5 * which
    low, high, start = table_ref[at], table_ref[at + 1], table_ref[at + 2]

    def halo_copies(above, below, image, buf):
        win = win_ref.at[buf]
        return [
            pltpu.make_async_copy(above.at[image], win.at[0:REACH], in_sems.at[buf, 2]),
            pltpu.make_async_copy(below.at[image], win.at[REACH + rows : 2 * REACH + rows], in_sems.at[buf, 3]),
        ]

    class Halo:
        def __init__(self, image, buf):
            self.image, self.buf = image, buf

        def start(self):
            @pl.when(self.image < split)
            def _():
                for copy in halo_copies(above_ref, below_ref, self.image, self.buf):
                    copy.start()

            @pl.when(self.image >= split)
            def _():
                for copy in halo_copies(far_above_ref, far_below_ref, self.image - split, self.buf):
                    copy.start()

        def wait(self):
            for copy in halo_copies(above_ref, below_ref, 0, self.buf):
                copy.wait()

    def fetch(i, buf):
        image = table_ref[i]
        win = win_ref.at[buf]
        near = copies([(own_ref.at[image], win.at[REACH : REACH + rows]), (gc_ref.at[i], gc_buf.at[buf])], in_sems, buf)
        return near + [Halo(image, buf)]

    def compute(i, buf):
        side = table_ref[count + i]

        def multiply(width):
            fill_pairs(pair_ref, win_ref.at[buf], width, side, start - REACH)
            for row in range(rows):
                for tile in range(channels // LANES):
                    line = gc_buf[buf, row, :, tile * LANES : (tile + 1) * LANES]
                    grad_ref[tile, row, EDGE : EDGE + cols, :] = line.astype(f32)
            for tile in range(channels // LANES):
                lanes = slice(tile * LANES, (tile + 1) * LANES)
                for col_off in range(TAPS):
                    at = EDGE + REACH - col_off
                    grads = []
                    for row in range(half):
                        two = [grad_ref[tile, r, at : at + width, :] for r in (row, row + half)]
                        grads.append(jnp.concatenate(two, axis=0).astype(bf16))
                    for row_off in range(TAPS):
                        total = grads[0] * pair_ref[tile, row_off, 0 : 2 * width]
                        for row in range(1, half):
                            total = total + grads[row] * pair_ref[tile, row_off + row, 0 : 2 * width]
                        short = total[0:16]
                        for begin in range(16, 2 * width, 16):
                            short = short + total[begin : begin + 16]
                        acc_ref[row_off * TAPS + col_off, :, lanes] += fold(short.astype(f32))

        by_width(cols, side, multiply)

    def prepare():
        acc_ref[...] = jnp.zeros_like(acc_ref)
        clear_edges(grad_ref, cols)

    walk(low, high, fetch, compute, lambda i, buf: [], None, prepare)
    pack_grads(owner_ref, jnp.sum(acc_ref[...], axis=1), vec_ref, bias_ref, out_ref, rows_ref)


def finish_kernel(
    which, table_ref, above_ref, gc_ref, below_ref, branch_ref, image_ref, cot_ref, pars_ref, *rest
):
    (out_ref, gim_ref, win_ref, branch_buf, image_buf, cot_buf, out_buf, gim_buf, pair_ref, part_ref, sum_ref, par_ref,
     in_sems, out_sems, par_sem) = rest[-15:]
    count, rows, cols, channels = image_ref.shape
    half = rows // 2
    at = 2 * count + 5 * which
    low, high, start = table_ref[at], table_ref[at + 1], table_ref[at + 2]
    plain_low, plain_high = table_ref[at + 3], table_ref[at + 4]

    def fetch(i, buf):
        image = table_ref[i]
        win = win_ref.at[buf]
        return copies(
            [
                (above_ref.at[i], win.at[0:REACH]),
                (gc_ref.at[i], win.at[REACH : REACH + rows]),
                (below_ref.at[i], win.at[REACH + rows : 2 * REACH + rows]),
                (branch_ref.at[i], branch_buf.at[buf]),
                (image_ref.at[image], image_buf.at[buf]),
                (cot_ref.at[image], cot_buf.at[buf]),
            ],
            in_sems,
            buf,
        )

    def store(i, buf):
        image = table_ref[i]
        return copies([(out_buf.at[buf], out_ref.at[image]), (gim_buf.at[buf], gim_ref.at[image])], out_sems, buf)

    def pass_in(i, buf):
        image = table_ref[i]
        return copies([(image_ref.at[image], image_buf.at[buf]), (cot_ref.at[image], cot_buf.at[buf])], in_sems, buf)

    def pass_out(i, buf):
        image = table_ref[i]
        return copies([(image_buf.at[buf], out_ref.at[image]), (cot_buf.at[buf], gim_ref.at[image])], out_sems, buf)

    def compute(i, buf):
        side = table_ref[count + i]

        def convolve(width):
            fill_pairs(pair_ref, win_ref.at[buf], width)
            for tile in range(channels // LANES):
                sums = conv_tile(pair_ref, part_ref, par_ref, tile, width, cols, True)
                for row in range(rows):
                    sum_ref[row, 0:width, tile * LANES : (tile + 1) * LANES] = sums[row]

        by_width(cols, side, convolve)

        @pl.when(i < high)
        def _():
            scale = par_ref[VEC + 4 : VEC + 5, :] * keep_scale
            for row in range(rows):
                inside = inside_cols(cols, start + row, side)
                for tile in range(channels // LANES):
                    lanes = slice(tile * LANES, (tile + 1) * LANES)
                    grad = cot_buf[buf, row, :, lanes].astype(f32) + jnp.where(inside, sum_ref[row, :, lanes], 0.0)
                    gim_buf[buf, row, :, lanes] = grad.astype(bf16)
                    extra = branch_buf[buf, row, :, lanes].astype(f32) * scale[:, lanes]
                    out = image_buf[buf, row, :, lanes].astype(f32) + jnp.where(inside, extra, 0.0)
                    out_buf[buf, row, :, lanes] = out.astype(bf16)

    load = pltpu.make_async_copy(pars_ref, par_ref, par_sem)
    walk(low, high, fetch, compute, store, load, lambda: clear_edges(part_ref, cols))
    walk(plain_low, plain_high, pass_in, lambda i, buf: None, pass_out, None, lambda: None)


def lane_mask(low, high):
    lanes = lax.broadcasted_iota(jnp.int32, (8, LANES), 1)
    return (lanes >= low) & (lanes < high)


def pack_kernel(
    spans, codes, space_size, rows, keep_ref, side_ref, kernel_ref, vectors_ref, bias_ref, up_ref, down_ref,
    small_ref, piece_ref, table_ref, owner_ref, rows_ref, seen_ref,
):
    part, channels = up_ref.shape
    width = kernel_ref.shape[0]
    count = keep_ref.shape[0]
    rows_ref[...] = jnp.zeros_like(rows_ref)
    rows_ref[0:width, 0:VEC] = kernel_ref[...]
    rows_ref[...] = rows_ref[...].T
    rows_ref[VEC : VEC + 5, 0:width] = vectors_ref[...]
    for at in range(part // width):
        rows_ref[VEC + 5 + at : VEC + 6 + at, 0:width] = bias_ref[0:1, at * width : (at + 1) * width]
    small = rows_ref[0:8, :]
    for group in range(1, ROWS // 8):
        small = small + pltpu.roll(rows_ref[8 * group : 8 * group + 8, :], group * width, 1)
    for device in range(small_ref.shape[0]):
        small_ref[device] = small
    piece_ref[:, 0:channels] = up_ref[...].astype(bf16)
    piece_ref[:, channels : 2 * channels] = down_ref[...].astype(bf16)

    def place(i, at):
        keep = keep_ref[i] > 0
        upper, lower = at
        seen_ref[i] = upper
        spot = jnp.where(keep, upper, lower)
        table_ref[spot] = i
        table_ref[count + spot] = side_ref[i]
        return jnp.where(keep, upper + 1, upper), jnp.where(keep, lower, lower + 1)

    kept = lax.fori_loop(0, count, lambda i, at: at + jnp.where(keep_ref[i] > 0, 1, 0), 0)
    lax.fori_loop(0, count, place, (0, kept))
    seen_ref[count] = kept
    me_space = lax.axis_index("space")
    me = lax.axis_index("dp") * space_size + me_space
    for which, (low, high, plain) in enumerate(spans):
        at = 2 * count + 5 * which
        table_ref[at] = seen_ref[low]
        table_ref[at + 1] = seen_ref[high]
        table_ref[at + 2] = me_space * rows
        table_ref[at + 3] = jnp.maximum(kept, plain)
        table_ref[at + 4] = jnp.maximum(kept, count)
    for at, code in enumerate(codes):
        owner_ref[at] = code if space_size != 4 or len(codes) != 32 else me ^ code


def join_kernel(*refs):
    outs, pieces = refs[-2:], refs[:-2]
    each = len(pieces) // 2
    for out, group in zip(outs, (pieces[:each], pieces[each:])):
        size = group[0].shape[0]
        for at, ref in enumerate(group):
            out[at * size : (at + 1) * size, :] = ref[...]


def unpack_kernel(order_ref, small_ref, par_ref, bias_ref):
    devices = small_ref.shape[0]
    channels = par_ref.shape[1]
    width = channels // devices
    part = bias_ref.shape[1] // devices
    for group in range(ROWS // 8):
        tiles = [jnp.zeros((8, LANES), f32) for _ in range(channels // LANES)]
        for device in range(devices):
            start = device * width
            tile, low = start // LANES, start % LANES
            moved = pltpu.roll(small_ref[device], (start - group * width) % LANES, 1)
            tiles[tile] = jnp.where(lane_mask(low, low + width), moved, tiles[tile])
            if low + width > LANES:
                tiles[tile + 1] = jnp.where(lane_mask(0, low + width - LANES), moved, tiles[tile + 1])
        for tile, value in enumerate(tiles):
            par_ref[8 * group : 8 * group + 8, tile * LANES : (tile + 1) * LANES] = value
    bias_ref[...] = jnp.zeros_like(bias_ref)
    for place in range(devices):
        for at in range(part // width):
            row = VEC + 5 + at
            group, line = row // 8, row % 8
            start = place * part + at * width
            tile, low = start // LANES, start % LANES
            source = small_ref[order_ref[place], line : line + 1, :]
            moved = pltpu.roll(jnp.broadcast_to(source, (8, LANES)), (start - group * width) % LANES, 1)
            for where_, lower, upper in ((tile, low, low + width), (tile + 1, 0, low + width - LANES)):
                if upper > lower:
                    lanes = slice(where_ * LANES, (where_ + 1) * LANES)
                    kept = jnp.broadcast_to(bias_ref[0:1, lanes], (8, LANES))
                    bias_ref[0:1, lanes] = jnp.where(lane_mask(lower, upper), moved, kept)[0:1]


def pack_grads(owner_ref, taps, vec_ref, bias_ref, out_ref, rows_ref):
    devices = out_ref.shape[0]
    channels = taps.shape[1]
    width = channels // devices
    part = bias_ref.shape[1] // devices
    rows_ref[...] = jnp.zeros_like(rows_ref)
    rows_ref[0:VEC, :] = taps
    rows_ref[VEC : VEC + 5, :] = vec_ref[0:5, :]

    def cut(row_slice, source, start, group):
        tile, low = start // LANES, start % LANES
        shift = (group * width - low) % LANES
        moved = pltpu.roll(source(row_slice, tile), shift, 1)
        if low + width > LANES:
            split = group * width + LANES - low
            moved = jnp.where(lane_mask(0, split), moved, pltpu.roll(source(row_slice, tile + 1), shift, 1))
        return moved

    def of_rows(rows, tile):
        return rows_ref[rows, tile * LANES : (tile + 1) * LANES]

    def of_bias(rows, tile):
        return jnp.broadcast_to(bias_ref[0:1, tile * LANES : (tile + 1) * LANES], (8, LANES))

    for device in range(devices):
        total = jnp.zeros((8, LANES), f32)
        for group in range(ROWS // 8):
            moved = cut(slice(8 * group, 8 * group + 8), of_rows, device * width, group)
            total = jnp.where(lane_mask(group * width, (group + 1) * width), moved, total)
        out_ref[device] = total
    for place in range(devices):
        device = owner_ref[place]
        for at in range(part // width):
            row = VEC + 5 + at
            group, line = row // 8, row % 8
            moved = cut(None, of_bias, place * part + at * width, group)
            kept = jnp.broadcast_to(out_ref[device, line : line + 1, :], (8, LANES))
            mask = lane_mask(group * width, (group + 1) * width)
            out_ref[device, line : line + 1, :] = jnp.where(mask, moved, kept)[0:1]


def total_kernel(small_ref, *refs):
    count = (len(refs) - 5) // 2
    parts, (own_ref, sums_ref, norm_ref), bufs, (sems, small_buf) = refs[:count], refs[count : count + 3], refs[count + 3 : -2], refs[-2:]
    size = own_ref.shape[0]
    loads = [pltpu.make_async_copy(small_ref, small_buf, sems.at[count])]
    for at, (ref, buf) in enumerate(zip(parts, bufs)):
        loads.append(pltpu.make_async_copy(ref.at[0:size], buf, sems.at[at]))
    for load in loads:
        load.start()
    for load in loads:
        load.wait()
    own = bufs[0][...].astype(f32)
    for buf in bufs[1:]:
        own = own + buf[...].astype(f32)
    own_ref[...] = own
    sums = jnp.sum(small_buf[...], axis=0)
    sums_ref[...] = sums
    local = jnp.sum(own * own) + jnp.sum(sums * sums)
    norm_ref[...] = jnp.full_like(norm_ref, local)


def adam(weight, moment, square, grad, factor, rate):
    scaled = grad * factor
    new_moment = beta_one * moment + (1.0 - beta_one) * scaled
    new_square = beta_two * square + (1.0 - beta_two) * scaled * scaled
    corrected = new_moment / (1.0 - beta_one**STEP)
    spread = jnp.sqrt(new_square / (1.0 - beta_two**STEP))
    return weight - rate * (corrected / (spread + adam_eps) + decay_rate * weight), new_moment, new_square


def adam_kernel(own_ref, sums_ref, norms_ref, *refs):
    states, outs, norm_ref, rows_ref, flip_ref = refs[:15], refs[15:30], refs[30], refs[31], refs[32]
    part, channels = states[6].shape
    width = states[0].shape[0]
    total = jnp.sum(norms_ref[:, 0, 0:1])
    norm = jnp.sqrt(jnp.full((8, LANES), total, f32))
    norm_ref[...] = norm[0:1, 0:1]
    factor = (clip_limit / jnp.maximum(norm, clip_limit))[0:1, 0:1]
    sums = sums_ref[...]
    rows_ref[...] = jnp.zeros_like(rows_ref)
    for group in range(ROWS // 8):
        rows_ref[8 * group : 8 * group + 8, :] = pltpu.roll(sums, (-group * width) % LANES, 1)
    flip_ref[...] = rows_ref[...].T
    grads = [
        flip_ref[0:width, 0:VEC],
        rows_ref[VEC : VEC + 5, 0:width],
        own_ref[:, 0:channels],
        None,
        own_ref[:, channels : 2 * channels],
    ]
    for index, (grad, rate) in enumerate(zip(grads, step_rates)):
        if grad is None:
            continue
        results = adam(*(ref[...] for ref in states[3 * index : 3 * index + 3]), grad, factor, rate)
        for ref, value in zip(outs[3 * index : 3 * index + 3], results):
            ref[...] = value
    for at in range(part // width):
        lanes = slice(at * width, (at + 1) * width)
        row = VEC + 5 + at
        grad = rows_ref[row : row + 1, 0:width]
        results = adam(*(ref[0:1, lanes] for ref in states[9:12]), grad, factor, step_rates[3])
        for ref, value in zip(outs[9:12], results):
            ref[0:1, lanes] = value


def mlp(which, table, unit, stat, cots, pieces, bias, pars, dims):
    count, rows, cols, channels = dims
    pixels = rows * cols
    total = count * pixels
    hidden_size = bias.shape[1]
    tall = MLP_SLOTS * pixels
    at = 2 * count + 5 * which + 1

    def last(i, n):
        return jnp.minimum(i, jnp.maximum((n[at] + MLP_SLOTS - 1) // MLP_SLOTS - 1, 0))

    tile_map = lambda i, n: (last(i, n), 0)
    slot_map = lambda i, n: (last(i, n), 0, 0, 0)
    whole = lambda i, n: (0, 0)
    grad = (hidden_size // 2, 2 * channels)
    halo = (count, REACH, cols, channels)
    once = pl.Buffered(1)
    rest = tall % DEEP * -(-count // MLP_SLOTS)
    return pl.pallas_call(
        functools.partial(mlp_kernel, at),
        grid_spec=pltpu.PrefetchScalarGridSpec(
            num_scalar_prefetch=1,
            grid=(-(-count // MLP_SLOTS),),
            in_specs=[
                pl.BlockSpec((tall, channels), tile_map),
                pl.BlockSpec((tall, LANES), tile_map),
                pl.BlockSpec((tall, channels), tile_map),
                pl.BlockSpec(bias.shape, whole),
                pl.BlockSpec(pars.shape, whole),
            ]
            + [pl.BlockSpec(value.shape, whole, pipeline_mode=once) for value in pieces],
            out_specs=[
                pl.BlockSpec((MLP_SLOTS, rows, cols, channels), slot_map),
                pl.BlockSpec((MLP_SLOTS, rows, cols, channels), slot_map),
                pl.BlockSpec((MLP_SLOTS, REACH, cols, channels), slot_map),
                pl.BlockSpec((MLP_SLOTS, REACH, cols, channels), slot_map),
                pl.BlockSpec(grad, whole),
                pl.BlockSpec(grad, whole),
                pl.BlockSpec((1, hidden_size), whole),
                pl.BlockSpec((8, channels), whole),
            ],
            scratch_shapes=[
                pltpu.VMEM((channels, hidden_size), f32),
                pltpu.VMEM((channels, hidden_size), f32),
                pltpu.VMEM((hidden_size, channels), bf16),
                pltpu.VMEM((hidden_size, 2 * channels), bf16),
                pltpu.VMEM((8, hidden_size), f32),
                pltpu.VMEM((40, channels), f32),
                pltpu.VMEM((rest, channels), bf16),
                pltpu.VMEM((rest, channels), bf16),
                pltpu.VMEM((rest, hidden_size), bf16),
                pltpu.VMEM((rest, hidden_size), bf16),
            ],
        ),
        out_shape=[
            shape(dims, bf16),
            shape(dims, bf16),
            shape(halo, bf16),
            shape(halo, bf16),
            shape(grad, bf16),
            shape(grad, bf16),
            shape((1, hidden_size), f32),
            shape((8, channels), f32),
        ],
        compiler_params=pltpu.CompilerParams(dimension_semantics=("arbitrary",), vmem_limit_bytes=VMEM_MIB * MIB),
        name="mlp",
    )(table, unit.reshape(total, channels), stat.reshape(total, LANES), cots.reshape(total, channels), bias, pars, *pieces)


IN_PLACE = pl.BlockSpec(memory_space=pltpu.HBM)
SCALARS = pl.BlockSpec(memory_space=pltpu.SMEM)
LOADED = pl.BlockSpec(memory_space=pltpu.VMEM)


def call(kernel, in_specs, out_specs, out_shape, scratch, name, aliases=None):
    return pl.pallas_call(
        kernel,
        in_specs=in_specs,
        out_specs=out_specs,
        out_shape=out_shape,
        scratch_shapes=scratch,
        input_output_aliases=aliases or {},
        compiler_params=pltpu.CompilerParams(vmem_limit_bytes=VMEM_MIB * MIB),
        name=name,
    )


def shape(dims, kind):
    return jax.ShapeDtypeStruct(dims, kind)


def window(rows, cols, channels):
    return pltpu.VMEM((DEPTH, rows + 2 * REACH, cols, channels), bf16)


def paired(rows, cols, channels):
    return pltpu.VMEM((channels // LANES, rows // 2 + 2 * REACH, 2 * cols, LANES), bf16)


def conv_norm(which, first, table, above, own, below, cot, pars, earlier):
    count, rows, cols, channels = own.shape
    pixels = rows * cols
    outs = [
        shape((count, pixels, channels), f32),
        shape((count, pixels, LANES), f32),
        shape((count, rows, cols, channels), bf16),
    ]
    run = call(
        functools.partial(conv_norm_kernel, which, first),
        [SCALARS] + [IN_PLACE] * (5 + len(earlier)),
        [IN_PLACE] * 3,
        outs,
        [
            window(rows, cols, channels),
            pltpu.VMEM((DEPTH, pixels, channels), f32),
            pltpu.VMEM((DEPTH, pixels, LANES), f32),
            pltpu.VMEM((DEPTH, rows, cols, channels), bf16),
            paired(rows, cols, channels),
            pltpu.VMEM((TAPS, rows, cols + 2 * EDGE, LANES), f32),
            pltpu.VMEM((pixels, channels), f32),
            pltpu.VMEM(pars.shape, f32),
            pltpu.SemaphoreType.DMA((DEPTH, 4)),
            pltpu.SemaphoreType.DMA((DEPTH, 3)),
            pltpu.SemaphoreType.DMA,
        ],
        "conv_norm",
        {6 + at: at for at in range(len(earlier))},
    )
    return run(table, above, own, below, cot, pars, *earlier)


def taps_grad(which, table, halos, own, gc, owners, vec, bias):
    count, rows, cols, channels = own.shape
    run = call(
        functools.partial(taps_grad_kernel, which, halos[0].shape[0]),
        [SCALARS] + [IN_PLACE] * 6 + [SCALARS] + [LOADED] * 2,
        LOADED,
        shape((owners.shape[0], 8, LANES), f32),
        [
            window(rows, cols, channels),
            pltpu.VMEM((DEPTH, rows, cols, channels), bf16),
            paired(rows, cols, channels),
            pltpu.VMEM((TAPS * TAPS, 8, channels), f32),
            pltpu.VMEM((channels // LANES, rows, cols + 2 * EDGE, LANES), f32),
            pltpu.VMEM((ROWS, channels), f32),
            pltpu.SemaphoreType.DMA((DEPTH, 4)),
        ],
        "taps_grad",
    )
    return run(table, halos[0], own, halos[1], halos[2], halos[3], gc, owners, vec, bias)


def finish(which, table, above, gc, below, branch, images, cot, pars, earlier):
    count, rows, cols, channels = images.shape
    block = (DEPTH, rows, cols, channels)
    run = call(
        functools.partial(finish_kernel, which),
        [SCALARS] + [IN_PLACE] * (7 + len(earlier)),
        [IN_PLACE] * 2,
        [shape(images.shape, bf16)] * 2,
        [
            window(rows, cols, channels),
            pltpu.VMEM(block, bf16),
            pltpu.VMEM(block, bf16),
            pltpu.VMEM(block, bf16),
            pltpu.VMEM(block, bf16),
            pltpu.VMEM(block, bf16),
            paired(rows, cols, channels),
            pltpu.VMEM((TAPS, rows, cols + 2 * EDGE, LANES), f32),
            pltpu.VMEM((rows, cols, channels), f32),
            pltpu.VMEM(pars.shape, f32),
            pltpu.SemaphoreType.DMA((DEPTH, 6)),
            pltpu.SemaphoreType.DMA((DEPTH, 2)),
            pltpu.SemaphoreType.DMA,
        ],
        "finish",
        {8 + at: at for at in range(len(earlier))},
    )
    maps = (value.reshape(images.shape) for value in (gc, branch))
    gc, branch = maps
    return run(table, above, gc, below, branch, images, cot, pars, *earlier)


def pack(spans, codes, space_size, rows, keep, sides, kernel, vectors, bias, up, down):
    channels, part = up.shape
    return call(
        functools.partial(pack_kernel, spans, codes, space_size, rows),
        [SCALARS] * 2 + [LOADED] * 5,
        [LOADED] * 2 + [SCALARS] * 2,
        [
            shape((len(codes), 8, LANES), f32),
            shape((part, 2 * channels), bf16),
            shape((2 * keep.shape[0] + 5 * len(spans),), jnp.int32),
            shape((len(codes),), jnp.int32),
        ],
        [pltpu.VMEM((LANES, LANES), f32), pltpu.SMEM((keep.shape[0] + 1,), jnp.int32)],
        "pack",
    )(keep, sides, kernel.T, vectors, bias.reshape(1, -1), up.T, down)


def join_two(*pieces):
    size, width = pieces[0].shape
    each = len(pieces) // 2
    out = shape((each * size, width), pieces[0].dtype)
    return call(join_kernel, [LOADED] * len(pieces), [LOADED] * 2, [out, out], [], "join")(*pieces)


def unpack(order, small, channels, hidden_size):
    return call(
        unpack_kernel,
        [SCALARS, LOADED],
        [LOADED] * 2,
        [shape((ROWS, channels), f32), shape((1, hidden_size), f32)],
        [],
        "unpack",
    )(order, small)


def add_up(small, parts, size):
    devices = small.shape[0]
    width = parts[0].shape[1]
    return call(
        total_kernel,
        [IN_PLACE] * (1 + len(parts)),
        [LOADED] * 3,
        [shape((size, width), f32), shape((8, LANES), f32), shape((devices, 8, LANES), f32)],
        [pltpu.VMEM((size, width), value.dtype) for value in parts]
        + [pltpu.SemaphoreType.DMA((len(parts) + 1,)), pltpu.VMEM(small.shape, f32)],
        "add_up",
    )(small, *parts)


def update(own, sums, norms, states):
    def view(at, value):
        if at // 3 in (0, 2):
            return value.T
        return value.reshape(1, -1) if at // 3 == 3 else value

    def unview(at, value):
        return value.reshape(-1) if at // 3 == 3 else view(at, value)

    views = [view(at, value) for at, value in enumerate(states)]
    results = call(
        adam_kernel,
        [LOADED] * 18,
        [LOADED] * 16,
        [shape(value.shape, f32) for value in views] + [shape((1, 1), f32)],
        [pltpu.VMEM((LANES, LANES), f32), pltpu.VMEM((LANES, LANES), f32)],
        "update",
    )(own, sums, norms, *views)
    return [unview(at, value) for at, value in enumerate(results[:15])], results[15].reshape(())


def pass_rows(top, low, places):
    above = lax.ppermute(low, "space", [(i, i + 1) for i in range(places - 1)])
    below = lax.ppermute(top, "space", [(i + 1, i) for i in range(places - 1)])
    return above, below


def flip_perm(size, bit):
    return [(i, i ^ bit) for i in range(size)]


def swap(value, bits):
    axis, bit, size = ("dp", bits[0], 8) if bits[0] else ("space", bits[1], 4)
    return lax.ppermute(value, axis, flip_perm(size, bit))


X, Y, CORE = (1, 0), (0, 2), (0, 1)
Z1, Z2, Z3 = (2, 0), (4, 0), (6, 0)


def cube_order():
    first = [0, 2 * 4]
    last = [4 * 4, 6 * 4]
    first = first + [v ^ 4 for v in first]
    last = last + [v ^ 2 for v in last]
    first = first + [v ^ 2 for v in first]
    last = last + [v ^ 4 for v in last]
    near = first + last
    return near + [v ^ 1 for v in near]


def after(value, *others):
    return lax.optimization_barrier((value,) + others)[0]


def behind(values, token):
    return lax.optimization_barrier((*values, token))[:-1]


def total_of(*pieces):
    total = pieces[0].astype(f32)
    for piece in pieces[1:]:
        total = total + piece.astype(f32)
    return total.astype(bf16)


def exchange(value):
    return lax.all_to_all(value, AXES, 0, 0, tiled=True)


def body(dp_size, space_size, images, cotangent, image_sides, keep_flags, *states):
    devices = dp_size * space_size
    count, rows, cols, channels = images.shape
    depth_kernel, block_vectors, up_weight, up_bias, down_weight = states[0::3]
    part = up_weight.shape[1]
    hidden_size = part * devices
    cube = dp_size == 8 and space_size == 4

    cut, mid = 3 * count // 8, 11 * count // 16
    spans = ((0, cut, count), (cut, mid, count), (mid, count, count), (mid, count, 0), (0, count, count), (0, count, 0))
    codes = tuple(cube_order()) if cube else tuple(range(devices))
    small, piece, table, owners = pack(
        spans, codes, space_size, rows, keep_flags, image_sides, depth_kernel, block_vectors, up_bias, up_weight, down_weight
    )
    small_all = exchange(small)
    piece, maps = after((piece, images), small) if cube else (piece, images)
    halos = pass_rows(maps[:cut, :REACH], maps[:cut, -REACH:], space_size)
    pars, bias = unpack(owners, small_all, channels, hidden_size)

    def conv_part(which, earlier, *waits):
        above, below = halos[:2] if which == 0 else halos[2:]
        first = 0 if which == 0 else cut
        return conv_norm(
            which, first, after(table, *waits), above, images, below, cotangent, pars, earlier
        )

    later = images
    if cube:
        first, last = join_two(*behind((piece, *(swap(piece, step) for step in (Z1, Z2, Z3))), small_all))
        later = after(images, first, last, *halos)
        got = (swap(first, X), swap(last, Y))
    halos += pass_rows(later[cut:, :REACH], later[cut:, -REACH:], space_size)
    if cube:
        made = conv_part(0, (), first, last)
        got = behind(got, made[1])
        first, last = join_two(first, got[0], last, got[1])
        got = (swap(first, Y), swap(last, X))
        made = conv_part(1, made, first, last)
        got = behind(got, made[1])
        pieces = [first, got[0], last, got[1]]
        far = [swap(value, CORE) for value in pieces]
        unit, stat, cots = conv_part(2, made, *pieces)
        pieces = pieces + list(behind(far, stat))
    else:
        pieces = [lax.all_gather(piece, AXES, axis=0, tiled=True)]
        made = conv_part(0, ())
        made = conv_part(1, made)
        unit, stat, cots = conv_part(2, made)
    branch, gc, top, low, grad_near, grad_far, bias_sum, vec_sum = mlp(
        4, table, unit, stat, cots, pieces, bias, pars, images.shape
    )

    def taps_part(which, *waits):
        return taps_grad(which, after(table, *waits), halos, images, gc, owners, vec_sum, bias_sum)

    def finish_part(which, earlier, *waits):
        return finish(
            which, after(table, *waits),
            gc_above, gc, gc_below, branch, images, cotangent, pars, earlier,
        )

    if cube:
        core = swap(grad_far, CORE)
        half = grad_near.shape[0] // 2
        quarter, eighth = half // 2, half // 4

        def kept_sum(which, low, high, *got):
            lines = slice(which * half + low, which * half + high)
            return total_of(grad_near[lines], core[lines], *(value[low:high] for value in got))

        gc_above, gc_below = pass_rows(top, low, space_size)
        send = [kept_sum(0, quarter, half), kept_sum(1, quarter, half)]
        two_a, two_b = swap(send[0], Y), swap(send[1], X)
        taps = taps_part(4, *send)
        two_a, two_b = behind((two_a, two_b), taps)
        got = exchange(taps)
        send = [kept_sum(0, eighth, quarter, two_a), kept_sum(1, eighth, quarter, two_b)]
        three_a, three_b = swap(send[0], X), swap(send[1], Y)
        made = finish_part(0, (), *send)
        three_a, three_b, got = behind((three_a, three_b, got), made[0])
        send = [
            kept_sum(0, part, 2 * part, two_a, three_a),
            kept_sum(1, 0, part, two_b, three_b),
            kept_sum(1, part, 2 * part, two_b, three_b),
        ]
        z_got = [swap(value, step) for value, step in zip(send, (Z1, Z2, Z3))]
        made = finish_part(1, made, *send)
        z_got = behind(z_got, made[0])
        own, sums, norm = add_up(got, [grad_near, core, two_a, three_a, *z_got], part)
        norms = exchange(norm)
        out_images, grad_images = finish_part(3, made, norm)
        norms, grad_images = lax.optimization_barrier((norms, grad_images))
    else:
        gc_above, gc_below = pass_rows(top, low, space_size)
        grads = jnp.concatenate([grad_near, grad_far]).astype(f32)
        parts = [lax.psum_scatter(grads, AXES, scatter_dimension=0, tiled=True)]
        got = exchange(taps_part(4))
        own, sums, norm = add_up(got, parts, part)
        norms = exchange(norm)
        out_images, grad_images = finish_part(5, ())
    results, grad_norm = update(own, sums, norms, states)
    return (out_images, grad_images, *results, grad_norm)


def solution(mesh):
    lanes = P(None, AXES)
    flat = P(AXES)
    tall = P(AXES, None)
    maps = P("dp", "space", None, None)
    in_specs = (maps, maps, P("dp"), P("dp")) + (lanes,) * 9 + (flat,) * 3 + (tall,) * 3
    out_specs = (maps, maps) + (lanes,) * 9 + (flat,) * 3 + (tall,) * 3 + (P(),)
    run = functools.partial(body, mesh.shape["dp"], mesh.shape["space"])
    return jax.shard_map(run, mesh=mesh, in_specs=in_specs, out_specs=out_specs, check_vma=False)
```

```python
import functools

import jax
import jax.numpy as jnp
from jax import lax
from jax.experimental import pallas as pl
from jax.experimental.pallas import tpu as pltpu
from jax.sharding import PartitionSpec as P

STEP = 5

keep_scale = 4.0 / 3.0
norm_eps = 1e-06
clip_limit = 1.0
beta_one = 0.9
beta_two = 0.999
adam_eps = 1e-08
decay_rate = 0.05
step_rates = (0.15, 0.5, 0.05, 0.2, 0.025)
inv_root_two = 0.7071067811865476
inv_root_tau = 0.3989422804014327
f32 = jnp.float32
bf16 = jnp.bfloat16
AXES = ("dp", "space")
LANES = 128
REACH = 3
TAPS = 7
VEC = TAPS * TAPS
ROWS = 64
NARROW = 16
EDGE = 8
MLP_SLOTS = 4
DEEP = 256
VMEM_MIB = 64
DEPTH = 5
AHEAD = DEPTH - 2
MLP_COLS = 768
MIB = 1 << 20


def dot_nn(a, b):
    return lax.dot_general(a, b, (((1,), (0,)), ((), ())), preferred_element_type=f32)


def dot_nt(a, b):
    return lax.dot_general(a, b, (((1,), (1,)), ((), ())), preferred_element_type=f32)


def fold(value):
    rows, channels = value.shape
    return jnp.sum(value.reshape(rows // 8, 8, channels), axis=0)


def mlp_kernel(
    at, table_ref, unit_ref, stat_ref, cot_ref, bias_ref, par_ref, *refs
):
    step = pl.program_id(0)
    rows, channels = unit_ref.shape
    pieces = refs[:-18]
    (branch_ref, gc_ref, top_ref, low_ref, grad_near_ref, grad_far_ref, bsum_ref, vsum_ref,
     up_acc, down_acc, scaled_ref, both_ref, bias_acc, vec_acc,
     rest_n, rest_c, rest_g, rest_a) = refs[-18:]
    hidden_size = both_ref.shape[0]
    half = hidden_size // 2
    pixels = rows // MLP_SLOTS
    used = table_ref[at] * pixels
    gamma = par_ref[VEC + 4 : VEC + 5, :] * keep_scale
    full = rows // DEEP * DEEP

    @pl.when(step == 0)
    def _():
        up_acc[...] = jnp.zeros_like(up_acc)
        down_acc[...] = jnp.zeros_like(down_acc)
        bias_acc[...] = jnp.zeros_like(bias_acc)
        vec_acc[...] = jnp.zeros_like(vec_acc)
        for ref in (rest_n, rest_c, rest_g, rest_a):
            ref[...] = jnp.zeros_like(ref)
        at = 0
        for ref in pieces:
            size = ref.shape[0]
            both_ref[at : at + size, :] = ref[...]
            down = ref[:, channels : 2 * channels].astype(f32)
            scaled_ref[at : at + size, :] = (down * gamma).astype(bf16)
            at += size

    @pl.when(step * rows < used)
    def _():
        inside = lax.broadcasted_iota(jnp.int32, (rows, channels), 0) < used - step * rows
        unit = jnp.where(inside, unit_ref[...], 0.0)
        valid = stat_ref[:, LANES // 2 : LANES // 2 + 1]
        cotm32 = jnp.where(inside, cot_ref[...].astype(f32) * valid, 0.0)
        cotm = cotm32.astype(bf16)
        normed = (unit * par_ref[VEC + 1 : VEC + 2, :] + par_ref[VEC + 2 : VEC + 3, :]).astype(bf16)
        left = rows - full
        spot = pl.ds(pl.multiple_of(step * left, left), left)
        rest_n[spot, :] = normed[full:]
        rest_c[spot, :] = cotm[full:]
        normed_t = normed[:full].T
        cotm_t = cotm[:full].T
        branch = None
        grad_normed = None
        for start in range(0, hidden_size, MLP_COLS):
            cols = slice(start, start + MLP_COLS)
            up = both_ref[cols, 0:channels]
            down = both_ref[cols, channels : 2 * channels]
            hidden = dot_nt(normed, up) + bias_ref[0:1, cols]
            cdf = 0.5 + 0.5 * lax.erf(hidden * inv_root_two)
            active = (hidden * cdf).astype(bf16)
            slope = cdf + hidden * (inv_root_tau * jnp.exp(-0.5 * hidden * hidden))
            part_branch = dot_nn(active, down)
            branch = part_branch if branch is None else branch + part_branch
            grad_hidden32 = dot_nt(cotm, scaled_ref[cols, :]) * slope
            bias_acc[:, cols] += fold(grad_hidden32)
            grad_hidden = grad_hidden32.astype(bf16)
            part_grad = dot_nn(grad_hidden, up)
            grad_normed = part_grad if grad_normed is None else grad_normed + part_grad
            rest_g[spot, cols] = grad_hidden[full:]
            rest_a[spot, cols] = active[full:]
            up_acc[:, cols] += dot_nn(normed_t, grad_hidden[:full])
            down_acc[:, cols] += dot_nn(cotm_t, active[:full])
        branch = branch + par_ref[VEC + 3 : VEC + 4, :]
        branch_ref[...] = branch.astype(bf16).reshape(branch_ref.shape)
        inv_std = stat_ref[:, 0:1]
        scaled = grad_normed * par_ref[VEC + 1 : VEC + 2, :]
        mean_a = jnp.mean(scaled, axis=-1, keepdims=True)
        mean_b = jnp.mean(scaled * unit, axis=-1, keepdims=True)
        grad_conv = inv_std * (scaled - mean_a - unit * mean_b)
        grad_conv = jnp.where(inside, grad_conv, 0.0)
        maps = grad_conv.reshape(gc_ref.shape).astype(bf16)
        gc_ref[...] = maps
        top_ref[...] = maps[:, :REACH]
        low_ref[...] = maps[:, -REACH:]
        vec_acc[0:8, :] += fold(grad_conv)
        vec_acc[8:16, :] += fold(grad_normed * unit)
        vec_acc[16:24, :] += fold(grad_normed)
        vec_acc[24:32, :] += fold(cotm32)
        vec_acc[32:40, :] += fold(cotm32 * branch)

    @pl.when(step == pl.num_programs(0) - 1)
    def _():
        rest_nt = rest_n[...].T
        rest_ct = rest_c[...].T
        for start in range(0, hidden_size, MLP_COLS):
            cols = slice(start, start + MLP_COLS)
            up_acc[:, cols] += dot_nn(rest_nt, rest_g[:, cols])
            down_acc[:, cols] += dot_nn(rest_ct, rest_a[:, cols])
            ref = grad_near_ref if start < half else grad_far_ref
            part = slice(start % half, start % half + MLP_COLS)
            ref[part, 0:channels] = up_acc[:, cols].T.astype(bf16)
            ref[part, channels : 2 * channels] = (down_acc[:, cols].T * gamma).astype(bf16)
        bsum_ref[...] = jnp.sum(bias_acc[...], axis=0, keepdims=True)
        vsum_ref[...] = jnp.zeros_like(vsum_ref)
        for row in range(5):
            total = jnp.sum(vec_acc[8 * row : 8 * row + 8, :], axis=0, keepdims=True)
            if row == 3:
                total = total * gamma
            if row == 4:
                total = total * keep_scale
            vsum_ref[row : row + 1, :] = total


def walk(low, high, fetch, compute, store, load, prepare):
    def begin(i, carry):
        for copy in fetch(i, lax.rem(i - low, DEPTH)):
            copy.start()
        return carry

    def end(i, carry):
        for copy in store(i, lax.rem(i - low, DEPTH)):
            copy.wait()
        return carry

    if load is not None:
        load.start()
    lax.fori_loop(low, jnp.minimum(high, low + AHEAD), begin, 0)
    prepare()
    if load is not None:
        load.wait()

    def step(i, carry):
        buf = lax.rem(i - low, DEPTH)
        for copy in fetch(i, buf):
            copy.wait()

        @pl.when(i - low >= 2)
        def _():
            end(i - 2, 0)

        @pl.when(i + AHEAD < high)
        def _():
            begin(i + AHEAD, 0)

        compute(i, buf)
        for copy in store(i, buf):
            copy.start()
        return carry

    lax.fori_loop(low, high, step, 0)
    lax.fori_loop(jnp.maximum(low, high - 2), high, end, 0)


def copies(pairs, sems, buf):
    return [pltpu.make_async_copy(src, dst, sems.at[buf, at]) for at, (src, dst) in enumerate(pairs)]


def clear_edges(pad_ref, cols):
    tiles, rows, width, lanes = pad_ref.shape
    for tile in range(tiles):
        for row in range(rows):
            pad_ref[tile, row, 0:EDGE, :] = jnp.zeros((EDGE, lanes), f32)
            pad_ref[tile, row, EDGE + cols : width, :] = jnp.zeros((width - EDGE - cols, lanes), f32)


def inside_cols(cols, row, side):
    reach = jnp.where(row < side, side, 0)
    return lax.broadcasted_iota(jnp.int32, (cols, LANES), 0) < reach


def fill_pairs(pair_ref, win_ref, width, side=None, first_row=None):
    tiles, pairs = pair_ref.shape[:2]
    rows = win_ref.shape[0]
    apart = rows - pairs
    for row in range(rows):
        if side is not None:
            mask = jnp.where(inside_cols(width, first_row + row, side), 1.0, 0.0).astype(bf16)
        for tile in range(tiles):
            line = win_ref[row, 0:width, tile * LANES : (tile + 1) * LANES]
            if side is not None:
                line = line * mask
            if row < pairs:
                pair_ref[tile, row, 0:width, :] = line
            if row >= apart:
                pair_ref[tile, row - apart, width : 2 * width, :] = line


def by_width(cols, side, work):
    if NARROW < cols:
        pl.when(side <= NARROW)(lambda: work(NARROW))
        pl.when(side > NARROW)(lambda: work(cols))
    else:
        work(cols)


def tree_sum(terms):
    while len(terms) > 1:
        pairs = [a + b for a, b in zip(terms[0::2], terms[1::2])]
        terms = pairs + ([terms[-1]] if len(terms) % 2 else [])
    return terms[0]


def conv_tile(pair_ref, part_ref, par_ref, tile, width, cols, flip):
    lanes = slice(tile * LANES, (tile + 1) * LANES)
    rows = part_ref.shape[1]
    half = rows // 2
    for col_off in range(TAPS):
        weights = []
        for row_off in range(TAPS):
            index = row_off * TAPS + col_off
            if flip:
                index = TAPS * TAPS - 1 - index
            weights.append(par_ref[index : index + 1, lanes].astype(bf16))
        for row in range(half):
            terms = [weights[row_off] * pair_ref[tile, row + row_off, 0 : 2 * width] for row_off in range(TAPS)]
            total = tree_sum(terms).astype(f32)
            for line, begin in ((row, 0), (row + half, width)):
                part_ref[col_off, line, EDGE : EDGE + width, :] = total[begin : begin + width]
                if width < cols:
                    part_ref[col_off, line, EDGE + width : EDGE + cols, :] = jnp.zeros((cols - width, LANES), f32)
    sums = []
    for row in range(rows):
        total = part_ref[REACH, row, EDGE : EDGE + width, :]
        for col_off in range(TAPS):
            if col_off != REACH:
                at = EDGE - REACH + col_off
                total = total + part_ref[col_off, row, at : at + width, :]
        sums.append(total)
    return sums


def conv_norm_kernel(
    which, first, table_ref, above_ref, own_ref, below_ref, cot_ref, pars_ref, *rest
):
    (unit_ref, stat_ref, cots_ref, win_ref, unit_buf, stat_buf, cot_buf, pair_ref, part_ref, conv_ref, par_ref,
     in_sems, out_sems, par_sem) = rest[-14:]
    count, rows, cols, channels = own_ref.shape
    at = 2 * count + 5 * which
    low, high, start = table_ref[at], table_ref[at + 1], table_ref[at + 2]

    def fetch(i, buf):
        image = table_ref[i]
        win = win_ref.at[buf]
        return copies(
            [
                (above_ref.at[image - first], win.at[0:REACH]),
                (own_ref.at[image], win.at[REACH : REACH + rows]),
                (below_ref.at[image - first], win.at[REACH + rows : 2 * REACH + rows]),
                (cot_ref.at[image], cot_buf.at[buf]),
            ],
            in_sems,
            buf,
        )

    def store(i, buf):
        pairs = [(unit_buf, unit_ref), (stat_buf, stat_ref), (cot_buf, cots_ref)]
        return copies([(mine.at[buf], ref.at[i]) for mine, ref in pairs], out_sems, buf)

    def compute(i, buf):
        side = table_ref[count + i]

        def convolve(width):
            fill_pairs(pair_ref, win_ref.at[buf], width, side, start - REACH)
            for tile in range(channels // LANES):
                lanes = slice(tile * LANES, (tile + 1) * LANES)
                sums = conv_tile(pair_ref, part_ref, par_ref, tile, width, cols, False)
                for row in range(rows):
                    begin, end = row * cols, (row + 1) * cols
                    conv_ref[begin : begin + width, lanes] = sums[row] + par_ref[VEC : VEC + 1, lanes]
                    if width < cols:
                        conv_ref[begin + width : end, lanes] = jnp.zeros((cols - width, LANES), f32)

        by_width(cols, side, convolve)

        @pl.when(i < high)
        def _():
            conv = conv_ref[...]
            mean = jnp.mean(conv, axis=-1, keepdims=True)
            centred = conv - mean
            var = jnp.mean(centred * centred, axis=-1, keepdims=True)
            inv_std = lax.rsqrt(var + norm_eps)
            unit_buf[buf] = centred * inv_std
            left = lax.broadcasted_iota(jnp.int32, (cols, LANES), 1) < LANES // 2
            for row in range(rows):
                inside = inside_cols(cols, start + row, side)
                spread_inv = jnp.broadcast_to(inv_std[row * cols : (row + 1) * cols], (cols, LANES))
                lines = slice(row * cols, (row + 1) * cols)
                stat_buf[buf, lines, :] = jnp.where(left, spread_inv, jnp.where(inside, 1.0, 0.0))

    load = pltpu.make_async_copy(pars_ref, par_ref, par_sem)
    walk(low, high, fetch, compute, store, load, lambda: clear_edges(part_ref, cols))


def taps_grad_kernel(
    which, split, table_ref, above_ref, own_ref, below_ref, far_above_ref, far_below_ref, gc_ref,
    owner_ref, vec_ref, bias_ref, out_ref, win_ref, gc_buf, pair_ref, acc_ref, grad_ref, rows_ref, in_sems,
):
    count, rows, cols, channels = own_ref.shape
    half = rows // 2
    at = 2 * count + 5 * which
    low, high, start = table_ref[at], table_ref[at + 1], table_ref[at + 2]

    def halo_copies(above, below, image, buf):
        win = win_ref.at[buf]
        return [
            pltpu.make_async_copy(above.at[image], win.at[0:REACH], in_sems.at[buf, 2]),
            pltpu.make_async_copy(below.at[image], win.at[REACH + rows : 2 * REACH + rows], in_sems.at[buf, 3]),
        ]

    class Halo:
        def __init__(self, image, buf):
            self.image, self.buf = image, buf

        def start(self):
            @pl.when(self.image < split)
            def _():
                for copy in halo_copies(above_ref, below_ref, self.image, self.buf):
                    copy.start()

            @pl.when(self.image >= split)
            def _():
                for copy in halo_copies(far_above_ref, far_below_ref, self.image - split, self.buf):
                    copy.start()

        def wait(self):
            for copy in halo_copies(above_ref, below_ref, 0, self.buf):
                copy.wait()

    def fetch(i, buf):
        image = table_ref[i]
        win = win_ref.at[buf]
        near = copies([(own_ref.at[image], win.at[REACH : REACH + rows]), (gc_ref.at[i], gc_buf.at[buf])], in_sems, buf)
        return near + [Halo(image, buf)]

    def compute(i, buf):
        side = table_ref[count + i]

        def multiply(width):
            fill_pairs(pair_ref, win_ref.at[buf], width, side, start - REACH)
            for row in range(rows):
                for tile in range(channels // LANES):
                    line = gc_buf[buf, row, :, tile * LANES : (tile + 1) * LANES]
                    grad_ref[tile, row, EDGE : EDGE + cols, :] = line.astype(f32)
            for tile in range(channels // LANES):
                lanes = slice(tile * LANES, (tile + 1) * LANES)
                for col_off in range(TAPS):
                    at = EDGE + REACH - col_off
                    grads = []
                    for row in range(half):
                        two = [grad_ref[tile, r, at : at + width, :] for r in (row, row + half)]
                        grads.append(jnp.concatenate(two, axis=0).astype(bf16))
                    for row_off in range(TAPS):
                        total = grads[0] * pair_ref[tile, row_off, 0 : 2 * width]
                        for row in range(1, half):
                            total = total + grads[row] * pair_ref[tile, row_off + row, 0 : 2 * width]
                        short = total[0:16]
                        for begin in range(16, 2 * width, 16):
                            short = short + total[begin : begin + 16]
                        acc_ref[row_off * TAPS + col_off, :, lanes] += fold(short.astype(f32))

        by_width(cols, side, multiply)

    def prepare():
        acc_ref[...] = jnp.zeros_like(acc_ref)
        clear_edges(grad_ref, cols)

    walk(low, high, fetch, compute, lambda i, buf: [], None, prepare)
    pack_grads(owner_ref, jnp.sum(acc_ref[...], axis=1), vec_ref, bias_ref, out_ref, rows_ref)


def finish_kernel(
    which, table_ref, above_ref, gc_ref, below_ref, branch_ref, image_ref, cot_ref, pars_ref, *rest
):
    (out_ref, gim_ref, win_ref, branch_buf, image_buf, cot_buf, out_buf, gim_buf, pair_ref, part_ref, sum_ref, par_ref,
     spare_buf, in_sems, out_sems, par_sem, spare_sems) = rest[-17:]
    count, rows, cols, channels = image_ref.shape
    half = rows // 2
    at = 2 * count + 5 * which
    low, high, start = table_ref[at], table_ref[at + 1], table_ref[at + 2]
    plain_low, plain_high = table_ref[at + 3], table_ref[at + 4]

    def fetch(i, buf):
        image = table_ref[i]
        win = win_ref.at[buf]
        return copies(
            [
                (above_ref.at[i], win.at[0:REACH]),
                (gc_ref.at[i], win.at[REACH : REACH + rows]),
                (below_ref.at[i], win.at[REACH + rows : 2 * REACH + rows]),
                (branch_ref.at[i], branch_buf.at[buf]),
                (image_ref.at[image], image_buf.at[buf]),
                (cot_ref.at[image], cot_buf.at[buf]),
            ],
            in_sems,
            buf,
        )

    def store(i, buf):
        image = table_ref[i]
        return copies([(out_buf.at[buf], out_ref.at[image]), (gim_buf.at[buf], gim_ref.at[image])], out_sems, buf)

    def pass_in(i, buf):
        image = table_ref[i]
        return copies([(image_ref.at[image], image_buf.at[buf]), (cot_ref.at[image], cot_buf.at[buf])], in_sems, buf)

    def pass_out(i, buf):
        image = table_ref[i]
        return copies([(image_buf.at[buf], out_ref.at[image]), (cot_buf.at[buf], gim_ref.at[image])], out_sems, buf)

    def compute(i, buf):
        side = table_ref[count + i]

        def convolve(width):
            fill_pairs(pair_ref, win_ref.at[buf], width)
            for tile in range(channels // LANES):
                sums = conv_tile(pair_ref, part_ref, par_ref, tile, width, cols, True)
                for row in range(rows):
                    sum_ref[row, 0:width, tile * LANES : (tile + 1) * LANES] = sums[row]

        by_width(cols, side, convolve)

        @pl.when(i < high)
        def _():
            scale = par_ref[VEC + 4 : VEC + 5, :] * keep_scale
            for row in range(rows):
                inside = inside_cols(cols, start + row, side)
                for tile in range(channels // LANES):
                    lanes = slice(tile * LANES, (tile + 1) * LANES)
                    grad = cot_buf[buf, row, :, lanes].astype(f32) + jnp.where(inside, sum_ref[row, :, lanes], 0.0)
                    gim_buf[buf, row, :, lanes] = grad.astype(bf16)
                    extra = branch_buf[buf, row, :, lanes].astype(f32) * scale[:, lanes]
                    out = image_buf[buf, row, :, lanes].astype(f32) + jnp.where(inside, extra, 0.0)
                    out_buf[buf, row, :, lanes] = out.astype(bf16)

    def each(copies_, what, then):
        for copy in copies_:
            copy.start() if what == "start" else copy.wait()
        for copy in then:
            copy.start()
        return 0

    def spare_in(i):
        image, buf = table_ref[i], i - plain_low
        return [
            pltpu.make_async_copy(image_ref.at[image], spare_buf.at[buf, 0], spare_sems.at[buf, 0]),
            pltpu.make_async_copy(cot_ref.at[image], spare_buf.at[buf, 1], spare_sems.at[buf, 1]),
        ]

    def spare_out(i):
        image, buf = table_ref[i], i - plain_low
        return [
            pltpu.make_async_copy(spare_buf.at[buf, 0], out_ref.at[image], spare_sems.at[buf, 2]),
            pltpu.make_async_copy(spare_buf.at[buf, 1], gim_ref.at[image], spare_sems.at[buf, 3]),
        ]

    spare = jnp.minimum(plain_high, plain_low + DEPTH)
    lax.fori_loop(plain_low, spare, lambda i, c: each(spare_in(i), "start", []), 0)
    load = pltpu.make_async_copy(pars_ref, par_ref, par_sem)
    walk(low, high, fetch, compute, store, load, lambda: clear_edges(part_ref, cols))
    lax.fori_loop(plain_low, spare, lambda i, c: each(spare_in(i), "wait", spare_out(i)), 0)
    walk(spare, plain_high, pass_in, lambda i, buf: None, pass_out, None, lambda: None)
    lax.fori_loop(plain_low, spare, lambda i, c: each(spare_out(i), "wait", []), 0)


def lane_mask(low, high):
    lanes = lax.broadcasted_iota(jnp.int32, (8, LANES), 1)
    return (lanes >= low) & (lanes < high)


def pack_kernel(
    spans, codes, space_size, rows, keep_ref, side_ref, kernel_ref, vectors_ref, bias_ref, up_ref, down_ref,
    small_ref, piece_ref, table_ref, owner_ref, rows_ref, seen_ref,
):
    part, channels = up_ref.shape
    width = kernel_ref.shape[0]
    count = keep_ref.shape[0]
    rows_ref[...] = jnp.zeros_like(rows_ref)
    rows_ref[0:width, 0:VEC] = kernel_ref[...]
    rows_ref[...] = rows_ref[...].T
    rows_ref[VEC : VEC + 5, 0:width] = vectors_ref[...]
    for at in range(part // width):
        rows_ref[VEC + 5 + at : VEC + 6 + at, 0:width] = bias_ref[0:1, at * width : (at + 1) * width]
    small = rows_ref[0:8, :]
    for group in range(1, ROWS // 8):
        small = small + pltpu.roll(rows_ref[8 * group : 8 * group + 8, :], group * width, 1)
    for device in range(small_ref.shape[0]):
        small_ref[device] = small
    piece_ref[:, 0:channels] = up_ref[...].astype(bf16)
    piece_ref[:, channels : 2 * channels] = down_ref[...].astype(bf16)

    def place(i, at):
        keep = keep_ref[i] > 0
        upper, lower = at
        seen_ref[i] = upper
        spot = jnp.where(keep, upper, lower)
        table_ref[spot] = i
        table_ref[count + spot] = side_ref[i]
        return jnp.where(keep, upper + 1, upper), jnp.where(keep, lower, lower + 1)

    kept = lax.fori_loop(0, count, lambda i, at: at + jnp.where(keep_ref[i] > 0, 1, 0), 0)
    lax.fori_loop(0, count, place, (0, kept))
    seen_ref[count] = kept
    me_space = lax.axis_index("space")
    me = lax.axis_index("dp") * space_size + me_space
    for which, (low, high, plain) in enumerate(spans):
        at = 2 * count + 5 * which
        table_ref[at] = seen_ref[low]
        table_ref[at + 1] = seen_ref[high]
        table_ref[at + 2] = me_space * rows
        table_ref[at + 3] = jnp.maximum(kept, plain)
        table_ref[at + 4] = jnp.maximum(kept, count)
    for at, code in enumerate(codes):
        owner_ref[at] = code if space_size != 4 or len(codes) != 32 else me ^ code


def join_kernel(*refs):
    outs, pieces = refs[-2:], refs[:-2]
    each = len(pieces) // 2
    for out, group in zip(outs, (pieces[:each], pieces[each:])):
        size = group[0].shape[0]
        for at, ref in enumerate(group):
            out[at * size : (at + 1) * size, :] = ref[...]


def unpack_kernel(order_ref, small_ref, par_ref, bias_ref):
    devices = small_ref.shape[0]
    channels = par_ref.shape[1]
    width = channels // devices
    part = bias_ref.shape[1] // devices
    for group in range(ROWS // 8):
        tiles = [jnp.zeros((8, LANES), f32) for _ in range(channels // LANES)]
        for device in range(devices):
            start = device * width
            tile, low = start // LANES, start % LANES
            moved = pltpu.roll(small_ref[device], (start - group * width) % LANES, 1)
            tiles[tile] = jnp.where(lane_mask(low, low + width), moved, tiles[tile])
            if low + width > LANES:
                tiles[tile + 1] = jnp.where(lane_mask(0, low + width - LANES), moved, tiles[tile + 1])
        for tile, value in enumerate(tiles):
            par_ref[8 * group : 8 * group + 8, tile * LANES : (tile + 1) * LANES] = value
    bias_ref[...] = jnp.zeros_like(bias_ref)
    for place in range(devices):
        for at in range(part // width):
            row = VEC + 5 + at
            group, line = row // 8, row % 8
            start = place * part + at * width
            tile, low = start // LANES, start % LANES
            source = small_ref[order_ref[place], line : line + 1, :]
            moved = pltpu.roll(jnp.broadcast_to(source, (8, LANES)), (start - group * width) % LANES, 1)
            for where_, lower, upper in ((tile, low, low + width), (tile + 1, 0, low + width - LANES)):
                if upper > lower:
                    lanes = slice(where_ * LANES, (where_ + 1) * LANES)
                    kept = jnp.broadcast_to(bias_ref[0:1, lanes], (8, LANES))
                    bias_ref[0:1, lanes] = jnp.where(lane_mask(lower, upper), moved, kept)[0:1]


def pack_grads(owner_ref, taps, vec_ref, bias_ref, out_ref, rows_ref):
    devices = out_ref.shape[0]
    channels = taps.shape[1]
    width = channels // devices
    part = bias_ref.shape[1] // devices
    rows_ref[...] = jnp.zeros_like(rows_ref)
    rows_ref[0:VEC, :] = taps
    rows_ref[VEC : VEC + 5, :] = vec_ref[0:5, :]

    def cut(row_slice, source, start, group):
        tile, low = start // LANES, start % LANES
        shift = (group * width - low) % LANES
        moved = pltpu.roll(source(row_slice, tile), shift, 1)
        if low + width > LANES:
            split = group * width + LANES - low
            moved = jnp.where(lane_mask(0, split), moved, pltpu.roll(source(row_slice, tile + 1), shift, 1))
        return moved

    def of_rows(rows, tile):
        return rows_ref[rows, tile * LANES : (tile + 1) * LANES]

    def of_bias(rows, tile):
        return jnp.broadcast_to(bias_ref[0:1, tile * LANES : (tile + 1) * LANES], (8, LANES))

    for device in range(devices):
        total = jnp.zeros((8, LANES), f32)
        for group in range(ROWS // 8):
            moved = cut(slice(8 * group, 8 * group + 8), of_rows, device * width, group)
            total = jnp.where(lane_mask(group * width, (group + 1) * width), moved, total)
        out_ref[device] = total
    for place in range(devices):
        device = owner_ref[place]
        for at in range(part // width):
            row = VEC + 5 + at
            group, line = row // 8, row % 8
            moved = cut(None, of_bias, place * part + at * width, group)
            kept = jnp.broadcast_to(out_ref[device, line : line + 1, :], (8, LANES))
            mask = lane_mask(group * width, (group + 1) * width)
            out_ref[device, line : line + 1, :] = jnp.where(mask, moved, kept)[0:1]


def total_kernel(small_ref, *refs):
    count = (len(refs) - 5) // 2
    parts, (own_ref, sums_ref, norm_ref), bufs, (sems, small_buf) = refs[:count], refs[count : count + 3], refs[count + 3 : -2], refs[-2:]
    size = own_ref.shape[0]
    loads = [pltpu.make_async_copy(small_ref, small_buf, sems.at[count])]
    for at, (ref, buf) in enumerate(zip(parts, bufs)):
        loads.append(pltpu.make_async_copy(ref.at[0:size], buf, sems.at[at]))
    for load in loads:
        load.start()
    for load in loads:
        load.wait()
    own = bufs[0][...].astype(f32)
    for buf in bufs[1:]:
        own = own + buf[...].astype(f32)
    own_ref[...] = own
    sums = jnp.sum(small_buf[...], axis=0)
    sums_ref[...] = sums
    local = jnp.sum(own * own) + jnp.sum(sums * sums)
    norm_ref[...] = jnp.full_like(norm_ref, local)


def adam(weight, moment, square, grad, factor, rate):
    scaled = grad * factor
    new_moment = beta_one * moment + (1.0 - beta_one) * scaled
    new_square = beta_two * square + (1.0 - beta_two) * scaled * scaled
    corrected = new_moment / (1.0 - beta_one**STEP)
    spread = jnp.sqrt(new_square / (1.0 - beta_two**STEP))
    return weight - rate * (corrected / (spread + adam_eps) + decay_rate * weight), new_moment, new_square


def adam_kernel(own_ref, sums_ref, norms_ref, *refs):
    states, outs, norm_ref, rows_ref, flip_ref = refs[:15], refs[15:30], refs[30], refs[31], refs[32]
    part, channels = states[6].shape
    width = states[0].shape[0]
    total = jnp.sum(norms_ref[:, 0, 0:1])
    norm = jnp.sqrt(jnp.full((8, LANES), total, f32))
    norm_ref[...] = norm[0:1, 0:1]
    factor = (clip_limit / jnp.maximum(norm, clip_limit))[0:1, 0:1]
    sums = sums_ref[...]
    rows_ref[...] = jnp.zeros_like(rows_ref)
    for group in range(ROWS // 8):
        rows_ref[8 * group : 8 * group + 8, :] = pltpu.roll(sums, (-group * width) % LANES, 1)
    flip_ref[...] = rows_ref[...].T
    grads = [
        flip_ref[0:width, 0:VEC],
        rows_ref[VEC : VEC + 5, 0:width],
        own_ref[:, 0:channels],
        None,
        own_ref[:, channels : 2 * channels],
    ]
    for index, (grad, rate) in enumerate(zip(grads, step_rates)):
        if grad is None:
            continue
        results = adam(*(ref[...] for ref in states[3 * index : 3 * index + 3]), grad, factor, rate)
        for ref, value in zip(outs[3 * index : 3 * index + 3], results):
            ref[...] = value
    for at in range(part // width):
        lanes = slice(at * width, (at + 1) * width)
        row = VEC + 5 + at
        grad = rows_ref[row : row + 1, 0:width]
        results = adam(*(ref[0:1, lanes] for ref in states[9:12]), grad, factor, step_rates[3])
        for ref, value in zip(outs[9:12], results):
            ref[0:1, lanes] = value


def mlp(which, table, unit, stat, cots, pieces, bias, pars, dims):
    count, rows, cols, channels = dims
    pixels = rows * cols
    total = count * pixels
    hidden_size = bias.shape[1]
    tall = MLP_SLOTS * pixels
    at = 2 * count + 5 * which + 1

    def last(i, n):
        return jnp.minimum(i, jnp.maximum((n[at] + MLP_SLOTS - 1) // MLP_SLOTS - 1, 0))

    tile_map = lambda i, n: (last(i, n), 0)
    slot_map = lambda i, n: (last(i, n), 0, 0, 0)
    whole = lambda i, n: (0, 0)
    grad = (hidden_size // 2, 2 * channels)
    halo = (count, REACH, cols, channels)
    once = pl.Buffered(1)
    rest = tall % DEEP * -(-count // MLP_SLOTS)
    return pl.pallas_call(
        functools.partial(mlp_kernel, at),
        grid_spec=pltpu.PrefetchScalarGridSpec(
            num_scalar_prefetch=1,
            grid=(-(-count // MLP_SLOTS),),
            in_specs=[
                pl.BlockSpec((tall, channels), tile_map),
                pl.BlockSpec((tall, LANES), tile_map),
                pl.BlockSpec((tall, channels), tile_map),
                pl.BlockSpec(bias.shape, whole),
                pl.BlockSpec(pars.shape, whole),
            ]
            + [pl.BlockSpec(value.shape, whole, pipeline_mode=once) for value in pieces],
            out_specs=[
                pl.BlockSpec((MLP_SLOTS, rows, cols, channels), slot_map),
                pl.BlockSpec((MLP_SLOTS, rows, cols, channels), slot_map),
                pl.BlockSpec((MLP_SLOTS, REACH, cols, channels), slot_map),
                pl.BlockSpec((MLP_SLOTS, REACH, cols, channels), slot_map),
                pl.BlockSpec(grad, whole),
                pl.BlockSpec(grad, whole),
                pl.BlockSpec((1, hidden_size), whole),
                pl.BlockSpec((8, channels), whole),
            ],
            scratch_shapes=[
                pltpu.VMEM((channels, hidden_size), f32),
                pltpu.VMEM((channels, hidden_size), f32),
                pltpu.VMEM((hidden_size, channels), bf16),
                pltpu.VMEM((hidden_size, 2 * channels), bf16),
                pltpu.VMEM((8, hidden_size), f32),
                pltpu.VMEM((40, channels), f32),
                pltpu.VMEM((rest, channels), bf16),
                pltpu.VMEM((rest, channels), bf16),
                pltpu.VMEM((rest, hidden_size), bf16),
                pltpu.VMEM((rest, hidden_size), bf16),
            ],
        ),
        out_shape=[
            shape(dims, bf16),
            shape(dims, bf16),
            shape(halo, bf16),
            shape(halo, bf16),
            shape(grad, bf16),
            shape(grad, bf16),
            shape((1, hidden_size), f32),
            shape((8, channels), f32),
        ],
        compiler_params=pltpu.CompilerParams(dimension_semantics=("arbitrary",), vmem_limit_bytes=VMEM_MIB * MIB),
        name="mlp",
    )(table, unit.reshape(total, channels), stat.reshape(total, LANES), cots.reshape(total, channels), bias, pars, *pieces)


IN_PLACE = pl.BlockSpec(memory_space=pltpu.HBM)
SCALARS = pl.BlockSpec(memory_space=pltpu.SMEM)
LOADED = pl.BlockSpec(memory_space=pltpu.VMEM)


def call(kernel, in_specs, out_specs, out_shape, scratch, name, aliases=None):
    return pl.pallas_call(
        kernel,
        in_specs=in_specs,
        out_specs=out_specs,
        out_shape=out_shape,
        scratch_shapes=scratch,
        input_output_aliases=aliases or {},
        compiler_params=pltpu.CompilerParams(vmem_limit_bytes=VMEM_MIB * MIB),
        name=name,
    )


def shape(dims, kind):
    return jax.ShapeDtypeStruct(dims, kind)


def window(rows, cols, channels):
    return pltpu.VMEM((DEPTH, rows + 2 * REACH, cols, channels), bf16)


def paired(rows, cols, channels):
    return pltpu.VMEM((channels // LANES, rows // 2 + 2 * REACH, 2 * cols, LANES), bf16)


def conv_norm(which, first, table, above, own, below, cot, pars, earlier):
    count, rows, cols, channels = own.shape
    pixels = rows * cols
    outs = [
        shape((count, pixels, channels), f32),
        shape((count, pixels, LANES), f32),
        shape((count, rows, cols, channels), bf16),
    ]
    run = call(
        functools.partial(conv_norm_kernel, which, first),
        [SCALARS] + [IN_PLACE] * (5 + len(earlier)),
        [IN_PLACE] * 3,
        outs,
        [
            window(rows, cols, channels),
            pltpu.VMEM((DEPTH, pixels, channels), f32),
            pltpu.VMEM((DEPTH, pixels, LANES), f32),
            pltpu.VMEM((DEPTH, rows, cols, channels), bf16),
            paired(rows, cols, channels),
            pltpu.VMEM((TAPS, rows, cols + 2 * EDGE, LANES), f32),
            pltpu.VMEM((pixels, channels), f32),
            pltpu.VMEM(pars.shape, f32),
            pltpu.SemaphoreType.DMA((DEPTH, 4)),
            pltpu.SemaphoreType.DMA((DEPTH, 3)),
            pltpu.SemaphoreType.DMA,
        ],
        "conv_norm",
        {6 + at: at for at in range(len(earlier))},
    )
    return run(table, above, own, below, cot, pars, *earlier)


def taps_grad(which, table, halos, own, gc, owners, vec, bias):
    count, rows, cols, channels = own.shape
    run = call(
        functools.partial(taps_grad_kernel, which, halos[0].shape[0]),
        [SCALARS] + [IN_PLACE] * 6 + [SCALARS] + [LOADED] * 2,
        LOADED,
        shape((owners.shape[0], 8, LANES), f32),
        [
            window(rows, cols, channels),
            pltpu.VMEM((DEPTH, rows, cols, channels), bf16),
            paired(rows, cols, channels),
            pltpu.VMEM((TAPS * TAPS, 8, channels), f32),
            pltpu.VMEM((channels // LANES, rows, cols + 2 * EDGE, LANES), f32),
            pltpu.VMEM((ROWS, channels), f32),
            pltpu.SemaphoreType.DMA((DEPTH, 4)),
        ],
        "taps_grad",
    )
    return run(table, halos[0], own, halos[1], halos[2], halos[3], gc, owners, vec, bias)


def finish(which, table, above, gc, below, branch, images, cot, pars, earlier):
    count, rows, cols, channels = images.shape
    block = (DEPTH, rows, cols, channels)
    run = call(
        functools.partial(finish_kernel, which),
        [SCALARS] + [IN_PLACE] * (7 + len(earlier)),
        [IN_PLACE] * 2,
        [shape(images.shape, bf16)] * 2,
        [
            window(rows, cols, channels),
            pltpu.VMEM(block, bf16),
            pltpu.VMEM(block, bf16),
            pltpu.VMEM(block, bf16),
            pltpu.VMEM(block, bf16),
            pltpu.VMEM(block, bf16),
            paired(rows, cols, channels),
            pltpu.VMEM((TAPS, rows, cols + 2 * EDGE, LANES), f32),
            pltpu.VMEM((rows, cols, channels), f32),
            pltpu.VMEM(pars.shape, f32),
            pltpu.VMEM((DEPTH, 2, rows, cols, channels), bf16),
            pltpu.SemaphoreType.DMA((DEPTH, 6)),
            pltpu.SemaphoreType.DMA((DEPTH, 2)),
            pltpu.SemaphoreType.DMA,
            pltpu.SemaphoreType.DMA((DEPTH, 4)),
        ],
        "finish",
        {8 + at: at for at in range(len(earlier))},
    )
    maps = (value.reshape(images.shape) for value in (gc, branch))
    gc, branch = maps
    return run(table, above, gc, below, branch, images, cot, pars, *earlier)


def pack(spans, codes, space_size, rows, keep, sides, kernel, vectors, bias, up, down):
    channels, part = up.shape
    return call(
        functools.partial(pack_kernel, spans, codes, space_size, rows),
        [SCALARS] * 2 + [LOADED] * 5,
        [LOADED] * 2 + [SCALARS] * 2,
        [
            shape((len(codes), 8, LANES), f32),
            shape((part, 2 * channels), bf16),
            shape((2 * keep.shape[0] + 5 * len(spans),), jnp.int32),
            shape((len(codes),), jnp.int32),
        ],
        [pltpu.VMEM((LANES, LANES), f32), pltpu.SMEM((keep.shape[0] + 1,), jnp.int32)],
        "pack",
    )(keep, sides, kernel.T, vectors, bias.reshape(1, -1), up.T, down)


def join_two(*pieces):
    size, width = pieces[0].shape
    each = len(pieces) // 2
    out = shape((each * size, width), pieces[0].dtype)
    return call(join_kernel, [LOADED] * len(pieces), [LOADED] * 2, [out, out], [], "join")(*pieces)


def unpack(order, small, channels, hidden_size):
    return call(
        unpack_kernel,
        [SCALARS, LOADED],
        [LOADED] * 2,
        [shape((ROWS, channels), f32), shape((1, hidden_size), f32)],
        [],
        "unpack",
    )(order, small)


def add_up(small, parts, size):
    devices = small.shape[0]
    width = parts[0].shape[1]
    return call(
        total_kernel,
        [IN_PLACE] * (1 + len(parts)),
        [LOADED] * 3,
        [shape((size, width), f32), shape((8, LANES), f32), shape((devices, 8, LANES), f32)],
        [pltpu.VMEM((size, width), value.dtype) for value in parts]
        + [pltpu.SemaphoreType.DMA((len(parts) + 1,)), pltpu.VMEM(small.shape, f32)],
        "add_up",
    )(small, *parts)


def update(own, sums, norms, states):
    def view(at, value):
        if at // 3 in (0, 2):
            return value.T
        return value.reshape(1, -1) if at // 3 == 3 else value

    def unview(at, value):
        return value.reshape(-1) if at // 3 == 3 else view(at, value)

    views = [view(at, value) for at, value in enumerate(states)]
    results = call(
        adam_kernel,
        [LOADED] * 18,
        [LOADED] * 16,
        [shape(value.shape, f32) for value in views] + [shape((1, 1), f32)],
        [pltpu.VMEM((LANES, LANES), f32), pltpu.VMEM((LANES, LANES), f32)],
        "update",
    )(own, sums, norms, *views)
    return [unview(at, value) for at, value in enumerate(results[:15])], results[15].reshape(())


def pass_rows(top, low, places):
    above = lax.ppermute(low, "space", [(i, i + 1) for i in range(places - 1)])
    below = lax.ppermute(top, "space", [(i + 1, i) for i in range(places - 1)])
    return above, below


def flip_perm(size, bit):
    return [(i, i ^ bit) for i in range(size)]


def swap(value, bits):
    axis, bit, size = ("dp", bits[0], 8) if bits[0] else ("space", bits[1], 4)
    return lax.ppermute(value, axis, flip_perm(size, bit))


X, Y, CORE = (1, 0), (0, 2), (0, 1)
Z1, Z2, Z3 = (2, 0), (4, 0), (6, 0)


def cube_order():
    first = [0, 2 * 4]
    last = [4 * 4, 6 * 4]
    first = first + [v ^ 4 for v in first]
    last = last + [v ^ 2 for v in last]
    first = first + [v ^ 2 for v in first]
    last = last + [v ^ 4 for v in last]
    near = first + last
    return near + [v ^ 1 for v in near]


def after(value, *others):
    return lax.optimization_barrier((value,) + others)[0]


def behind(values, token):
    return lax.optimization_barrier((*values, token))[:-1]


def total_of(*pieces):
    total = pieces[0].astype(f32)
    for piece in pieces[1:]:
        total = total + piece.astype(f32)
    return total.astype(bf16)


def exchange(value):
    return lax.all_to_all(value, AXES, 0, 0, tiled=True)


def body(dp_size, space_size, images, cotangent, image_sides, keep_flags, *states):
    devices = dp_size * space_size
    count, rows, cols, channels = images.shape
    depth_kernel, block_vectors, up_weight, up_bias, down_weight = states[0::3]
    part = up_weight.shape[1]
    hidden_size = part * devices
    cube = dp_size == 8 and space_size == 4

    cut, mid = count // 2, 25 * count // 32
    low_cut, high_cut = 3 * count // 8, 11 * count // 16
    spans = (
        (0, cut, count), (cut, mid, count), (mid, count, count),
        (0, low_cut, count), (low_cut, high_cut, count), (high_cut, count, 0),
        (0, count, count), (0, count, 0),
    )
    codes = tuple(cube_order()) if cube else tuple(range(devices))
    small, piece, table, owners = pack(
        spans, codes, space_size, rows, keep_flags, image_sides, depth_kernel, block_vectors, up_bias, up_weight, down_weight
    )
    small_all = exchange(small)
    piece, maps = after((piece, images), small) if cube else (piece, images)
    halos = pass_rows(maps[:cut, :REACH], maps[:cut, -REACH:], space_size)
    pars, bias = unpack(owners, small_all, channels, hidden_size)

    def conv_part(which, earlier, *waits):
        above, below = halos[:2] if which == 0 else halos[2:]
        first = 0 if which == 0 else cut
        return conv_norm(
            which, first, after(table, *waits), above, images, below, cotangent, pars, earlier
        )

    later_rows = (images[cut:, :REACH], images[cut:, -REACH:])
    if cube:
        later = after(images, small_all)
        later_rows = (later[cut:, :REACH], later[cut:, -REACH:])
        z_got = [swap(piece, step) for step in (Z1, Z2, Z3)]
        held = behind((piece, *z_got, *later_rows), pars)
        first, last = join_two(*held[:4])
        later_rows = after(held[4:], first, last, *halos)
        got = (swap(first, X), swap(last, Y))
    halos += pass_rows(*later_rows, space_size)
    if cube:
        made = conv_part(0, (), first, last)
        got = behind(got, made[1])
        first, last = join_two(first, got[0], last, got[1])
        got = (swap(first, Y), swap(last, X))
        made = conv_part(1, made, first, last)
        got = behind(got, made[1])
        pieces = [first, got[0], last, got[1]]
        far = [swap(value, CORE) for value in pieces]
        unit, stat, cots = conv_part(2, made, *pieces)
        pieces = pieces + list(behind(far, stat))
    else:
        pieces = [lax.all_gather(piece, AXES, axis=0, tiled=True)]
        made = conv_part(0, ())
        made = conv_part(1, made)
        unit, stat, cots = conv_part(2, made)
    branch, gc, top, low, grad_near, grad_far, bias_sum, vec_sum = mlp(
        6, table, unit, stat, cots, pieces, bias, pars, images.shape
    )

    def taps_part(which, *waits):
        return taps_grad(which, after(table, *waits), halos, images, gc, owners, vec_sum, bias_sum)

    def finish_part(which, earlier, *waits):
        return finish(
            which, after(table, *waits),
            gc_above, gc, gc_below, branch, images, cotangent, pars, earlier,
        )

    if cube:
        core = swap(grad_far, CORE)
        half = grad_near.shape[0] // 2
        quarter, eighth = half // 2, half // 4

        def kept_sum(which, low, high, *got):
            lines = slice(which * half + low, which * half + high)
            return total_of(grad_near[lines], core[lines], *(value[low:high] for value in got))

        gc_above, gc_below = pass_rows(top, low, space_size)
        send = [kept_sum(0, quarter, half), kept_sum(1, quarter, half)]
        two_a, two_b = swap(send[0], Y), swap(send[1], X)
        taps = taps_part(6, *send)
        two_a, two_b = behind((two_a, two_b), taps)
        got = exchange(taps)
        send = [kept_sum(0, eighth, quarter, two_a), kept_sum(1, eighth, quarter, two_b)]
        three_a, three_b = swap(send[0], X), swap(send[1], Y)
        made = finish_part(3, (), *send)
        three_a, three_b, got = behind((three_a, three_b, got), made[0])
        send = [
            kept_sum(0, part, 2 * part, two_a, three_a),
            kept_sum(1, 0, part, two_b, three_b),
            kept_sum(1, part, 2 * part, two_b, three_b),
        ]
        z_got = [swap(value, step) for value, step in zip(send, (Z1, Z2, Z3))]
        made = finish_part(4, made, *send)
        z_got = behind(z_got, made[0])
        own, sums, norm = add_up(got, [grad_near, core, two_a, three_a, *z_got], part)
        norms = exchange(norm)
        out_images, grad_images = finish_part(5, made, norm)
        norms, grad_images = lax.optimization_barrier((norms, grad_images))
    else:
        gc_above, gc_below = pass_rows(top, low, space_size)
        grads = jnp.concatenate([grad_near, grad_far]).astype(f32)
        parts = [lax.psum_scatter(grads, AXES, scatter_dimension=0, tiled=True)]
        got = exchange(taps_part(6))
        own, sums, norm = add_up(got, parts, part)
        norms = exchange(norm)
        out_images, grad_images = finish_part(7, ())
    results, grad_norm = update(own, sums, norms, states)
    return (out_images, grad_images, *results, grad_norm)


def solution(mesh):
    lanes = P(None, AXES)
    flat = P(AXES)
    tall = P(AXES, None)
    maps = P("dp", "space", None, None)
    in_specs = (maps, maps, P("dp"), P("dp")) + (lanes,) * 9 + (flat,) * 3 + (tall,) * 3
    out_specs = (maps, maps) + (lanes,) * 9 + (flat,) * 3 + (tall,) * 3 + (P(),)
    run = functools.partial(body, mesh.shape["dp"], mesh.shape["space"])
    return jax.shard_map(run, mesh=mesh, in_specs=in_specs, out_specs=out_specs, check_vma=False)
```
